32 devices in a mesh: dp: 16 (over z, y, x), tp: 2 (over core).
Axes of the slice: x: 2, y: 2, z: 4, core: 2. Of those that a mesh axis runs over, the one named last changes fastest.
Arguments:
- hidden: bfloat16 [19456, 384], P('dp'), may hold values from -6 to 6
- frames: bfloat16 [176, 1500, 384], P('dp'), may hold values from -6 to 6
- lengths: int32 [176], P('dp'), may hold values from 1 to 448, as said below
- cotangent: bfloat16 [19456, 384], P('dp'), may hold values from -6 to 6
- ln1_gain: bfloat16 [384], replicated, may hold values from 0.5 to 1.5
- ln1_bias: bfloat16 [384], replicated, may hold values from -1.75 to 1.75
- sq_weight: bfloat16 [384, 384], P(None, 'tp'), may hold values from -0.3125 to 0.3125
- sq_bias: bfloat16 [384], P('tp'), may hold values from -1.75 to 1.75
- sk_weight: bfloat16 [384, 384], P(None, 'tp'), may hold values from -0.3125 to 0.3125
- sv_weight: bfloat16 [384, 384], P(None, 'tp'), may hold values from -0.3125 to 0.3125
- sv_bias: bfloat16 [384], P('tp'), may hold values from -1.75 to 1.75
- so_weight: bfloat16 [384, 384], P('tp'), may hold values from -0.875 to 0.875
- so_bias: bfloat16 [384], replicated, may hold values from -1.75 to 1.75
- ln2_gain: bfloat16 [384], replicated, may hold values from 0.5 to 1.5
- ln2_bias: bfloat16 [384], replicated, may hold values from -1.75 to 1.75
- cq_weight: bfloat16 [384, 384], P(None, 'tp'), may hold values from -0.3125 to 0.3125
- cq_bias: bfloat16 [384], P('tp'), may hold values from -1.75 to 1.75
- ck_weight: bfloat16 [384, 384], P(None, 'tp'), may hold values from -0.3125 to 0.3125
- cv_weight: bfloat16 [384, 384], P(None, 'tp'), may hold values from -0.3125 to 0.3125
- cv_bias: bfloat16 [384], P('tp'), may hold values from -1.75 to 1.75
- co_weight: bfloat16 [384, 384], P('tp'), may hold values from -0.875 to 0.875
- co_bias: bfloat16 [384], replicated, may hold values from -1.75 to 1.75
- ln3_gain: bfloat16 [384], replicated, may hold values from 0.5 to 1.5
- ln3_bias: bfloat16 [384], replicated, may hold values from -1.75 to 1.75
- fc1_weight: bfloat16 [384, 1536], P(None, 'tp'), may hold values from -0.3125 to 0.3125
- fc1_bias: bfloat16 [1536], P('tp'), may hold values from -3 to 3
- fc2_weight: bfloat16 [1536, 384], P('tp'), may hold values from -0.15625 to 0.15625
- fc2_bias: bfloat16 [384], replicated, may hold values from -1.75 to 1.75
Outputs:
- block_out: bfloat16 [19456, 384], P('dp')
- d_hidden: bfloat16 [19456, 384], P('dp')
- grad_ln1_gain: float32 [384], replicated
- grad_ln1_bias: float32 [384], replicated
- grad_sq_weight: float32 [384, 384], P(None, 'tp')
- grad_sq_bias: float32 [384], P('tp')
- grad_sk_weight: float32 [384, 384], P(None, 'tp')
- grad_sv_weight: float32 [384, 384], P(None, 'tp')
- grad_sv_bias: float32 [384], P('tp')
- grad_so_weight: float32 [384, 384], P('tp')
- grad_so_bias: float32 [384], replicated
- grad_ln2_gain: float32 [384], replicated
- grad_ln2_bias: float32 [384], replicated
- grad_cq_weight: float32 [384, 384], P(None, 'tp')
- grad_cq_bias: float32 [384], P('tp')
- grad_ck_weight: float32 [384, 384], P(None, 'tp')
- grad_cv_weight: float32 [384, 384], P(None, 'tp')
- grad_cv_bias: float32 [384], P('tp')
- grad_co_weight: float32 [384, 384], P('tp')
- grad_co_bias: float32 [384], replicated
- grad_ln3_gain: float32 [384], replicated
- grad_ln3_bias: float32 [384], replicated
- grad_fc1_weight: float32 [384, 1536], P(None, 'tp')
- grad_fc1_bias: float32 [1536], P('tp')
- grad_fc2_weight: float32 [1536, 384], P('tp')
- grad_fc2_bias: float32 [384], replicated
The draws below stay inside these ranges and needn't reach their ends.
Inputs may be any that keep to these rules, and one draw needn't show every extreme that they name: `lengths`: in every group of 11 transcripts the first 8 have 1 to 64 tokens, the next 2 have 64 + 1 to 128, the last 1 have 128 + 1 to 448; each of 64, 128 and 448 is the length of some transcript.
All inputs are finite; a program needn't handle non-finite values.
Results may differ from the reference program's by a relative error of at most 0.015.
The reference program's roundings to bfloat16 on the way count: a program that leaves them out, or rounds other values in their place, can miss the bound.
Values may be sent and summed in bfloat16 or wider, within the bound.
No kernel may reach another device: no remote copies, remote signals or barrier semaphores. Data moves between devices by JAX's collectives and lax.ppermute only.
A program may use at most 192 MiB of HBM per device.

```python
import jax
import jax.numpy as jnp
from jax import lax

D = 384
HEADS = 6
HEAD = 64
FF = 1536
FRAMES = 1500
SHORT_LEN = 64
MID_LEN = 128
LONG_LEN = 448
SHORT_N = 8
MID_N = 2
LONG_N = 1
SEQ_GROUP = 11
GROUP_ROWS = 1216
SEQS = 176
TOKENS = 19456


def draw_lengths(key, part):
    slot_place = jnp.arange(SEQS, dtype=jnp.int32) % SEQ_GROUP
    in_short = slot_place < SHORT_N
    in_middle = slot_place < SHORT_N + MID_N
    lowest = jnp.where(in_short, 1, jnp.where(in_middle, SHORT_LEN + 1, MID_LEN + 1))
    highest_len = jnp.where(in_short, SHORT_LEN, jnp.where(in_middle, MID_LEN, LONG_LEN))
    draws = jax.random.randint(jax.random.fold_in(key, 1), (SEQS,), 0, 1 << 20)
    drawn = lowest + draws % (highest_len - lowest + 1)
    picks = jax.random.randint(jax.random.fold_in(key, 2), (3,), 0, SEQS // SEQ_GROUP)
    within = jax.random.randint(jax.random.fold_in(key, 3), (3,), 0, 1 << 20)
    starts = jnp.array([0, SHORT_N, SHORT_N + MID_N], dtype=jnp.int32)
    bucket_sizes = jnp.array([SHORT_N, MID_N, LONG_N], dtype=jnp.int32)
    top_lengths = jnp.array([SHORT_LEN, MID_LEN, LONG_LEN], dtype=jnp.int32)
    forced_at = picks * SEQ_GROUP + starts + within % bucket_sizes
    drawn = drawn.at[forced_at].set(top_lengths)
    return drawn.astype(jnp.int32)


def steps_of(key, shape, cuts, smallest, top_value):
    def one(dim, blocks):
        heights = jax.random.uniform(jax.random.fold_in(jax.random.fold_in(key, 6), dim), (blocks,), jnp.float32, smallest / len(cuts), top_value / len(cuts))
        return jnp.repeat(jnp.exp(heights), shape[dim] // blocks).reshape((-1,) + (1,) * (len(shape) - dim - 1))

    loudness = one(*cuts[0])
    for cut in cuts[1:]:
        loudness = loudness * one(*cut)
    return loudness


def gaussian(stream_key, shape, scale, limit, shards=(), kind=jnp.bfloat16):
    entries = jax.random.normal(stream_key, shape, jnp.float32) * scale
    if len(shards) > 0:
        entries = steps_of(stream_key, shape, shards, -0.22, 0.18) * entries
    return jnp.clip(entries, min=-limit, max=limit).astype(kind)


def setup_inputs(seed: int = 0) -> dict:
    splits = jax.random.split(jax.random.key(seed), 29)
    return {
        "hidden": gaussian(splits[0], (TOKENS, D), 1.0, 6.0, ((0, 16),)),
        "frames": gaussian(splits[1], (SEQS, FRAMES, D), 1.0, 6.0, ((0, 16),)),
        "lengths": draw_lengths(jax.random.fold_in(splits[28], 71), 0),
        "cotangent": gaussian(splits[3], (TOKENS, D), 1.0, 6.0, ((0, 16),)),
        "ln1_gain": jnp.clip(1.0 + 0.1 * jax.random.normal(splits[4], (D,), jnp.float32), 0.5, 1.5).astype(jnp.bfloat16),
        "ln1_bias": gaussian(splits[5], (D,), 0.3, 1.75),
        "sq_weight": gaussian(splits[6], (D, D), D ** -0.5, 0.3125, ((1, 2),)),
        "sq_bias": gaussian(splits[7], (D,), 0.3, 1.75, ((0, 2),)),
        "sk_weight": gaussian(splits[8], (D, D), D ** -0.5, 0.3125, ((1, 2),)),
        "sv_weight": gaussian(splits[9], (D, D), D ** -0.5, 0.3125, ((1, 2),)),
        "sv_bias": gaussian(splits[10], (D,), 0.3, 1.75, ((0, 2),)),
        "so_weight": gaussian(splits[11], (D, D), (D // 8) ** -0.5, 0.875, ((0, 2),)),
        "so_bias": gaussian(splits[12], (D,), 0.3, 1.75),
        "ln2_gain": jnp.clip(1.0 + 0.1 * jax.random.normal(splits[13], (D,), jnp.float32), 0.5, 1.5).astype(jnp.bfloat16),
        "ln2_bias": gaussian(splits[14], (D,), 0.3, 1.75),
        "cq_weight": gaussian(splits[15], (D, D), D ** -0.5, 0.3125, ((1, 2),)),
        "cq_bias": gaussian(splits[16], (D,), 0.3, 1.75, ((0, 2),)),
        "ck_weight": gaussian(splits[17], (D, D), D ** -0.5, 0.3125, ((1, 2),)),
        "cv_weight": gaussian(splits[18], (D, D), D ** -0.5, 0.3125, ((1, 2),)),
        "cv_bias": gaussian(splits[19], (D,), 0.3, 1.75, ((0, 2),)),
        "co_weight": gaussian(splits[20], (D, D), (D // 8) ** -0.5, 0.875, ((0, 2),)),
        "co_bias": gaussian(splits[21], (D,), 0.3, 1.75),
        "ln3_gain": jnp.clip(1.0 + 0.1 * jax.random.normal(splits[22], (D,), jnp.float32), 0.5, 1.5).astype(jnp.bfloat16),
        "ln3_bias": gaussian(splits[23], (D,), 0.3, 1.75),
        "fc1_weight": gaussian(splits[24], (D, FF), D ** -0.5, 0.3125, ((1, 2),)),
        "fc1_bias": gaussian(splits[25], (FF,), 0.5, 3.0, ((0, 2),)),
        "fc2_weight": gaussian(splits[26], (FF, D), FF ** -0.5, 0.15625, ((0, 2),)),
        "fc2_bias": gaussian(splits[27], (D,), 0.3, 1.75),
    }


highest = lax.Precision.HIGHEST
epsilon = 1e-05
masked = -1e+30

@jax.custom_vjp
def low(v):
    return lax.optimization_barrier(v.astype(jnp.bfloat16)).astype(jnp.float32)

@jax.custom_vjp
def low_back(v):
    return v

def low_keep(v):
    return (low(v), None)

def low_pass(kept, grad):
    return (grad,)

def back_keep(v):
    return (v, None)

def back_low(kept, grad):
    return (low(grad),)
low.defvjp(low_keep, low_pass)
low_back.defvjp(back_keep, back_low)

def product(left, right):
    return jnp.dot(left, right, precision=highest, preferred_element_type=jnp.float32)

def normalize(values, gain, bias):
    row_mean = lax.optimization_barrier(jnp.mean(values, -1, keepdims=True))
    centered = values - row_mean
    variance = lax.optimization_barrier(jnp.mean(centered * centered, -1, keepdims=True))
    return centered * lax.rsqrt(variance + epsilon) * gain + bias

def bucket_list():
    buckets = []
    first_seq = 0
    first_row = 0
    for seq_count, slot_len in ((SHORT_N, SHORT_LEN), (MID_N, MID_LEN), (LONG_N, LONG_LEN)):
        buckets.append((first_seq, seq_count, slot_len, first_row))
        first_seq = first_seq + seq_count
        first_row = first_row + seq_count * slot_len
    return buckets

def row_layout(lengths):
    row_length = []
    slot_place = []
    for first_seq, seq_count, slot_len, first_row in bucket_list():
        row_length.append(jnp.repeat(lengths[first_seq:first_seq + seq_count], slot_len))
        slot_place.append(jnp.tile(jnp.arange(slot_len, dtype=jnp.int32), seq_count))
    return (jnp.concatenate(row_length), jnp.concatenate(slot_place))

def softmax_rows(scores):
    row_max = lax.optimization_barrier(jnp.max(scores, -1, keepdims=True))
    expo = jnp.exp(scores - row_max)
    return expo / lax.optimization_barrier(jnp.sum(expo, -1, keepdims=True))

def self_attention(queries, keys, values, lengths):
    pieces = []
    for first_seq, seq_count, slot_len, first_row in bucket_list():
        last_row = first_row + seq_count * slot_len
        query_block = queries[first_row:last_row].reshape(seq_count, slot_len, HEADS, HEAD)
        key_block = keys[first_row:last_row].reshape(seq_count, slot_len, HEADS, HEAD)
        value_block = values[first_row:last_row].reshape(seq_count, slot_len, HEADS, HEAD)
        scores = jnp.einsum('nqhe,nkhe->nhqk', query_block, key_block, precision=highest) * HEAD ** (-0.5)
        scores = low_back(scores)
        places = jnp.arange(slot_len, dtype=jnp.int32)
        bucket_lengths = lengths[first_seq:first_seq + seq_count]
        allowed = (places[None, None, None, :] <= places[None, None, :, None]) & (places[None, None, None, :] < bucket_lengths[:, None, None, None])
        scores = jnp.where(allowed, scores, masked)
        weights = low(softmax_rows(scores))
        context = jnp.einsum('nhqk,nkhe->nqhe', weights, value_block, precision=highest)
        pieces.append(context.reshape(seq_count * slot_len, HEADS * HEAD))
    return jnp.concatenate(pieces, 0)

def cross_attention(queries, keys, values):
    pieces = []
    for first_seq, seq_count, slot_len, first_row in bucket_list():
        last_row = first_row + seq_count * slot_len
        query_block = queries[first_row:last_row].reshape(seq_count, slot_len, HEADS, HEAD)
        key_block = keys[first_seq:first_seq + seq_count]
        value_block = values[first_seq:first_seq + seq_count]
        scores = jnp.einsum('nqhe,nfhe->nhqf', query_block, key_block, precision=highest) * HEAD ** (-0.5)
        scores = low_back(scores)
        weights = low(softmax_rows(scores))
        context = jnp.einsum('nhqf,nfhe->nqhe', weights, value_block, precision=highest)
        pieces.append(context.reshape(seq_count * slot_len, HEADS * HEAD))
    return jnp.concatenate(pieces, 0)

def group_forward(params, inputs, frames_float, lengths):
    gain_one, bias_one, sq_w, sq_b, sk_w, sv_w, sv_b, so_w, so_b, gain_two, bias_two, cq_w, cq_b, ck_w, cv_w, cv_b, co_w, co_b, gain_three, bias_three, fc1_w, fc1_b, fc2_w, fc2_b = params
    row_length, slot_place = row_layout(lengths)
    valid_rows = slot_place < row_length
    norm_one = low(normalize(inputs, gain_one, bias_one))
    query_self = low_back(low(product(norm_one, sq_w) + sq_b))
    key_self = low_back(low(product(norm_one, sk_w)))
    value_self = low_back(low(product(norm_one, sv_w) + sv_b))
    context_self = low_back(low(self_attention(query_self, key_self, value_self, lengths)))
    resid_one = inputs + low_back(product(context_self, so_w)) + so_b
    norm_two = low(normalize(resid_one, gain_two, bias_two))
    query_cross = low_back(low(product(norm_two, cq_w) + cq_b))
    key_flat = jnp.einsum('sfd,dc->sfc', frames_float, ck_w, precision=highest)
    value_flat = jnp.einsum('sfd,dc->sfc', frames_float, cv_w, precision=highest) + cv_b
    key_cross = low_back(low(key_flat)).reshape(SEQ_GROUP, FRAMES, HEADS, HEAD)
    value_cross = low_back(low(value_flat)).reshape(SEQ_GROUP, FRAMES, HEADS, HEAD)
    context_cross = low_back(low(cross_attention(query_cross, key_cross, value_cross)))
    resid_two = resid_one + low_back(product(context_cross, co_w)) + co_b
    norm_three = low(normalize(resid_two, gain_three, bias_three))
    pre_act = low_back(product(norm_three, fc1_w) + fc1_b)
    activation = low(jax.nn.gelu(pre_act, approximate=False))
    resid_three = resid_two + low_back(product(activation, fc2_w)) + fc2_b
    return jnp.where(valid_rows[:, None], resid_three, 0.0)

def reference(hidden, frames, lengths, cotangent, ln1_gain, ln1_bias, sq_weight, sq_bias, sk_weight, sv_weight, sv_bias, so_weight, so_bias, ln2_gain, ln2_bias, cq_weight, cq_bias, ck_weight, cv_weight, cv_bias, co_weight, co_bias, ln3_gain, ln3_bias, fc1_weight, fc1_bias, fc2_weight, fc2_bias):
    params = tuple((weight_array.astype(jnp.float32) for weight_array in (ln1_gain, ln1_bias, sq_weight, sq_bias, sk_weight, sv_weight, sv_bias, so_weight, so_bias, ln2_gain, ln2_bias, cq_weight, cq_bias, ck_weight, cv_weight, cv_bias, co_weight, co_bias, ln3_gain, ln3_bias, fc1_weight, fc1_bias, fc2_weight, fc2_bias)))
    groups = TOKENS // GROUP_ROWS
    carried = (hidden.reshape(groups, GROUP_ROWS, D), frames.reshape(groups, SEQ_GROUP, FRAMES, D), lengths.reshape(groups, SEQ_GROUP).astype(jnp.int32), cotangent.reshape(groups, GROUP_ROWS, D))

    def group_step(totals, group_item):
        hidden_group, frames_group, lengths_group, cot_group = group_item
        frames_float = frames_group.astype(jnp.float32)

        def forward(weights, inputs):
            return group_forward(weights, inputs, frames_float, lengths_group)
        outputs, pullback = jax.vjp(forward, params, hidden_group.astype(jnp.float32))
        grad_weights, grad_inputs = pullback(cot_group.astype(jnp.float32))
        totals = tuple((total_grad + new_grad for total_grad, new_grad in zip(totals, grad_weights)))
        return (totals, (outputs.astype(jnp.bfloat16), grad_inputs.astype(jnp.bfloat16)))
    zero_grads = tuple((jnp.zeros_like(weight_array) for weight_array in params))
    totals, (block_rows, grad_rows) = lax.scan(group_step, zero_grads, carried)
    return (block_rows.reshape(TOKENS, D), grad_rows.reshape(TOKENS, D), totals[0], totals[1], totals[2], totals[3], totals[4], totals[5], totals[6], totals[7], totals[8], totals[9], totals[10], totals[11], totals[12], totals[13], totals[14], totals[15], totals[16], totals[17], totals[18], totals[19], totals[20], totals[21], totals[22], totals[23])
```

```python
from functools import partial

import jax
import jax.numpy as jnp
from jax import lax
from jax.experimental import pallas as pl
from jax.experimental.pallas import tpu as pltpu
from jax.sharding import PartitionSpec as P

D = 384
HEAD = 64
HALF = D // 2
SHORT_LEN = 64
MID_LEN = 128
LONG_LEN = 448
SHORT_N = 8
MID_N = 2
LONG_N = 1
SEQ_TOTAL = SHORT_N + MID_N + LONG_N
GROUP_ROWS = SHORT_N * SHORT_LEN + MID_N * MID_LEN + LONG_N * LONG_LEN

HEAD_SHORTS = 3
BLOCK = 64
FIRST_ROWS = HEAD_SHORTS * BLOCK
ROWS = FIRST_ROWS + LONG_LEN
BLOCKS = ROWS // BLOCK
REGION_BLOCKS = LONG_LEN // BLOCK
STEPS = 7
PAIRS = D // 128


epsilon = 1e-05
masked = -1e30
scale = HEAD ** (-0.5)

f32 = jnp.float32
bf16 = jnp.bfloat16


def dot(left, right):
    return lax.dot_general(left, right, (((1,), (0,)), ((), ())), preferred_element_type=f32)


def dot_nt(left, right):
    return lax.dot_general(left, right, (((1,), (1,)), ((), ())), preferred_element_type=f32)


def dot_tn(left, right):
    return lax.dot_general(left, right, (((0,), (0,)), ((), ())), preferred_element_type=f32)


def norm_parts(values):
    row_mean = jnp.mean(values, -1, keepdims=True)
    centered = values - row_mean
    variance = jnp.mean(centered * centered, -1, keepdims=True)
    inverse = lax.rsqrt(variance + epsilon)
    return centered * inverse, inverse


def norm_back(normed, inverse, gain, incoming):
    scaled = incoming * gain
    return inverse * (
        scaled
        - jnp.mean(scaled, -1, keepdims=True)
        - normed * jnp.mean(scaled * normed, -1, keepdims=True)
    )


def column_sum(values):
    return jnp.sum(values, 0, keepdims=True)


def own_row(block, core):
    first = (core * HEAD_SHORTS + block) * BLOCK
    region = jnp.where(core == 0, SHORT_N * SHORT_LEN + MID_N * MID_LEN, 2 * FIRST_ROWS)
    return jnp.where(block < HEAD_SHORTS, first, region + (block - HEAD_SHORTS) * BLOCK)


def block_segment(block, core, lens):
    place = block - HEAD_SHORTS
    start = jnp.where(
        place < 2, place * BLOCK, jnp.where(place < 4, 2 * BLOCK, jnp.where(place < 6, 4 * BLOCK, 6 * BLOCK))
    )
    start = jnp.where((block < HEAD_SHORTS) | (core == 0), 0, start)
    seq = jnp.where(place < 2, 2 * HEAD_SHORTS + place, jnp.where(place < 4, SHORT_N, SHORT_N + 1))
    seq = jnp.where(core == 0, SEQ_TOTAL - 1, seq)
    seq = jnp.where(block < HEAD_SHORTS, core * HEAD_SHORTS + block, seq)
    padding = (core == 1) & (block == BLOCKS - 1)
    length = jnp.where(padding, BLOCK, lens[seq])
    return start, length, padding


def rows_of(index, count):
    return pl.ds(pl.multiple_of(index * count, count), count)


def head_masks():
    lane = lax.broadcasted_iota(jnp.int32, (BLOCK, 128), 1)
    low = (lane < HEAD).astype(f32)
    return low.astype(bf16), (1.0 - low).astype(bf16), lane < HEAD


def stacked(values, low, high):
    return jnp.concatenate([values * low, values * high], 0)


def joined(product, is_low):
    return jnp.where(is_low, product[:BLOCK], product[BLOCK:])


def self_mask(block, core, lens, key_count):
    start, length, _ = block_segment(block, core, lens)
    place = jnp.where(block < HEAD_SHORTS, 0, (block - HEAD_SHORTS) * BLOCK)
    row = lax.broadcasted_iota(jnp.int32, (2 * BLOCK, key_count), 0) & (BLOCK - 1)
    column = lax.broadcasted_iota(jnp.int32, (2 * BLOCK, key_count), 1)
    return (column <= row + place) & (column >= start) & (column < start + length)


def self_forward_kernel(
    core_ref, lens_ref, hidden_ref, vec_ref, wq_ref, wk_ref, wv_ref, wo_ref, wc_ref,
    own_ref, n1_ref, q_ref, k_ref, v_ref, ctx_ref, r1_ref, n2_ref, qc_ref, lse_ref,
):
    core = core_ref[0]

    def gather(block, carry):
        own_ref[rows_of(block, BLOCK), :] = hidden_ref[
            pl.ds(pl.multiple_of(own_row(block, core), BLOCK), BLOCK), :
        ]
        return carry

    lax.fori_loop(0, BLOCKS, gather, 0)

    def project(chunk, carry):
        rows = rows_of(chunk, 128)
        normed, _ = norm_parts(own_ref[rows, :].astype(f32))
        n1 = (normed * vec_ref[0:1, :] + vec_ref[1:2, :]).astype(bf16)
        n1_ref[rows, :] = n1
        q_ref[rows, :] = (dot(n1, wq_ref[...]) + vec_ref[9:10, :]).astype(bf16)
        k_ref[rows, :] = dot(n1, wk_ref[...]).astype(bf16)
        v_ref[rows, :] = (dot(n1, wv_ref[...]) + vec_ref[10:11, :]).astype(bf16)
        return carry

    lax.fori_loop(0, ROWS // 128, project, 0)
    low, high, is_low = head_masks()

    def attend(block, keys, key_count):
        rows = rows_of(block, BLOCK)
        allowed = self_mask(block, core, lens_ref, key_count)
        for pair in range(PAIRS):
            cols = slice(pair * 128, pair * 128 + 128)
            query = stacked(q_ref[rows, cols] * scale, low, high)
            scores = jnp.where(allowed, dot_nt(query, k_ref[keys, cols]), masked)
            top = jnp.max(scores, -1, keepdims=True)
            expo = jnp.exp(scores - top)
            total = jnp.sum(expo, -1, keepdims=True)
            weights = (expo * (1.0 / total)).astype(bf16)
            ctx_ref[rows, cols] = joined(dot(weights, v_ref[keys, cols]), is_low).astype(bf16)
            lse_ref[rows_of(block, 2 * BLOCK), pair : pair + 1] = top + jnp.log(total)

    def first(block, carry):
        attend(block, rows_of(block, BLOCK), BLOCK)
        return carry

    def second(block, carry):
        attend(block, pl.ds(FIRST_ROWS, LONG_LEN), LONG_LEN)
        return carry

    lax.fori_loop(0, HEAD_SHORTS, first, 0)
    lax.fori_loop(HEAD_SHORTS, BLOCKS, second, 0)

    def finish(chunk, carry):
        rows = rows_of(chunk, 128)
        r1 = own_ref[rows, :].astype(f32) + dot(ctx_ref[rows, :], wo_ref[...]) + vec_ref[2:3, :]
        r1_ref[rows, :] = r1
        normed, _ = norm_parts(r1)
        n2 = (normed * vec_ref[3:4, :] + vec_ref[4:5, :]).astype(bf16)
        n2_ref[rows, :] = n2
        qc_ref[rows, :] = (dot(n2, wc_ref[...]) + vec_ref[11:12, :]).astype(bf16)
        return carry

    lax.fori_loop(0, ROWS // 128, finish, 0)


def step_count(core):
    return jnp.where(core == 0, HEAD_SHORTS + 1, STEPS)


def step_seq(step, core):
    step = jnp.minimum(step, step_count(core) - 1)
    return jnp.where(core == 0, jnp.where(step < HEAD_SHORTS, step, SEQ_TOTAL - 1), HEAD_SHORTS + step)


def step_blocks(step, core):
    count = jnp.where(step < HEAD_SHORTS, 1, jnp.where(core == 0, REGION_BLOCKS, jnp.where(step < 5, 1, 2)))
    first = jnp.where(step < 6, step, 7)
    return first, count


def cross_forward_kernel(
    frame_total, core_ref, frames_ref, qc_ref, vec_ref, wk_ref, wv_ref, k_ref, v_ref, ctx_ref, lse_ref
):
    step = pl.program_id(0)
    core = core_ref[0]
    padded = k_ref.shape[1]
    tail = padded - 128
    low, high, is_low = head_masks()

    @pl.when(step == 0)
    def _():
        ctx_ref[ROWS - BLOCK :, :] = jnp.zeros((BLOCK, D), bf16)

    @pl.when(step < step_count(core))
    def _():
        k_ref[0, padded - 64 :, :] = jnp.zeros((64, D), bf16)
        v_ref[0, padded - 64 :, :] = jnp.zeros((64, D), bf16)
        bias = vec_ref[12:13, :]
        for top in range(0, frame_total, 512):
            end = min(top + 512, frame_total)
            part = frames_ref[0, top:end, :]
            k_ref[0, top:end, :] = dot(part, wk_ref[...]).astype(bf16)
            v_ref[0, top:end, :] = (dot(part, wv_ref[...]) + bias).astype(bf16)
        first, count = step_blocks(step, core)

        def attend(turn, carry):
            block = first + turn
            rows = rows_of(block, BLOCK)
            inside = lax.broadcasted_iota(jnp.int32, (2 * BLOCK, 128), 1) < frame_total - tail
            for pair in range(PAIRS):
                cols = slice(pair * 128, pair * 128 + 128)
                query = stacked(qc_ref[rows, cols] * scale, low, high)
                scores = dot_nt(query, k_ref[0, :, cols])
                scores = jnp.concatenate([scores[:, :tail], jnp.where(inside, scores[:, tail:], masked)], 1)
                top = jnp.max(scores, -1, keepdims=True)
                expo = jnp.exp(scores - top)
                total = jnp.sum(expo, -1, keepdims=True)
                weights = (expo * (1.0 / total)).astype(bf16)
                ctx_ref[rows, cols] = joined(dot(weights, v_ref[0, :, cols]), is_low).astype(bf16)
                lse_ref[rows_of(block, 2 * BLOCK), pair : pair + 1] = top + jnp.log(total)
            return carry

        lax.fori_loop(0, count, attend, 0)


def feed_kernel(
    core_ref, lens_ref, cot_ref, r1_ref, ctx_ref, vec_ref, b1_ref, wo_ref, w1_ref, w2_ref,
    out_ref, g2_ref, dctx_ref, keep_ref, send_ref, small_ref,
    top_ref, n3_ref, act_ref, pre_ref, low_ref,
):
    core = core_ref[0]
    wide = b1_ref.shape[1]
    half = wide // 2

    def block_rows(block, carry):
        rows = rows_of(block, BLOCK)
        start, length, padding = block_segment(block, core, lens_ref)
        place = jnp.where(block < HEAD_SHORTS, 0, (block - HEAD_SHORTS) * BLOCK) - start
        length = jnp.where(padding, 0, length)
        row = lax.broadcasted_iota(jnp.int32, (BLOCK, D), 0) + place
        cot = cot_ref[pl.ds(pl.multiple_of(own_row(block, core), BLOCK), BLOCK), :].astype(f32)
        top_ref[rows, :] = jnp.where(row < length, cot, 0.0).astype(bf16)
        return carry

    lax.fori_loop(0, BLOCKS, block_rows, 0)
    small_ref[...] = jnp.zeros(small_ref.shape, f32)

    def chunk_rows(chunk, sums):
        rows = rows_of(chunk, 128)
        r2 = r1_ref[rows, :] + dot(ctx_ref[rows, :], wo_ref[...]) + vec_ref[5:6, :]
        normed, inverse = norm_parts(r2)
        gain = vec_ref[6:7, :]
        n3 = (normed * gain + vec_ref[7:8, :]).astype(bf16)
        n3_ref[rows, :] = n3
        pre = dot(n3, w1_ref[...]) + b1_ref[...]
        phi = 0.5 * (1.0 + lax.erf(pre * (0.5**0.5)))
        act = (pre * phi).astype(bf16)
        act_ref[rows, :] = act
        out_ref[rows, :] = (r2 + dot(act, w2_ref[...]) + vec_ref[8:9, :]).astype(bf16)
        top = top_ref[rows, :]
        slope = phi + pre * (jnp.exp(-0.5 * pre * pre) * 0.3989422804014327)
        grad_pre = (dot_nt(top, w2_ref[...]) * slope).astype(bf16)
        pre_ref[rows, :] = grad_pre
        grad_n3 = dot_nt(grad_pre, w1_ref[...])
        top32 = top.astype(f32)
        g2 = top32 + norm_back(normed, inverse, gain, grad_n3)
        g2_ref[rows, :] = g2
        low = g2.astype(bf16)
        low_ref[rows, :] = low
        dctx_ref[rows, :] = dot_nt(low, wo_ref[...]).astype(bf16)
        small_ref[0:1, :] += column_sum(top32)
        small_ref[1:2, :] += column_sum(grad_n3 * normed)
        small_ref[2:3, :] += column_sum(grad_n3)
        small_ref[3:4, :] += column_sum(g2)
        bias = column_sum(grad_pre.astype(f32))
        for part in range(4):
            small_ref[4 + part : 5 + part, :] += bias[:, part * D : part * D + D]
        return sums

    lax.fori_loop(0, ROWS // 128, chunk_rows, 0)

    def mask_rows(block, carry):
        rows = rows_of(block, BLOCK)
        start, length, padding = block_segment(block, core, lens_ref)
        place = jnp.where(block < HEAD_SHORTS, 0, (block - HEAD_SHORTS) * BLOCK) - start
        row = lax.broadcasted_iota(jnp.int32, (BLOCK, D), 0) + place
        out_ref[rows, :] = jnp.where(row < length, out_ref[rows, :].astype(f32), 0.0).astype(bf16)
        return carry

    lax.fori_loop(0, BLOCKS, mask_rows, 0)
    for part in range(4):
        cols = slice(part * D, part * D + D)
        target, at = (keep_ref, part) if part < 2 else (send_ref, part - 2)
        target[at * D : at * D + D, :] = dot_tn(n3_ref[...], pre_ref[:, cols]).astype(target.dtype)
        grad = dot_tn(act_ref[:, cols], top_ref[...])
        target[half + at * D : half + at * D + D, :] = grad.astype(target.dtype)
    grad = dot_tn(ctx_ref[...], low_ref[...])
    keep_ref[2 * half : 2 * half + HALF, :] = grad[:HALF]
    send_ref[2 * half : 2 * half + HALF, :] = grad[HALF:].astype(bf16)
    extra = keep_ref.shape[0] - (2 * half + HALF)
    if extra:
        keep_ref[2 * half + HALF :, :] = jnp.zeros((extra, D), f32)
        send_ref[2 * half + HALF :, :] = jnp.zeros((extra, D), bf16)


def pack_halves(left, right):
    lane = lax.broadcasted_iota(jnp.int32, left.shape, 1) < HALF
    own = jnp.where(lane, left, pltpu.roll(right, HALF, 1))
    other = jnp.where(lane, pltpu.roll(left, HALF, 1), right)
    return own, other


def cross_backward_kernel(
    frame_total, core_ref, frames_ref, k_ref, v_ref, qc_ref, dctx_ref, lse_ref,
    dq_ref, keep_ref, send_ref, bias_ref, dk_ref, dv_ref, grad_ref,
):
    step = pl.program_id(0)
    core = core_ref[0]
    padded = k_ref.shape[1]
    low, high, is_low = head_masks()

    @pl.when(step == 0)
    def _():
        dq_ref[ROWS - BLOCK :, :] = jnp.zeros((BLOCK, D), bf16)
        grad_ref[...] = jnp.zeros(grad_ref.shape, f32)
        bias_ref[...] = jnp.zeros(bias_ref.shape, f32)

    @pl.when(step < step_count(core))
    def _():
        first, count = step_blocks(step, core)

        def attend(turn, carry):
            block = first + turn
            rows = rows_of(block, BLOCK)
            for pair in range(PAIRS):
                cols = slice(pair * 128, pair * 128 + 128)
                query = stacked(qc_ref[rows, cols] * scale, low, high)
                grad_out = stacked(dctx_ref[rows, cols], low, high)
                scores = dot_nt(query, k_ref[0, :, cols])
                weights = jnp.exp(scores - lse_ref[rows_of(block, 2 * BLOCK), pair : pair + 1])
                grad_weights = dot_nt(grad_out, v_ref[0, :, cols])
                spread = jnp.sum(weights * grad_weights, -1, keepdims=True)
                grad_scores = (weights * (grad_weights - spread)).astype(bf16)
                grad_query = dot(grad_scores, k_ref[0, :, cols])
                dq_ref[rows, cols] = (joined(grad_query, is_low) * scale).astype(bf16)
                grad_key = dot(query.T, grad_scores)
                grad_value = dot(grad_out.T, weights.astype(bf16))

                @pl.when(turn == 0)
                def _():
                    dk_ref[cols, :] = grad_key
                    dv_ref[cols, :] = grad_value

                @pl.when(turn > 0)
                def _():
                    dk_ref[cols, :] += grad_key
                    dv_ref[cols, :] += grad_value

            return carry

        lax.fori_loop(0, count, attend, 0)
        frames = frames_ref[0]
        grad_ref[:D, :] += dot(dk_ref[:, :frame_total].astype(bf16), frames)
        grad_value = dv_ref[:, :frame_total].astype(bf16)
        grad_ref[D:, :] += dot(grad_value, frames)
        bias_ref[:, 0:1] += jnp.sum(grad_value.astype(f32), -1, keepdims=True)

    @pl.when(step == pl.num_programs(0) - 1)
    def _():
        own, other = pack_halves(grad_ref[:D, :].T, grad_ref[D:, :].T)
        keep_ref[...] = own
        send_ref[...] = other.astype(bf16)


def self_backward_kernel(
    core_ref, lens_ref, own_ref, vec_ref, wq_ref, wk_ref, wv_ref, wo_ref, wc_ref,
    n1_ref, q_ref, k_ref, v_ref, ctx_ref, r1_ref, n2_ref, lse_ref,
    dqc_ref, g2_ref, feed_small_ref, cross_bias_ref, cross_keep_ref, cross_send_ref,
    dh_ref, keep_ref, send_ref,
    g1_ref, low_ref, dctx_ref, dq_ref, dk_ref, dv_ref, dk_acc, dv_acc, small_ref,
):
    core = core_ref[0]
    small_ref[...] = jnp.zeros(small_ref.shape, f32)
    dk_acc[...] = jnp.zeros(dk_acc.shape, f32)
    dv_acc[...] = jnp.zeros(dv_acc.shape, f32)

    def enter(chunk, carry):
        rows = rows_of(chunk, 128)
        dqc = dqc_ref[rows, :]
        grad_n2 = dot_nt(dqc, wc_ref[...])
        normed, inverse = norm_parts(r1_ref[rows, :])
        g1 = g2_ref[rows, :] + norm_back(normed, inverse, vec_ref[3:4, :], grad_n2)
        g1_ref[rows, :] = g1
        low = g1.astype(bf16)
        low_ref[rows, :] = low
        dctx_ref[rows, :] = dot_nt(low, wo_ref[...]).astype(bf16)
        small_ref[0:1, :] += column_sum(dqc.astype(f32))
        small_ref[1:2, :] += column_sum(grad_n2 * normed)
        small_ref[2:3, :] += column_sum(grad_n2)
        small_ref[3:4, :] += column_sum(g1)
        return carry

    lax.fori_loop(0, ROWS // 128, enter, 0)
    low, high, is_low = head_masks()

    def attend(block, keys, key_count):
        rows = rows_of(block, BLOCK)
        allowed = self_mask(block, core, lens_ref, key_count)
        for pair in range(PAIRS):
            cols = slice(pair * 128, pair * 128 + 128)
            query = stacked(q_ref[rows, cols] * scale, low, high)
            grad_out = stacked(dctx_ref[rows, cols], low, high)
            scores = dot_nt(query, k_ref[keys, cols])
            weights = jnp.where(
                allowed, jnp.exp(scores - lse_ref[rows_of(block, 2 * BLOCK), pair : pair + 1]), 0.0
            )
            grad_weights = dot_nt(grad_out, v_ref[keys, cols])
            spread = jnp.sum(weights * grad_weights, -1, keepdims=True)
            grad_scores = (weights * (grad_weights - spread)).astype(bf16)
            dq_ref[rows, cols] = (joined(dot(grad_scores, k_ref[keys, cols]), is_low) * scale).astype(bf16)
            dk_acc[keys, cols] += dot_tn(grad_scores, query)
            dv_acc[keys, cols] += dot_tn(weights.astype(bf16), grad_out)

    def first(block, carry):
        attend(block, rows_of(block, BLOCK), BLOCK)
        return carry

    def second(block, carry):
        attend(block, pl.ds(FIRST_ROWS, LONG_LEN), LONG_LEN)
        return carry

    lax.fori_loop(0, HEAD_SHORTS, first, 0)
    lax.fori_loop(HEAD_SHORTS, BLOCKS, second, 0)

    def leave(chunk, carry):
        rows = rows_of(chunk, 128)
        dq = dq_ref[rows, :]
        dk = dk_acc[rows, :].astype(bf16)
        dv = dv_acc[rows, :].astype(bf16)
        dk_ref[rows, :] = dk
        dv_ref[rows, :] = dv
        grad_n1 = dot_nt(dq, wq_ref[...]) + dot_nt(dk, wk_ref[...]) + dot_nt(dv, wv_ref[...])
        normed, inverse = norm_parts(own_ref[rows, :].astype(f32))
        g1 = g1_ref[rows, :] + norm_back(normed, inverse, vec_ref[0:1, :], grad_n1)
        dh_ref[rows, :] = g1.astype(bf16)
        small_ref[4:5, :] += column_sum(dq.astype(f32))
        small_ref[5:6, :] += column_sum(dv.astype(f32))
        small_ref[6:7, :] += column_sum(grad_n1 * normed)
        small_ref[7:8, :] += column_sum(grad_n1)
        return carry

    lax.fori_loop(0, ROWS // 128, leave, 0)
    keep_ref[:D, :] = cross_keep_ref[...]
    send_ref[:D, :] = cross_send_ref[...]
    own, other = pack_halves(dot_tn(n1_ref[...], dq_ref[...]), dot_tn(n1_ref[...], dk_ref[...]))
    keep_ref[D : 2 * D, :] = own
    send_ref[D : 2 * D, :] = other.astype(bf16)
    own, other = pack_halves(dot_tn(n1_ref[...], dv_ref[...]), dot_tn(n2_ref[...], dqc_ref[...]))
    keep_ref[2 * D : 3 * D, :] = own
    send_ref[2 * D : 3 * D, :] = other.astype(bf16)
    grad = dot_tn(ctx_ref[...], low_ref[...])
    keep_ref[3 * D : 3 * D + HALF, :] = grad[:HALF]
    send_ref[3 * D : 3 * D + HALF, :] = grad[HALF:].astype(bf16)

    base = 3 * D + HALF
    cross_bias = cross_bias_ref[...].T[0:8, :]
    left = jnp.concatenate([small_ref[4:5, :], small_ref[0:1, :], jnp.zeros((6, D), f32)], 0)
    right = jnp.concatenate([small_ref[5:6, :], cross_bias[0:1, :], jnp.zeros((6, D), f32)], 0)
    own, other = pack_halves(left, right)
    shared = jnp.concatenate(
        [
            small_ref[6:7, :], small_ref[7:8, :], small_ref[3:4, :], small_ref[1:2, :], small_ref[2:3, :],
            feed_small_ref[3:4, :], feed_small_ref[1:2, :], feed_small_ref[2:3, :], feed_small_ref[0:1, :],
            jnp.zeros((3, D), f32),
        ],
        0,
    )
    tail = keep_ref.shape[0] - base
    rest = jnp.zeros((tail - 16, D), f32)
    keep_ref[base:, :] = jnp.concatenate([own[0:2], feed_small_ref[4:6, :], shared, rest], 0)
    send_ref[base:, :] = jnp.concatenate([other[0:2], feed_small_ref[6:8, :], shared, rest], 0).astype(bf16)


def whole(shape):
    return pl.BlockSpec(memory_space=pltpu.VMEM)


vmem = pl.BlockSpec(memory_space=pltpu.VMEM)
smem = pl.BlockSpec(memory_space=pltpu.SMEM)


def shaped(shape, dtype):
    return jax.ShapeDtypeStruct(shape, dtype)


def constant(shape):
    return pl.BlockSpec(shape, lambda step, core: (0,) * len(shape))


def call(kernel, name, scalars, operands, outs, scratch=(), flops=0, nbytes=0):
    return pl.pallas_call(
        kernel,
        out_shape=outs,
        in_specs=[smem] * len(scalars) + [vmem] * len(operands),
        out_specs=[vmem] * len(outs),
        scratch_shapes=list(scratch),
        cost_estimate=pl.CostEstimate(flops=flops, bytes_accessed=nbytes, transcendentals=0),
        name=name,
    )(*scalars, *operands)


def stage_list(count):
    stages = []
    stride = 1
    while stride < count:
        radix = 4 if count // stride % 4 == 0 else 2
        stages.append((stride, radix))
        stride = stride * radix
    return stages


def partner(count, stride, radix, turn):
    pairs = []
    for index in range(count):
        digit = index // stride % radix
        pairs.append((index, index + ((digit ^ turn) - digit) * stride))
    return pairs


def spread_kernel(radix, received, digit_ref, keep_in_ref, *refs):
    arrived = refs[:received]
    outs = refs[received:]
    digit = digit_ref[0]
    part = outs[0].shape[0]
    for turn, out_ref in enumerate(outs):
        rows = pl.ds(pl.multiple_of((digit ^ turn) * part, part), part)
        total = keep_in_ref[rows, :]
        for ref in arrived:
            total = total + ref[rows, :].astype(f32)
        out_ref[...] = total.astype(out_ref.dtype)


def last_kernel(keep_in_ref, *refs):
    total = keep_in_ref[...]
    for ref in refs[:-1]:
        total = total + ref[...].astype(f32)
    refs[-1][...] = total.astype(bf16)


def gather_kernel(digit_ref, *refs):
    out_ref = refs[-1]
    digit = digit_ref[0]
    part = refs[0].shape[0]
    for turn, ref in enumerate(refs[:-1]):
        out_ref[pl.ds(pl.multiple_of((digit ^ turn) * part, part), part), :] = ref[...]


def permute(value, axis, pairs):
    return lax.ppermute(value, axis, pairs)


def reduce_rows(keep, send, swap, name):
    count = lax.axis_size("dp")
    index = lax.axis_index("dp")
    stages = stage_list(count)
    arrived = [permute(send, "tp", swap)]
    current = keep
    digits = []
    for number, (stride, radix) in enumerate(stages):
        digit = (index // stride % radix).reshape(1)
        digits.append(digit)
        rows = current.shape[0] // radix
        outs = [shaped((rows, D), f32)] + [shaped((rows, D), bf16)] * (radix - 1)
        pieces = call(
            partial(spread_kernel, radix, len(arrived)), f"{name}_spread{number}", [digit], [current] + arrived, outs,
            nbytes=current.size * 8,
        )
        current = pieces[0]
        arrived = [
            permute(piece, "dp", partner(count, stride, radix, turn + 1)) for turn, piece in enumerate(pieces[1:])
        ]
    total = call(last_kernel, f"{name}_last", [], [current] + arrived, [shaped(current.shape, bf16)], nbytes=current.size * 8)[0]
    for number, (stride, radix) in reversed(list(enumerate(stages))):
        pieces = [total] + [
            permute(total, "dp", partner(count, stride, radix, turn)) for turn in range(1, radix)
        ]
        if number == 0:
            return pieces, digits[0]
        total = call(
            gather_kernel, f"{name}_gather{number}", [digits[number]], pieces, [shaped((total.shape[0] * radix, D), bf16)],
            nbytes=total.size * 8 * 2,
        )[0]


def assemble(digit, pieces, full_ref):
    part = pieces[0].shape[0]
    for turn, ref in enumerate(pieces):
        full_ref[pl.ds(pl.multiple_of((digit ^ turn) * part, part), part), :] = ref[...]


def feed_finish_kernel(count, digit_ref, *refs):
    w1_ref, w2_ref, wo_ref, full_ref = refs[count:]
    assemble(digit_ref[0], refs[:count], full_ref)
    half = w2_ref.shape[0]
    for part in range(half // D):
        w1_ref[:, part * D : part * D + D] = full_ref[part * D : part * D + D, :].astype(f32)
    w2_ref[...] = full_ref[half : 2 * half, :].astype(f32)
    wo_ref[...] = full_ref[2 * half : 2 * half + HALF, :].astype(f32)


def attention_finish_kernel(count, digit_ref, *refs):
    ck_ref, cv_ref, sq_ref, sk_ref, sv_ref, cq_ref, so_ref, small_ref, full_ref = refs[count:]
    assemble(digit_ref[0], refs[:count], full_ref)
    for part, (left, right) in enumerate(((ck_ref, cv_ref), (sq_ref, sk_ref), (sv_ref, cq_ref))):
        both = full_ref[part * D : part * D + D, :].astype(f32)
        left[...] = both[:, :HALF]
        right[...] = pltpu.roll(both, HALF, 1)[:, :HALF]
    so_ref[...] = full_ref[3 * D : 3 * D + HALF, :].astype(f32)
    small_ref[...] = full_ref[3 * D + HALF : 3 * D + HALF + 16, :].astype(f32)


def round_up(value, unit):
    return -(-value // unit) * unit


def local(
    hidden, frames, lengths, cotangent,
    ln1_gain, ln1_bias, sq_weight, sq_bias, sk_weight, sv_weight, sv_bias, so_weight, so_bias,
    ln2_gain, ln2_bias, cq_weight, cq_bias, ck_weight, cv_weight, cv_bias, co_weight, co_bias,
    ln3_gain, ln3_bias, fc1_weight, fc1_bias, fc2_weight, fc2_bias,
):
    tp_index = lax.axis_index("tp")
    core = tp_index.astype(jnp.int32).reshape(1)
    swap = [(0, 1), (1, 0)]
    half = fc1_weight.shape[1]
    wide = 2 * half
    frame_total = frames.shape[1]
    padded = round_up(frame_total, 128)

    columns = jnp.concatenate([sq_weight, sk_weight, sv_weight, cq_weight, ck_weight, cv_weight], 1)
    rows_pack = jnp.concatenate([so_weight, co_weight], 0)
    biases = jnp.concatenate([sq_bias, sv_bias, cq_bias, cv_bias, fc1_bias])
    columns_far = lax.ppermute(columns, "tp", swap)
    rows_far = lax.ppermute(rows_pack, "tp", swap)
    biases_far = lax.ppermute(biases, "tp", swap)
    fc1_far = lax.ppermute(fc1_weight, "tp", swap)
    fc2_far = lax.ppermute(fc2_weight, "tp", swap)

    def both_columns(number):
        cols = slice(number * HALF, number * HALF + HALF)
        return jnp.concatenate([columns[:, cols], columns_far[:, cols]], 1)

    wq, wk, wv, wcq, wck, wcv = [both_columns(number) for number in range(6)]
    wso = jnp.concatenate([so_weight, rows_far[:HALF]], 0)
    wco = jnp.concatenate([co_weight, rows_far[HALF:]], 0)
    w1 = jnp.concatenate([fc1_weight, fc1_far], 1)
    w2 = jnp.concatenate([fc2_weight, fc2_far], 0)
    bias_rows = [
        jnp.concatenate([biases[i * HALF : i * HALF + HALF], biases_far[i * HALF : i * HALF + HALF]]) for i in range(4)
    ]
    vec = jnp.stack(
        [ln1_gain, ln1_bias, so_bias, ln2_gain, ln2_bias, co_bias, ln3_gain, ln3_bias, fc2_bias] + bias_rows
        + [jnp.zeros((D,), bf16)] * 3
    ).astype(f32)
    b1 = jnp.concatenate([biases[4 * HALF :], biases_far[4 * HALF :]])[None, :].astype(f32)

    row_low = shaped((ROWS, D), bf16)
    row_wide = shaped((ROWS, D), f32)
    lse_shape = shaped((2 * ROWS, 128), f32)
    own, n1, q, k, v, ctx, r1, n2, qc, lse = call(
        self_forward_kernel, "self_forward", [core, lengths], [hidden, vec, wq, wk, wv, wso, wcq],
        [row_low] * 6 + [row_wide, row_low, row_low, lse_shape],
        flops=2 * ROWS * D * D * 5, nbytes=8 << 20,
    )
    frame_spec = pl.BlockSpec((1, frame_total, D), lambda step, core: (step_seq(step, core[0]), 0, 0))
    stored_spec = pl.BlockSpec(
        (1, padded, D), lambda step, core: (jnp.minimum(step, step_count(core[0]) - 1), 0, 0)
    )
    key_shape = shaped((STEPS, padded, D), bf16)
    ck, cv, ctx_cross, lse_cross = pl.pallas_call(
        partial(cross_forward_kernel, frame_total),
        out_shape=[key_shape, key_shape, row_low, lse_shape],
        grid_spec=pltpu.PrefetchScalarGridSpec(
            num_scalar_prefetch=1,
            grid=(STEPS,),
            in_specs=[frame_spec, constant((ROWS, D)), constant((16, D)), constant((D, D)), constant((D, D))],
            out_specs=[stored_spec, stored_spec, constant((ROWS, D)), constant((2 * ROWS, 128))],
        ),
        cost_estimate=pl.CostEstimate(flops=20 << 30, bytes_accessed=32 << 20, transcendentals=0),
        name="cross_forward",
    )(core, frames, qc, vec, wck, wcv)

    dp_count = lax.axis_size("dp")
    feed_rows = round_up(2 * half + HALF, 16 * dp_count)
    out_own, g2, dctx, feed_keep, feed_send, feed_small = call(
        feed_kernel, "feed", [core, lengths], [cotangent, r1, ctx_cross, vec, b1, wco, w1, w2],
        [row_low, row_wide, row_low, shaped((feed_rows, D), f32), shaped((feed_rows, D), bf16), shaped((8, D), f32)],
        scratch=[
            pltpu.VMEM((ROWS, D), bf16), pltpu.VMEM((ROWS, D), bf16), pltpu.VMEM((ROWS, wide), bf16),
            pltpu.VMEM((ROWS, wide), bf16), pltpu.VMEM((ROWS, D), bf16),
        ],
        flops=2 * ROWS * D * wide * 6, nbytes=16 << 20,
    )
    feed_pieces, feed_digit = reduce_rows(feed_keep, feed_send, swap, "feed")
    out_far = lax.ppermute(out_own, "tp", swap)

    dqc, cross_keep, cross_send, cross_bias = pl.pallas_call(
        partial(cross_backward_kernel, frame_total),
        out_shape=[row_low, shaped((D, D), f32), shaped((D, D), bf16), shaped((D, 128), f32)],
        grid_spec=pltpu.PrefetchScalarGridSpec(
            num_scalar_prefetch=1,
            grid=(STEPS,),
            in_specs=[
                frame_spec, stored_spec, stored_spec, constant((ROWS, D)), constant((ROWS, D)),
                constant((2 * ROWS, 128)),
            ],
            out_specs=[constant((ROWS, D)), constant((D, D)), constant((D, D)), constant((D, 128))],
            scratch_shapes=[
                pltpu.VMEM((D, padded), f32), pltpu.VMEM((D, padded), f32), pltpu.VMEM((2 * D, D), f32),
            ],
        ),
        cost_estimate=pl.CostEstimate(flops=40 << 30, bytes_accessed=32 << 20, transcendentals=0),
        name="cross_backward",
    )(core, frames, ck, cv, qc, dctx, lse_cross)

    attention_rows = round_up(3 * D + HALF + 16, 16 * dp_count)
    dh_own, keep, send = call(
        self_backward_kernel, "self_backward", [core, lengths],
        [own, vec, wq, wk, wv, wso, wcq, n1, q, k, v, ctx, r1, n2, lse, dqc, g2, feed_small, cross_bias, cross_keep, cross_send],
        [row_low, shaped((attention_rows, D), f32), shaped((attention_rows, D), bf16)],
        scratch=[pltpu.VMEM((ROWS, D), f32)] + [pltpu.VMEM((ROWS, D), bf16)] * 5
        + [pltpu.VMEM((ROWS, D), f32)] * 2 + [pltpu.VMEM((8, D), f32)],
        flops=2 * ROWS * D * D * 10, nbytes=8 << 20,
    )
    dh_far = lax.ppermute(dh_own, "tp", swap)
    pieces, digit = reduce_rows(keep, send, swap, "attention")

    grad_fc1, grad_fc2, grad_co = call(
        partial(feed_finish_kernel, len(feed_pieces)), "feed_finish", [feed_digit], feed_pieces,
        [shaped((D, half), f32), shaped((half, D), f32), shaped((HALF, D), f32)],
        scratch=[pltpu.VMEM((feed_rows, D), bf16)], nbytes=8 << 20,
    )
    narrow = shaped((D, HALF), f32)
    grad_ck, grad_cv, grad_sq, grad_sk, grad_sv, grad_cq, grad_so, small = call(
        partial(attention_finish_kernel, len(pieces)), "attention_finish", [digit], pieces,
        [narrow] * 6 + [shaped((HALF, D), f32), shaped((16, D), f32)],
        scratch=[pltpu.VMEM((attention_rows, D), bf16)], nbytes=8 << 20,
    )

    def group_rows(mine, far):
        first = jnp.where(tp_index == 0, mine, far)
        second = jnp.where(tp_index == 0, far, mine)
        return jnp.concatenate(
            [
                first[:FIRST_ROWS], second[:FIRST_ROWS],
                second[FIRST_ROWS : FIRST_ROWS + 2 * BLOCK + 2 * MID_LEN], first[FIRST_ROWS:],
            ],
            0,
        )

    return (
        group_rows(out_own, out_far),
        group_rows(dh_own, dh_far),
        small[4],
        small[5],
        grad_sq,
        small[0, :HALF],
        grad_sk,
        grad_sv,
        small[0, HALF:],
        grad_so,
        small[6],
        small[7],
        small[8],
        grad_cq,
        small[1, :HALF],
        grad_ck,
        grad_cv,
        small[1, HALF:],
        grad_co,
        small[9],
        small[10],
        small[11],
        grad_fc1,
        small[2:4].reshape(2 * D),
        grad_fc2,
        small[12],
    )


def solution(mesh):
    return jax.shard_map(
        local,
        mesh=mesh,
        in_specs=(
            P("dp", None),
            P("dp", None, None),
            P("dp"),
            P("dp", None),
            P(),
            P(),
            P(None, "tp"),
            P("tp"),
            P(None, "tp"),
            P(None, "tp"),
            P("tp"),
            P("tp", None),
            P(),
            P(),
            P(),
            P(None, "tp"),
            P("tp"),
            P(None, "tp"),
            P(None, "tp"),
            P("tp"),
            P("tp", None),
            P(),
            P(),
            P(),
            P(None, "tp"),
            P("tp"),
            P("tp", None),
            P(),
        ),
        out_specs=(
            P("dp", None),
            P("dp", None),
            P(),
            P(),
            P(None, "tp"),
            P("tp"),
            P(None, "tp"),
            P(None, "tp"),
            P("tp"),
            P("tp", None),
            P(),
            P(),
            P(),
            P(None, "tp"),
            P("tp"),
            P(None, "tp"),
            P(None, "tp"),
            P("tp"),
            P("tp", None),
            P(),
            P(),
            P(),
            P(None, "tp"),
            P("tp"),
            P("tp", None),
            P(),
        ),
        check_vma=False,
    )
```

```python
from functools import partial

import jax
import jax.numpy as jnp
from jax import lax
from jax.experimental import pallas as pl
from jax.experimental.pallas import tpu as pltpu
from jax.sharding import PartitionSpec as P

D = 384
HEAD = 64
HALF = D // 2
SHORT_LEN = 64
MID_LEN = 128
LONG_LEN = 448
SHORT_N = 8
MID_N = 2
LONG_N = 1
SEQ_TOTAL = SHORT_N + MID_N + LONG_N
GROUP_ROWS = SHORT_N * SHORT_LEN + MID_N * MID_LEN + LONG_N * LONG_LEN

HEAD_SHORTS = 3
BLOCK = 64
FIRST_ROWS = HEAD_SHORTS * BLOCK
ROWS = FIRST_ROWS + LONG_LEN
BLOCKS = ROWS // BLOCK
REGION_BLOCKS = LONG_LEN // BLOCK
STEPS = 7
PAIRS = D // 128
CHUNK = 256
WEIGHTS = 8


epsilon = 1e-05
masked = -1e30
scale = HEAD ** (-0.5)

f32 = jnp.float32
bf16 = jnp.bfloat16


def dot(left, right):
    return lax.dot_general(left, right, (((1,), (0,)), ((), ())), preferred_element_type=f32)


def dot_nt(left, right):
    return lax.dot_general(left, right, (((1,), (1,)), ((), ())), preferred_element_type=f32)


def dot_tn(left, right):
    return lax.dot_general(left, right, (((0,), (0,)), ((), ())), preferred_element_type=f32)


def norm_parts(values):
    row_mean = jnp.mean(values, -1, keepdims=True)
    centered = values - row_mean
    variance = jnp.mean(centered * centered, -1, keepdims=True)
    inverse = lax.rsqrt(variance + epsilon)
    return centered * inverse, inverse


def norm_back(normed, inverse, gain, incoming):
    scaled = incoming * gain
    return inverse * (
        scaled
        - jnp.mean(scaled, -1, keepdims=True)
        - normed * jnp.mean(scaled * normed, -1, keepdims=True)
    )


def column_sum(values):
    return jnp.sum(values, 0, keepdims=True)


def own_row(block, core):
    first = (core * HEAD_SHORTS + block) * BLOCK
    region = jnp.where(core == 0, SHORT_N * SHORT_LEN + MID_N * MID_LEN, 2 * FIRST_ROWS)
    return jnp.where(block < HEAD_SHORTS, first, region + (block - HEAD_SHORTS) * BLOCK)


def block_segment(block, core, lens):
    place = block - HEAD_SHORTS
    start = jnp.where(
        place < 2, place * BLOCK, jnp.where(place < 4, 2 * BLOCK, jnp.where(place < 6, 4 * BLOCK, 6 * BLOCK))
    )
    start = jnp.where((block < HEAD_SHORTS) | (core == 0), 0, start)
    seq = jnp.where(place < 2, 2 * HEAD_SHORTS + place, jnp.where(place < 4, SHORT_N, SHORT_N + 1))
    seq = jnp.where(core == 0, SEQ_TOTAL - 1, seq)
    seq = jnp.where(block < HEAD_SHORTS, core * HEAD_SHORTS + block, seq)
    padding = (core == 1) & (block == BLOCKS - 1)
    length = jnp.where(padding, BLOCK, lens[seq])
    return start, length, padding


def rows_of(index, count):
    return pl.ds(pl.multiple_of(index * count, count), count)


def head_masks():
    lane = lax.broadcasted_iota(jnp.int32, (BLOCK, 128), 1)
    low = (lane < HEAD).astype(f32)
    return low.astype(bf16), (1.0 - low).astype(bf16), lane < HEAD


def stacked(values, low, high):
    return jnp.concatenate([values * low, values * high], 0)


def joined(product, is_low):
    return jnp.where(is_low, product[:BLOCK], product[BLOCK:])


def self_mask(block, core, lens, key_count):
    start, length, _ = block_segment(block, core, lens)
    place = jnp.where(block < HEAD_SHORTS, 0, (block - HEAD_SHORTS) * BLOCK)
    row = lax.broadcasted_iota(jnp.int32, (2 * BLOCK, key_count), 0) & (BLOCK - 1)
    column = lax.broadcasted_iota(jnp.int32, (2 * BLOCK, key_count), 1)
    return (column <= row + place) & (column >= start) & (column < start + length)


def pack_halves(left, right):
    lane = lax.broadcasted_iota(jnp.int32, left.shape, 1) < HALF
    own = jnp.where(lane, left, pltpu.roll(right, HALF, 1))
    other = jnp.where(lane, pltpu.roll(left, HALF, 1), right)
    return own, other


def pack_kernel(*refs):
    weights, vectors, biases = refs[:WEIGHTS], refs[WEIGHTS : WEIGHTS + 9], refs[WEIGHTS + 9 : WEIGHTS + 14]
    pack_ref, vec_ref, bias_ref = refs[WEIGHTS + 14 :]
    for number, ref in enumerate(weights):
        pack_ref[number * HALF : number * HALF + HALF, :] = ref[...]
    vec_ref[...] = jnp.zeros(vec_ref.shape, f32)
    bias_ref[...] = jnp.zeros(bias_ref.shape, f32)
    for number, ref in enumerate(vectors):
        vec_ref[number : number + 1, :] = ref[...].astype(f32).reshape(1, D)
    for number, ref in enumerate(biases[:4]):
        at = number % 2 * HALF
        bias_ref[number // 2 : number // 2 + 1, at : at + HALF] = ref[...].astype(f32).reshape(1, HALF)
    for part in range(2):
        bias_ref[2 + part : 3 + part, :] = biases[4][part * D : part * D + D].astype(f32).reshape(1, D)
    pack_ref[WEIGHTS * HALF :, :] = bias_ref[...].astype(bf16)


def bias_rows(near_ref, far_ref):
    near, far = near_ref[...].astype(f32)[:8], far_ref[...].astype(f32)[:8]
    return pack_halves(near, far)[0], pack_halves(near, far)[1], near, far


def weight_copies(near_refs, far_ref, numbers, full_refs, sem):
    copies = []
    for index, (near_ref, number, full_ref) in enumerate(zip(near_refs, numbers, full_refs)):
        copies.append(pltpu.make_async_copy(near_ref, full_ref.at[pl.ds(0, HALF)], sem.at[2 * index]))
        copies.append(
            pltpu.make_async_copy(
                far_ref.at[pl.ds(number * HALF, HALF)], full_ref.at[pl.ds(HALF, HALF)], sem.at[2 * index + 1]
            )
        )
    for copy in copies:
        copy.start()
    return copies


def self_forward_kernel(
    core_ref, lens_ref, hidden_ref, vec_ref, near_ref, far_bias_ref, wq_near, wk_near, wv_near, wo_near, wc_near, far_ref,
    own_ref, n1_ref, q_ref, k_ref, v_ref, ctx_ref, r1_ref, n2_ref, qc_ref, lse_ref,
    wq_ref, wk_ref, wv_ref, wo_ref, wc_ref, sem,
):
    core = core_ref[0]
    copies = weight_copies(
        (wq_near, wk_near, wv_near, wo_near, wc_near), far_ref, (0, 1, 2, 6, 3),
        (wq_ref, wk_ref, wv_ref, wo_ref, wc_ref), sem,
    )
    first_bias, second_bias, _, _ = bias_rows(near_ref, far_bias_ref)
    q_bias, v_bias, c_bias = first_bias[0:1], second_bias[0:1], first_bias[1:2]

    def gather(block, carry):
        own_ref[rows_of(block, BLOCK), :] = hidden_ref[
            pl.ds(pl.multiple_of(own_row(block, core), BLOCK), BLOCK), :
        ]
        return carry

    lax.fori_loop(0, BLOCKS, gather, 0)
    for copy in copies:
        copy.wait()

    def project(chunk, carry):
        rows = rows_of(chunk, 128)
        normed, _ = norm_parts(own_ref[rows, :].astype(f32))
        n1 = (normed * vec_ref[0:1, :] + vec_ref[1:2, :]).astype(bf16)
        n1_ref[rows, :] = n1
        q_ref[rows, :] = (dot_nt(n1, wq_ref[...]) + q_bias).astype(bf16)
        k_ref[rows, :] = dot_nt(n1, wk_ref[...]).astype(bf16)
        v_ref[rows, :] = (dot_nt(n1, wv_ref[...]) + v_bias).astype(bf16)
        return carry

    lax.fori_loop(0, ROWS // 128, project, 0)
    low, high, is_low = head_masks()

    def attend(block, keys, key_count):
        rows = rows_of(block, BLOCK)
        allowed = self_mask(block, core, lens_ref, key_count)
        cols = [slice(pair * 128, pair * 128 + 128) for pair in range(PAIRS)]
        scores = [dot_nt(stacked(q_ref[rows, c] * scale, low, high), k_ref[keys, c]) for c in cols]
        scores = [jnp.where(allowed, values, masked) for values in scores]
        tops = [jnp.max(values, -1, keepdims=True) for values in scores]
        expo = [jnp.exp(values - top) for values, top in zip(scores, tops)]
        totals = [jnp.sum(values, -1, keepdims=True) for values in expo]
        parts = [dot(values.astype(bf16), v_ref[keys, c]) for values, c in zip(expo, cols)]
        for pair in range(PAIRS):
            ctx_ref[rows, cols[pair]] = joined(parts[pair] * (1.0 / totals[pair]), is_low).astype(bf16)
            lse_ref[rows_of(block, 2 * BLOCK), pair : pair + 1] = tops[pair] + jnp.log(totals[pair])

    def first(block, carry):
        attend(block, rows_of(block, BLOCK), BLOCK)
        return carry

    def second(block, carry):
        attend(block, pl.ds(FIRST_ROWS, LONG_LEN), LONG_LEN)
        return carry

    lax.fori_loop(0, HEAD_SHORTS, first, 0)
    lax.fori_loop(HEAD_SHORTS, BLOCKS, second, 0)

    def finish(chunk, carry):
        rows = rows_of(chunk, 128)
        r1 = own_ref[rows, :].astype(f32) + dot(ctx_ref[rows, :], wo_ref[...]) + vec_ref[2:3, :]
        r1_ref[rows, :] = r1
        normed, _ = norm_parts(r1)
        n2 = (normed * vec_ref[3:4, :] + vec_ref[4:5, :]).astype(bf16)
        n2_ref[rows, :] = n2
        qc_ref[rows, :] = (dot_nt(n2, wc_ref[...]) + c_bias).astype(bf16)
        return carry

    lax.fori_loop(0, ROWS // 128, finish, 0)


def step_count(core):
    return jnp.where(core == 0, HEAD_SHORTS + 1, STEPS)


def step_seq(step, core):
    step = jnp.minimum(step, step_count(core) - 1)
    return jnp.where(core == 0, jnp.where(step < HEAD_SHORTS, step, SEQ_TOTAL - 1), HEAD_SHORTS + step)


def step_blocks(step, core):
    count = jnp.where(step < HEAD_SHORTS, 1, jnp.where(core == 0, REGION_BLOCKS, jnp.where(step < 5, 1, 2)))
    first = jnp.where(step < 6, step, 7)
    return first, count


def cross_forward_kernel(
    frame_total, core_ref, frames_ref, qc_ref, near_ref, far_bias_ref, wk_near, wv_near, far_ref,
    k_ref, v_ref, ctx_ref, lse_ref, wk_ref, wv_ref, score_ref, sem,
):
    step = pl.program_id(0)
    core = core_ref[0]
    padded = k_ref.shape[1]
    tail = padded - 128
    low, high, is_low = head_masks()

    @pl.when(step == 0)
    def _():
        copies = weight_copies((wk_near, wv_near), far_ref, (4, 5), (wk_ref, wv_ref), sem)
        ctx_ref[ROWS - BLOCK :, :] = jnp.zeros((BLOCK, D), bf16)
        for copy in copies:
            copy.wait()

    @pl.when(step < step_count(core))
    def _():
        k_ref[0, padded - 64 :, :] = jnp.zeros((64, D), bf16)
        v_ref[0, padded - 64 :, :] = jnp.zeros((64, D), bf16)
        bias = bias_rows(near_ref, far_bias_ref)[1][1:2]
        for top in range(0, frame_total, 512):
            end = min(top + 512, frame_total)
            part = frames_ref[0, top:end, :]
            k_ref[0, top:end, :] = dot_nt(part, wk_ref[...]).astype(bf16)
            v_ref[0, top:end, :] = (dot_nt(part, wv_ref[...]) + bias).astype(bf16)
        first, count = step_blocks(step, core)

        def attend(turn, carry):
            block = first + turn
            rows = rows_of(block, BLOCK)
            inside = lax.broadcasted_iota(jnp.int32, (2 * BLOCK, 128), 1) < frame_total - tail

            def score(pair):
                cols = slice(pair * 128, pair * 128 + 128)
                query = stacked(qc_ref[rows, cols] * scale, low, high)
                tops = jnp.full((2 * BLOCK, 128), masked, f32)
                for at in range(0, padded, CHUNK):
                    values = dot_nt(query, k_ref[0, at : at + CHUNK, cols])
                    if at + CHUNK == padded:
                        values = jnp.concatenate(
                            [values[:, : CHUNK - 128], jnp.where(inside, values[:, CHUNK - 128 :], masked)], 1
                        )
                    score_ref[pair % 2, :, at : at + CHUNK] = values
                    for lane in range(0, CHUNK, 128):
                        tops = jnp.maximum(tops, values[:, lane : lane + 128])
                return jnp.max(tops, -1, keepdims=True)

            def weigh(pair, top):
                cols = slice(pair * 128, pair * 128 + 128)
                totals = jnp.zeros((2 * BLOCK, 128), f32)
                product = jnp.zeros((2 * BLOCK, 128), f32)
                for at in range(0, padded, CHUNK):
                    expo = jnp.exp(score_ref[pair % 2, :, at : at + CHUNK] - top)
                    for lane in range(0, CHUNK, 128):
                        totals = totals + expo[:, lane : lane + 128]
                    product = product + dot(expo.astype(bf16), v_ref[0, at : at + CHUNK, cols])
                total = jnp.sum(totals, -1, keepdims=True)
                ctx_ref[rows, cols] = joined(product * (1.0 / total), is_low).astype(bf16)
                lse_ref[rows_of(block, 2 * BLOCK), pair : pair + 1] = top + jnp.log(total)

            top = score(0)
            for pair in range(PAIRS):
                following = score(pair + 1) if pair + 1 < PAIRS else None
                weigh(pair, top)
                top = following
            return carry

        lax.fori_loop(0, count, attend, 0)


def feed_kernel(
    core_ref, lens_ref, cot_ref, r1_ref, ctx_ref, vec_ref, near_ref, far_bias_ref,
    wo_near, far_ref, w1_near, w1_far, w2_near, w2_far,
    out_ref, g2_ref, dctx_ref, keep_ref, send_ref, small_ref,
    top_ref, n3_ref, act_ref, pre_ref, low_ref, wo_ref, w1_ref, w2_ref, sem,
):
    core = core_ref[0]
    half = w2_near.shape[0]
    copies = weight_copies((wo_near,), far_ref, (7,), (wo_ref,), sem)
    copies.append(pltpu.make_async_copy(w1_near, w1_ref.at[:, pl.ds(0, half)], sem.at[2]))
    copies.append(pltpu.make_async_copy(w1_far, w1_ref.at[:, pl.ds(half, half)], sem.at[3]))
    copies.append(pltpu.make_async_copy(w2_near, w2_ref.at[pl.ds(0, half)], sem.at[4]))
    copies.append(pltpu.make_async_copy(w2_far, w2_ref.at[pl.ds(half, half)], sem.at[5]))
    for copy in copies[2:]:
        copy.start()
    _, _, near, far = bias_rows(near_ref, far_bias_ref)
    b1 = jnp.concatenate([near[2:3], near[3:4], far[2:3], far[3:4]], 1)

    def block_rows(block, carry):
        rows = rows_of(block, BLOCK)
        start, length, padding = block_segment(block, core, lens_ref)
        place = jnp.where(block < HEAD_SHORTS, 0, (block - HEAD_SHORTS) * BLOCK) - start
        length = jnp.where(padding, 0, length)
        row = lax.broadcasted_iota(jnp.int32, (BLOCK, D), 0) + place
        cot = cot_ref[pl.ds(pl.multiple_of(own_row(block, core), BLOCK), BLOCK), :].astype(f32)
        top_ref[rows, :] = jnp.where(row < length, cot, 0.0).astype(bf16)
        return carry

    lax.fori_loop(0, BLOCKS, block_rows, 0)
    small_ref[...] = jnp.zeros(small_ref.shape, f32)
    for copy in copies:
        copy.wait()

    def chunk_rows(chunk, sums):
        rows = rows_of(chunk, 128)
        r2 = r1_ref[rows, :] + dot(ctx_ref[rows, :], wo_ref[...]) + vec_ref[5:6, :]
        normed, inverse = norm_parts(r2)
        gain = vec_ref[6:7, :]
        n3 = (normed * gain + vec_ref[7:8, :]).astype(bf16)
        n3_ref[rows, :] = n3
        pre = dot(n3, w1_ref[...]) + b1
        phi = 0.5 * (1.0 + lax.erf(pre * (0.5**0.5)))
        act = (pre * phi).astype(bf16)
        act_ref[rows, :] = act
        out_ref[rows, :] = (r2 + dot(act, w2_ref[...]) + vec_ref[8:9, :]).astype(bf16)
        top = top_ref[rows, :]
        slope = phi + pre * (jnp.exp(-0.5 * pre * pre) * 0.3989422804014327)
        grad_pre = (dot_nt(top, w2_ref[...]) * slope).astype(bf16)
        pre_ref[rows, :] = grad_pre
        grad_n3 = dot_nt(grad_pre, w1_ref[...])
        top32 = top.astype(f32)
        g2 = top32 + norm_back(normed, inverse, gain, grad_n3)
        g2_ref[rows, :] = g2
        low = g2.astype(bf16)
        low_ref[rows, :] = low
        dctx_ref[rows, :] = dot_nt(low, wo_ref[...]).astype(bf16)
        small_ref[0:1, :] += column_sum(top32)
        small_ref[1:2, :] += column_sum(grad_n3 * normed)
        small_ref[2:3, :] += column_sum(grad_n3)
        small_ref[3:4, :] += column_sum(g2)
        bias = column_sum(grad_pre.astype(f32))
        for part in range(4):
            small_ref[4 + part : 5 + part, :] += bias[:, part * D : part * D + D]
        return sums

    lax.fori_loop(0, ROWS // 128, chunk_rows, 0)

    def mask_rows(block, carry):
        rows = rows_of(block, BLOCK)
        start, length, padding = block_segment(block, core, lens_ref)
        place = jnp.where(block < HEAD_SHORTS, 0, (block - HEAD_SHORTS) * BLOCK) - start
        row = lax.broadcasted_iota(jnp.int32, (BLOCK, D), 0) + place
        out_ref[rows, :] = jnp.where(row < length, out_ref[rows, :].astype(f32), 0.0).astype(bf16)
        return carry

    lax.fori_loop(0, BLOCKS, mask_rows, 0)
    for part in range(4):
        cols = slice(part * D, part * D + D)
        target, at = (keep_ref, part) if part < 2 else (send_ref, part - 2)
        target[at * D : at * D + D, :] = dot_tn(n3_ref[...], pre_ref[:, cols]).astype(target.dtype)
        grad = dot_tn(act_ref[:, cols], top_ref[...])
        target[half + at * D : half + at * D + D, :] = grad.astype(target.dtype)
    grad = dot_tn(ctx_ref[...], low_ref[...])
    keep_ref[2 * half : 2 * half + HALF, :] = grad[:HALF]
    send_ref[2 * half : 2 * half + HALF, :] = grad[HALF:].astype(bf16)
    extra = keep_ref.shape[0] - (2 * half + HALF)
    if extra:
        keep_ref[2 * half + HALF :, :] = jnp.zeros((extra, D), f32)
        send_ref[2 * half + HALF :, :] = jnp.zeros((extra, D), bf16)


def cross_backward_kernel(
    frame_total, first_step, core_ref, frames_ref, k_ref, v_ref, qc_ref, ctx_ref, dctx_ref, lse_ref,
    dq_in_ref, grad_in_ref, bias_in_ref, after_ref,
    dq_ref, grad_ref, bias_ref, dk_ref, dv_ref,
):
    step = pl.program_id(0) + first_step
    core = core_ref[0]
    padded = k_ref.shape[1]
    low, high, is_low = head_masks()

    @pl.when(step == first_step)
    def _():
        if first_step:
            dq_ref[:FIRST_ROWS, :] = dq_in_ref[:FIRST_ROWS, :]
            dq_ref[ROWS - BLOCK :, :] = jnp.zeros((BLOCK, D), bf16)
            grad_ref[...] = grad_in_ref[...]
            bias_ref[...] = bias_in_ref[...]
        else:
            grad_ref[...] = jnp.zeros(grad_ref.shape, f32)
            bias_ref[...] = jnp.zeros(bias_ref.shape, f32)

    @pl.when(step < step_count(core))
    def _():
        first, count = step_blocks(step, core)

        def attend(turn, carry):
            block = first + turn
            rows = rows_of(block, BLOCK)
            carried = turn > 0
            setups = []
            for pair in range(PAIRS):
                cols = slice(pair * 128, pair * 128 + 128)
                query = stacked(qc_ref[rows, cols] * scale, low, high)
                grad_out = stacked(dctx_ref[rows, cols], low, high)
                ctx = ctx_ref[rows, cols].astype(f32)
                spread = jnp.sum(grad_out.astype(f32) * jnp.concatenate([ctx, ctx], 0), -1, keepdims=True)
                lse = lse_ref[rows_of(block, 2 * BLOCK), pair : pair + 1]
                setups.append((cols, query, grad_out, query.T, grad_out.T, spread, lse))

            def begin(pair, at):
                cols, query, grad_out = setups[pair][:3]
                keys = slice(at, at + CHUNK)
                return dot_nt(query, k_ref[0, keys, cols]), dot_nt(grad_out, v_ref[0, keys, cols])

            def end(pair, at, scores, grad_weights):
                cols, _, _, query_t, grad_out_t, spread, lse = setups[pair]
                keys = slice(at, at + CHUNK)
                weights = jnp.exp(scores - lse)
                grad_scores = (weights * (grad_weights - spread)).astype(bf16)
                old_key = jnp.where(carried, dk_ref[cols, keys], 0.0)
                old_value = jnp.where(carried, dv_ref[cols, keys], 0.0)
                dk_ref[cols, keys] = old_key + dot(query_t, grad_scores)
                dv_ref[cols, keys] = old_value + dot(grad_out_t, weights.astype(bf16))
                return dot(grad_scores, k_ref[0, keys, cols])

            order = [(pair, at) for pair in range(PAIRS) for at in range(0, padded, CHUNK)]
            ahead = begin(*order[0])
            grad_query = None
            for index, (pair, at) in enumerate(order):
                now = ahead
                if index + 1 < len(order):
                    ahead = begin(*order[index + 1])
                part = end(pair, at, *now)
                grad_query = part if at == 0 else grad_query + part
                if at + CHUNK == padded:
                    dq_ref[rows, setups[pair][0]] = (joined(grad_query, is_low) * scale).astype(bf16)
            return carry

        lax.fori_loop(0, count, attend, 0)
        frames = frames_ref[0]
        grad_ref[:D, :] += dot(dk_ref[:, :frame_total].astype(bf16), frames)
        grad_value = dv_ref[:, :frame_total].astype(bf16)
        grad_ref[D:, :] += dot(grad_value, frames)
        bias_ref[:, 0:1] += jnp.sum(grad_value.astype(f32), -1, keepdims=True)


def self_attention_back_kernel(
    core_ref, lens_ref, vec_ref, wo_near, wc_near, far_ref, q_ref, k_ref, v_ref, ctx_ref, r1_ref, lse_ref,
    dqc_ref, g2_ref, after_ref,
    g1_ref, low_ref, dq_ref, dk_ref, dv_ref, small_ref,
    dctx_ref, dk_acc, dv_acc, wo_ref, wc_ref, sem,
):
    core = core_ref[0]
    copies = weight_copies((wo_near, wc_near), far_ref, (6, 3), (wo_ref, wc_ref), sem)
    small_ref[...] = jnp.zeros(small_ref.shape, f32)
    dk_acc[...] = jnp.zeros(dk_acc.shape, f32)
    dv_acc[...] = jnp.zeros(dv_acc.shape, f32)
    for copy in copies:
        copy.wait()

    def enter(chunk, carry):
        rows = rows_of(chunk, 128)
        dqc = dqc_ref[rows, :]
        grad_n2 = dot(dqc, wc_ref[...])
        normed, inverse = norm_parts(r1_ref[rows, :])
        g1 = g2_ref[rows, :] + norm_back(normed, inverse, vec_ref[3:4, :], grad_n2)
        g1_ref[rows, :] = g1
        low = g1.astype(bf16)
        low_ref[rows, :] = low
        dctx_ref[rows, :] = dot_nt(low, wo_ref[...]).astype(bf16)
        small_ref[0:1, :] += column_sum(dqc.astype(f32))
        small_ref[1:2, :] += column_sum(grad_n2 * normed)
        small_ref[2:3, :] += column_sum(grad_n2)
        small_ref[3:4, :] += column_sum(g1)
        return carry

    lax.fori_loop(0, ROWS // 128, enter, 0)
    low, high, is_low = head_masks()

    def attend(block, keys, key_count, store):
        rows = rows_of(block, BLOCK)
        allowed = self_mask(block, core, lens_ref, key_count)
        cols = [slice(pair * 128, pair * 128 + 128) for pair in range(PAIRS)]
        queries = [stacked(q_ref[rows, c] * scale, low, high) for c in cols]
        grad_outs = [stacked(dctx_ref[rows, c], low, high) for c in cols]
        ctxs = [ctx_ref[rows, c].astype(f32) for c in cols]
        spreads = [
            jnp.sum(grad_out.astype(f32) * jnp.concatenate([ctx, ctx], 0), -1, keepdims=True)
            for grad_out, ctx in zip(grad_outs, ctxs)
        ]
        scores = [dot_nt(query, k_ref[keys, c]) for query, c in zip(queries, cols)]
        grad_weights = [dot_nt(grad_out, v_ref[keys, c]) for grad_out, c in zip(grad_outs, cols)]
        for pair, c in enumerate(cols):
            lse = lse_ref[rows_of(block, 2 * BLOCK), pair : pair + 1]
            weights = jnp.exp(jnp.where(allowed, scores[pair] - lse, masked))
            grad_scores = (weights * (grad_weights[pair] - spreads[pair])).astype(bf16)
            dq_ref[rows, c] = (joined(dot(grad_scores, k_ref[keys, c]), is_low) * scale).astype(bf16)
            store(rows, c, queries[pair], grad_outs[pair], weights.astype(bf16), grad_scores)

    def store_block(rows, cols, query, grad_out, weights, grad_scores):
        dk_ref[rows, cols] = dot_tn(grad_scores, query).astype(bf16)
        dv_ref[rows, cols] = dot_tn(weights, grad_out).astype(bf16)

    def store_region(rows, cols, query, grad_out, weights, grad_scores):
        dk_acc[cols, :] += dot(query.T, grad_scores)
        dv_acc[cols, :] += dot(grad_out.T, weights)

    def first(block, carry):
        attend(block, rows_of(block, BLOCK), BLOCK, store_block)
        return carry

    def second(block, carry):
        attend(block, pl.ds(FIRST_ROWS, LONG_LEN), LONG_LEN, store_region)
        return carry

    lax.fori_loop(0, HEAD_SHORTS, first, 0)
    lax.fori_loop(HEAD_SHORTS, BLOCKS, second, 0)
    dk_ref[FIRST_ROWS:, :] = dk_acc[...].T.astype(bf16)
    dv_ref[FIRST_ROWS:, :] = dv_acc[...].T.astype(bf16)


def self_finish_kernel(
    own_ref, vec_ref, wq_near, wk_near, wv_near, far_ref, n1_ref, n2_ref, ctx_ref,
    g1_ref, low_ref, dq_ref, dk_ref, dv_ref, dqc_ref, back_small_ref, feed_small_ref, cross_bias_ref, cross_ref, after_ref,
    dh_ref, keep_ref, send_ref,
    small_ref, wq_ref, wk_ref, wv_ref, sem,
):
    copies = weight_copies((wq_near, wk_near, wv_near), far_ref, (0, 1, 2), (wq_ref, wk_ref, wv_ref), sem)
    small_ref[...] = jnp.zeros(small_ref.shape, f32)
    for copy in copies:
        copy.wait()

    def leave(chunk, carry):
        rows = rows_of(chunk, 128)
        dq, dk, dv = dq_ref[rows, :], dk_ref[rows, :], dv_ref[rows, :]
        grad_n1 = dot(dq, wq_ref[...]) + dot(dk, wk_ref[...]) + dot(dv, wv_ref[...])
        normed, inverse = norm_parts(own_ref[rows, :].astype(f32))
        g1 = g1_ref[rows, :] + norm_back(normed, inverse, vec_ref[0:1, :], grad_n1)
        dh_ref[rows, :] = g1.astype(bf16)
        small_ref[4:5, :] += column_sum(dq.astype(f32))
        small_ref[5:6, :] += column_sum(dv.astype(f32))
        small_ref[6:7, :] += column_sum(grad_n1 * normed)
        small_ref[7:8, :] += column_sum(grad_n1)
        return carry

    lax.fori_loop(0, ROWS // 128, leave, 0)

    def place(number, grad):
        rows = slice(number * HALF, number * HALF + HALF)
        keep_ref[rows, :] = grad[:HALF]
        send_ref[rows, :] = grad[HALF:].astype(bf16)

    place(0, cross_ref[:D, :])
    place(1, cross_ref[D:, :])
    place(2, dot_tn(dq_ref[...], n1_ref[...]))
    place(3, dot_tn(dk_ref[...], n1_ref[...]))
    place(4, dot_tn(dv_ref[...], n1_ref[...]))
    place(5, dot_tn(dqc_ref[...], n2_ref[...]))
    place(6, dot_tn(ctx_ref[...], low_ref[...]))

    base = 7 * HALF
    cross_bias = cross_bias_ref[...].T[0:8, :]
    left = jnp.concatenate([small_ref[4:5, :], back_small_ref[0:1, :], jnp.zeros((6, D), f32)], 0)
    right = jnp.concatenate([small_ref[5:6, :], cross_bias[0:1, :], jnp.zeros((6, D), f32)], 0)
    own, other = pack_halves(left, right)
    shared = jnp.concatenate(
        [
            small_ref[6:7, :], small_ref[7:8, :], back_small_ref[3:4, :], back_small_ref[1:2, :], back_small_ref[2:3, :],
            feed_small_ref[3:4, :], feed_small_ref[1:2, :], feed_small_ref[2:3, :], feed_small_ref[0:1, :],
            jnp.zeros((3, D), f32),
        ],
        0,
    )
    tail = keep_ref.shape[0] - base
    rest = jnp.zeros((tail - 16, D), f32)
    keep_ref[base:, :] = jnp.concatenate([own[0:2], feed_small_ref[4:6, :], shared, rest], 0)
    send_ref[base:, :] = jnp.concatenate([other[0:2], feed_small_ref[6:8, :], shared, rest], 0).astype(bf16)


vmem = pl.BlockSpec(memory_space=pltpu.VMEM)
smem = pl.BlockSpec(memory_space=pltpu.SMEM)
anywhere = pl.BlockSpec(memory_space=pl.ANY)


def shaped(shape, dtype):
    return jax.ShapeDtypeStruct(shape, dtype)


def constant(shape):
    return pl.BlockSpec(shape, lambda step, core: (0,) * len(shape))


def call(kernel, name, scalars, operands, outs, scratch=(), flops=0, nbytes=0, far=()):
    return pl.pallas_call(
        kernel,
        out_shape=outs,
        in_specs=[smem] * len(scalars) + [anywhere if place in far else vmem for place in range(len(operands))],
        out_specs=[vmem] * len(outs),
        scratch_shapes=list(scratch),
        cost_estimate=pl.CostEstimate(flops=flops, bytes_accessed=nbytes, transcendentals=0),
        name=name,
    )(*scalars, *operands)


def stage_list(count):
    stages = []
    stride = 1
    while stride < count:
        radix = 4 if count // stride % 4 == 0 else 2
        stages.append((stride, radix))
        stride = stride * radix
    return stages


def partner(count, stride, radix, turn):
    pairs = []
    for index in range(count):
        digit = index // stride % radix
        pairs.append((index, index + ((digit ^ turn) - digit) * stride))
    return pairs


def spread_kernel(radix, received, digit_ref, keep_in_ref, *refs):
    arrived = refs[:received]
    outs = refs[received:]
    digit = digit_ref[0]
    part = outs[0].shape[0]
    for turn, out_ref in enumerate(outs):
        rows = pl.ds(pl.multiple_of((digit ^ turn) * part, part), part)
        total = keep_in_ref[rows, :]
        for ref in arrived:
            total = total + ref[rows, :].astype(f32)
        out_ref[...] = total.astype(out_ref.dtype)


def last_kernel(keep_in_ref, *refs):
    total = keep_in_ref[...]
    for ref in refs[:-1]:
        total = total + ref[...].astype(f32)
    refs[-1][...] = total.astype(bf16)


def gather_kernel(digit_ref, *refs):
    out_ref = refs[-1]
    digit = digit_ref[0]
    part = refs[0].shape[0]
    for turn, ref in enumerate(refs[:-1]):
        out_ref[pl.ds(pl.multiple_of((digit ^ turn) * part, part), part), :] = ref[...]


def permute(value, axis, pairs):
    return lax.ppermute(value, axis, pairs)


class RowSum:
    def __init__(self, keep, send, swap, name):
        self.count = lax.axis_size("dp")
        self.index = lax.axis_index("dp")
        self.stages = stage_list(self.count)
        self.name = name
        self.current = keep
        self.arrived = [lax.ppermute(send, "tp", swap)]
        self.digits = [(self.index // stride % radix).reshape(1) for stride, radix in self.stages]

    def permute(self, value, number, turn):
        stride, radix = self.stages[number]
        return lax.ppermute(value, "dp", partner(self.count, stride, radix, turn))

    def spread(self, number):
        _, radix = self.stages[number]
        rows = self.current.shape[0] // radix
        pieces = call(
            partial(spread_kernel, radix, len(self.arrived)), f"{self.name}_spread{number}",
            [self.digits[number]], [self.current] + self.arrived,
            [shaped((rows, D), f32)] + [shaped((rows, D), bf16)] * (radix - 1), nbytes=self.current.size * 8,
        )
        self.current = pieces[0]
        self.arrived = [self.permute(piece, number, turn + 1) for turn, piece in enumerate(pieces[1:])]
        return pieces[0]

    def last(self):
        total = call(
            last_kernel, f"{self.name}_last", [], [self.current] + self.arrived,
            [shaped(self.current.shape, bf16)], nbytes=self.current.size * 8,
        )[0]
        return self.widen(total, len(self.stages) - 1)

    def widen(self, total, number):
        self.pieces = [total] + [self.permute(total, number, turn) for turn in range(1, self.stages[number][1])]
        return total

    def gather(self, number):
        total = self.pieces[0]
        total = call(
            gather_kernel, f"{self.name}_gather{number}", [self.digits[number]], self.pieces,
            [shaped((total.shape[0] * self.stages[number][1], D), bf16)], nbytes=total.size * 16,
        )[0]
        return self.widen(total, number - 1)

    def steps(self):
        numbers = range(len(self.stages))
        return (
            [partial(self.spread, number) for number in numbers]
            + [self.last]
            + [partial(self.gather, number) for number in reversed(numbers) if number]
        )


def assemble(digit, pieces, full_ref):
    part = pieces[0].shape[0]
    for turn, ref in enumerate(pieces):
        full_ref[pl.ds(pl.multiple_of((digit ^ turn) * part, part), part), :] = ref[...]


def feed_finish_kernel(count, digit_ref, *refs):
    w1_ref, w2_ref, wo_ref, full_ref = refs[count:]
    assemble(digit_ref[0], refs[:count], full_ref)
    half = w2_ref.shape[0]
    for part in range(half // D):
        w1_ref[:, part * D : part * D + D] = full_ref[part * D : part * D + D, :].astype(f32)
    w2_ref[...] = full_ref[half : 2 * half, :].astype(f32)
    wo_ref[...] = full_ref[2 * half : 2 * half + HALF, :].astype(f32)


def attention_finish_kernel(count, digit_ref, *refs):
    outs, full_ref = refs[count:-1], refs[-1]
    assemble(digit_ref[0], refs[:count], full_ref)
    for number, ref in enumerate(outs[:7]):
        ref[...] = full_ref[number * HALF : number * HALF + HALF, :].astype(f32)
    small = full_ref[7 * HALF : 7 * HALF + 16, :].astype(f32)
    for number, ref in enumerate(outs[7:11]):
        at = number % 2 * HALF
        ref[...] = small[number // 2 : number // 2 + 1, at : at + HALF].reshape(HALF)
    for part in range(2):
        outs[11][part * D : part * D + D] = small[2 + part : 3 + part, :].reshape(D)
    for number, ref in enumerate(outs[12:]):
        ref[...] = small[4 + number : 5 + number, :].reshape(D)


def round_up(value, unit):
    return -(-value // unit) * unit


def local(
    hidden, frames, lengths, cotangent,
    ln1_gain, ln1_bias, sq_weight, sq_bias, sk_weight, sv_weight, sv_bias, so_weight, so_bias,
    ln2_gain, ln2_bias, cq_weight, cq_bias, ck_weight, cv_weight, cv_bias, co_weight, co_bias,
    ln3_gain, ln3_bias, fc1_weight, fc1_bias, fc2_weight, fc2_bias,
):
    tp_index = lax.axis_index("tp")
    core = tp_index.astype(jnp.int32).reshape(1)
    swap = [(0, 1), (1, 0)]
    half = fc1_weight.shape[1]
    wide = 2 * half
    frame_total = frames.shape[1]
    padded = round_up(frame_total, CHUNK)

    near = [w.T for w in (sq_weight, sk_weight, sv_weight, cq_weight, ck_weight, cv_weight)] + [so_weight, co_weight]
    vectors = [ln1_gain, ln1_bias, so_bias, ln2_gain, ln2_bias, co_bias, ln3_gain, ln3_bias, fc2_bias]
    pack, vec, near_bias = call(
        pack_kernel, "pack", [], near + vectors + [sq_bias, sv_bias, cq_bias, cv_bias, fc1_bias],
        [shaped((WEIGHTS * HALF + 16, D), bf16), shaped((16, D), f32), shaped((16, D), f32)],
        nbytes=4 << 20,
    )
    far = lax.ppermute(pack, "tp", swap)
    fc1_far = lax.ppermute(fc1_weight, "tp", swap)
    fc2_far = lax.ppermute(fc2_weight, "tp", swap)
    far_bias = far[WEIGHTS * HALF :]

    row_low = shaped((ROWS, D), bf16)
    row_wide = shaped((ROWS, D), f32)
    lse_shape = shaped((2 * ROWS, 128), f32)
    square = pltpu.VMEM((D, D), bf16)
    own, n1, q, k, v, ctx, r1, n2, qc, lse = call(
        self_forward_kernel, "self_forward", [core, lengths],
        [hidden, vec, near_bias, far_bias, near[0], near[1], near[2], near[6], near[3], far],
        [row_low] * 6 + [row_wide, row_low, row_low, lse_shape],
        scratch=[square] * 5 + [pltpu.SemaphoreType.DMA((10,))],
        flops=2 * ROWS * D * D * 5, nbytes=8 << 20, far=range(4, 10),
    )

    def cross_specs(first):
        frame_spec = pl.BlockSpec((1, frame_total, D), lambda step, core: (step_seq(step + first, core[0]), 0, 0))
        stored_spec = pl.BlockSpec(
            (1, padded, D), lambda step, core: (jnp.minimum(step + first, step_count(core[0]) - 1), 0, 0)
        )
        return frame_spec, stored_spec

    frame_spec, stored_spec = cross_specs(0)
    key_shape = shaped((STEPS, padded, D), bf16)
    ck, cv, ctx_cross, lse_cross = pl.pallas_call(
        partial(cross_forward_kernel, frame_total),
        out_shape=[key_shape, key_shape, row_low, lse_shape],
        grid_spec=pltpu.PrefetchScalarGridSpec(
            num_scalar_prefetch=1,
            grid=(STEPS,),
            in_specs=[frame_spec, constant((ROWS, D)), constant((16, D)), constant((16, D))] + [anywhere] * 3,
            out_specs=[stored_spec, stored_spec, constant((ROWS, D)), constant((2 * ROWS, 128))],
            scratch_shapes=[square, square, pltpu.VMEM((2, 2 * BLOCK, padded), f32), pltpu.SemaphoreType.DMA((4,))],
        ),
        cost_estimate=pl.CostEstimate(flops=20 << 30, bytes_accessed=32 << 20, transcendentals=0),
        name="cross_forward",
    )(core, frames, qc, near_bias, far_bias, near[4], near[5], far)

    dp_count = lax.axis_size("dp")
    feed_rows = round_up(2 * half + HALF, 16 * dp_count)
    out_own, g2, dctx, feed_keep, feed_send, feed_small = call(
        feed_kernel, "feed", [core, lengths],
        [cotangent, r1, ctx_cross, vec, near_bias, far_bias, near[7], far, fc1_weight, fc1_far, fc2_weight, fc2_far],
        [row_low, row_wide, row_low, shaped((feed_rows, D), f32), shaped((feed_rows, D), bf16), shaped((8, D), f32)],
        scratch=[
            pltpu.VMEM((ROWS, D), bf16), pltpu.VMEM((ROWS, D), bf16), pltpu.VMEM((ROWS, wide), bf16),
            pltpu.VMEM((ROWS, wide), bf16), pltpu.VMEM((ROWS, D), bf16), square,
            pltpu.VMEM((D, wide), bf16), pltpu.VMEM((wide, D), bf16), pltpu.SemaphoreType.DMA((6,)),
        ],
        flops=2 * ROWS * D * wide * 6, nbytes=16 << 20, far=range(6, 12),
    )
    feed_sum = RowSum(feed_keep, feed_send, swap, "feed")
    pending = feed_sum.steps()

    def advance():
        return pending.pop(0)() if pending else feed_sum.current

    def cross_backward(first, count, dq_in, grad_in, bias_in, after):
        frame_spec, stored_spec = cross_specs(first)
        return pl.pallas_call(
            partial(cross_backward_kernel, frame_total, first),
            out_shape=[row_low, shaped((2 * D, D), f32), shaped((D, 128), f32)],
            grid_spec=pltpu.PrefetchScalarGridSpec(
                num_scalar_prefetch=1,
                grid=(count,),
                in_specs=[frame_spec, stored_spec, stored_spec] + [constant((ROWS, D))] * 3
                + [constant((2 * ROWS, 128)), constant((ROWS, D)), constant((2 * D, D)), constant((D, 128)), anywhere],
                out_specs=[constant((ROWS, D)), constant((2 * D, D)), constant((D, 128))],
                scratch_shapes=[pltpu.VMEM((D, padded), f32), pltpu.VMEM((D, padded), f32)],
            ),
            cost_estimate=pl.CostEstimate(flops=20 << 30, bytes_accessed=16 << 20, transcendentals=0),
            name=f"cross_backward{first}",
        )(core, frames, ck, cv, qc, ctx_cross, dctx, lse_cross, dq_in, grad_in, bias_in, after)

    dqc, cross_grad, cross_bias = cross_backward(0, HEAD_SHORTS, qc, feed_keep[: 2 * D], lse_cross[:D], feed_small)
    after = advance()
    dqc, cross_grad, cross_bias = cross_backward(
        HEAD_SHORTS, STEPS - HEAD_SHORTS, dqc, cross_grad, cross_bias, after
    )
    after = advance()
    half_acc = pltpu.VMEM((D, LONG_LEN), f32)
    g1, low, dq, dk, dv, back_small = call(
        self_attention_back_kernel, "self_attention_back", [core, lengths],
        [vec, near[6], near[3], far, q, k, v, ctx, r1, lse, dqc, g2, after],
        [row_wide, row_low, row_low, row_low, row_low, shaped((8, D), f32)],
        scratch=[pltpu.VMEM((ROWS, D), bf16), half_acc, half_acc, square, square, pltpu.SemaphoreType.DMA((4,))],
        flops=2 * ROWS * D * D * 10, nbytes=8 << 20, far=(1, 2, 3, 12),
    )
    after = advance()
    attention_rows = round_up(7 * HALF + 16, 16 * dp_count)
    dh_own, keep, send = call(
        self_finish_kernel, "self_finish", [],
        [own, vec, near[0], near[1], near[2], far, n1, n2, ctx, g1, low, dq, dk, dv, dqc, back_small, feed_small,
         cross_bias, cross_grad, after],
        [row_low, shaped((attention_rows, D), f32), shaped((attention_rows, D), bf16)],
        scratch=[pltpu.VMEM((8, D), f32), square, square, square, pltpu.SemaphoreType.DMA((6,))],
        flops=2 * ROWS * D * D * 10, nbytes=8 << 20, far=(2, 3, 4, 5, 19),
    )
    attention_sum = RowSum(keep, send, swap, "attention")
    while pending:
        advance()
    out_far = lax.ppermute(out_own, "tp", swap)
    dh_far = lax.ppermute(dh_own, "tp", swap)
    for step in attention_sum.steps():
        step()
    feed_pieces, pieces = feed_sum.pieces, attention_sum.pieces

    grad_fc1, grad_fc2, grad_co = call(
        partial(feed_finish_kernel, len(feed_pieces)), "feed_finish", [feed_sum.digits[0]], feed_pieces,
        [shaped((D, half), f32), shaped((half, D), f32), shaped((HALF, D), f32)],
        scratch=[pltpu.VMEM((feed_rows, D), bf16)], nbytes=8 << 20,
    )
    (
        grad_ck, grad_cv, grad_sq, grad_sk, grad_sv, grad_cq, grad_so,
        grad_sq_bias, grad_sv_bias, grad_cq_bias, grad_cv_bias, grad_fc1_bias,
        grad_ln1_gain, grad_ln1_bias, grad_so_bias, grad_ln2_gain, grad_ln2_bias,
        grad_co_bias, grad_ln3_gain, grad_ln3_bias, grad_fc2_bias,
    ) = call(
        partial(attention_finish_kernel, len(pieces)), "attention_finish", [attention_sum.digits[0]], pieces,
        [shaped((HALF, D), f32)] * 7 + [shaped((HALF,), f32)] * 4 + [shaped((half,), f32)] + [shaped((D,), f32)] * 9,
        scratch=[pltpu.VMEM((attention_rows, D), bf16)], nbytes=8 << 20,
    )

    def group_rows(mine, far):
        first = jnp.where(tp_index == 0, mine, far)
        second = jnp.where(tp_index == 0, far, mine)
        return jnp.concatenate(
            [
                first[:FIRST_ROWS], second[:FIRST_ROWS],
                second[FIRST_ROWS : FIRST_ROWS + 2 * BLOCK + 2 * MID_LEN], first[FIRST_ROWS:],
            ],
            0,
        )

    return (
        group_rows(out_own, out_far),
        group_rows(dh_own, dh_far),
        grad_ln1_gain,
        grad_ln1_bias,
        grad_sq.T,
        grad_sq_bias,
        grad_sk.T,
        grad_sv.T,
        grad_sv_bias,
        grad_so,
        grad_so_bias,
        grad_ln2_gain,
        grad_ln2_bias,
        grad_cq.T,
        grad_cq_bias,
        grad_ck.T,
        grad_cv.T,
        grad_cv_bias,
        grad_co,
        grad_co_bias,
        grad_ln3_gain,
        grad_ln3_bias,
        grad_fc1,
        grad_fc1_bias,
        grad_fc2,
        grad_fc2_bias,
    )


def solution(mesh):
    return jax.shard_map(
        local,
        mesh=mesh,
        in_specs=(
            P("dp", None),
            P("dp", None, None),
            P("dp"),
            P("dp", None),
            P(),
            P(),
            P(None, "tp"),
            P("tp"),
            P(None, "tp"),
            P(None, "tp"),
            P("tp"),
            P("tp", None),
            P(),
            P(),
            P(),
            P(None, "tp"),
            P("tp"),
            P(None, "tp"),
            P(None, "tp"),
            P("tp"),
            P("tp", None),
            P(),
            P(),
            P(),
            P(None, "tp"),
            P("tp"),
            P("tp", None),
            P(),
        ),
        out_specs=(
            P("dp", None),
            P("dp", None),
            P(),
            P(),
            P(None, "tp"),
            P("tp"),
            P(None, "tp"),
            P(None, "tp"),
            P("tp"),
            P("tp", None),
            P(),
            P(),
            P(),
            P(None, "tp"),
            P("tp"),
            P(None, "tp"),
            P(None, "tp"),
            P("tp"),
            P("tp", None),
            P(),
            P(),
            P(),
            P(None, "tp"),
            P("tp"),
            P("tp", None),
            P(),
        ),
        check_vma=False,
    )
```

```python
from functools import partial

import jax
import jax.numpy as jnp
from jax import lax
from jax.experimental import pallas as pl
from jax.experimental.pallas import tpu as pltpu
from jax.sharding import PartitionSpec as P


D = 384
HEAD = 64
HALF = D // 2
SHORT_LEN = 64
MID_LEN = 128
LONG_LEN = 448
SHORT_N = 8
MID_N = 2
LONG_N = 1
SEQ_TOTAL = SHORT_N + MID_N + LONG_N

HEAD_SHORTS = 3
BLOCK = 64
FIRST_ROWS = HEAD_SHORTS * BLOCK
ROWS = FIRST_ROWS + LONG_LEN
BLOCKS = ROWS // BLOCK
REGION_BLOCKS = LONG_LEN // BLOCK
STEPS = 7
PAIRS = D // 128
CHUNK = 256
WEIGHTS = 8
LINES = 320
SMALL = 24


epsilon = 1e-05
masked = -1e30
scale = HEAD ** (-0.5)

f32 = jnp.float32
bf16 = jnp.bfloat16


def round_up(value, unit):
    return -(-value // unit) * unit


def dot(left, right):
    return lax.dot_general(left, right, (((1,), (0,)), ((), ())), preferred_element_type=f32)


def dot_nt(left, right):
    return lax.dot_general(left, right, (((1,), (1,)), ((), ())), preferred_element_type=f32)


def dot_tn(left, right):
    return lax.dot_general(left, right, (((0,), (0,)), ((), ())), preferred_element_type=f32)


def norm_parts(values):
    row_mean = jnp.mean(values, -1, keepdims=True)
    centered = values - row_mean
    variance = jnp.mean(centered * centered, -1, keepdims=True)
    inverse = lax.rsqrt(variance + epsilon)
    return centered * inverse, inverse


def norm_back(normed, inverse, gain, incoming):
    scaled = incoming * gain
    return inverse * (
        scaled
        - jnp.mean(scaled, -1, keepdims=True)
        - normed * jnp.mean(scaled * normed, -1, keepdims=True)
    )


def column_sum(values):
    return jnp.sum(values, 0, keepdims=True)


def own_row(block, core):
    first = (core * HEAD_SHORTS + block) * BLOCK
    region = jnp.where(core == 0, SHORT_N * SHORT_LEN + MID_N * MID_LEN, 2 * FIRST_ROWS)
    return jnp.where(block < HEAD_SHORTS, first, region + (block - HEAD_SHORTS) * BLOCK)


def block_segment(block, core, lens):
    place = block - HEAD_SHORTS
    start = jnp.where(
        place < 2, place * BLOCK, jnp.where(place < 4, 2 * BLOCK, jnp.where(place < 6, 4 * BLOCK, 6 * BLOCK))
    )
    start = jnp.where((block < HEAD_SHORTS) | (core == 0), 0, start)
    seq = jnp.where(place < 2, 2 * HEAD_SHORTS + place, jnp.where(place < 4, SHORT_N, SHORT_N + 1))
    seq = jnp.where(core == 0, SEQ_TOTAL - 1, seq)
    seq = jnp.where(block < HEAD_SHORTS, core * HEAD_SHORTS + block, seq)
    padding = (core == 1) & (block == BLOCKS - 1)
    length = jnp.where(padding, BLOCK, lens[seq])
    return start, length, padding


def rows_of(index, count):
    return pl.ds(pl.multiple_of(index * count, count), count)


def head_masks():
    lane = lax.broadcasted_iota(jnp.int32, (BLOCK, 128), 1)
    low = (lane < HEAD).astype(f32)
    return low.astype(bf16), (1.0 - low).astype(bf16), lane < HEAD


def stacked(values, low, high):
    return jnp.concatenate([values * low, values * high], 0)


def joined(product, is_low):
    return jnp.where(is_low, product[:BLOCK], product[BLOCK:])


def key_span(block):
    if block < HEAD_SHORTS:
        return block * BLOCK, BLOCK
    return FIRST_ROWS, min(LONG_LEN, round_up((block - HEAD_SHORTS + 1) * BLOCK, 128))


def self_mask(block, core, lens, key_count):
    start, length, _ = block_segment(block, core, lens)
    place = jnp.where(block < HEAD_SHORTS, 0, (block - HEAD_SHORTS) * BLOCK)
    row = lax.broadcasted_iota(jnp.int32, (2 * BLOCK, key_count), 0) & (BLOCK - 1)
    column = lax.broadcasted_iota(jnp.int32, (2 * BLOCK, key_count), 1)
    return (column <= row + place) & (column >= start) & (column < start + length)


def pack_halves(left, right):
    lane = lax.broadcasted_iota(jnp.int32, left.shape, 1) < HALF
    own = jnp.where(lane, left, pltpu.roll(right, HALF, 1))
    other = jnp.where(lane, pltpu.roll(left, HALF, 1), right)
    return own, other


def pack_kernel(*refs):
    weights, vectors, biases = refs[:WEIGHTS], refs[WEIGHTS : WEIGHTS + 9], refs[WEIGHTS + 9 : WEIGHTS + 14]
    pack_ref, vec_ref, bias_ref = refs[WEIGHTS + 14 :]
    for number, ref in enumerate(weights):
        pack_ref[number * HALF : number * HALF + HALF, :] = ref[...]
    vec_ref[...] = jnp.zeros(vec_ref.shape, f32)
    bias_ref[...] = jnp.zeros(bias_ref.shape, f32)
    for number, ref in enumerate(vectors):
        vec_ref[number : number + 1, :] = ref[...].astype(f32).reshape(1, D)
    for number, ref in enumerate(biases[:4]):
        at = number % 2 * HALF
        bias_ref[number // 2 : number // 2 + 1, at : at + HALF] = ref[...].astype(f32).reshape(1, HALF)
    for part in range(2):
        bias_ref[2 + part : 3 + part, :] = biases[4][part * D : part * D + D].astype(f32).reshape(1, D)
    pack_ref[WEIGHTS * HALF :, :] = bias_ref[...].astype(bf16)


def bias_rows(near_ref, far_ref):
    near, far = near_ref[...].astype(f32)[:8], far_ref[...].astype(f32)[:8]
    return pack_halves(near, far)[0], pack_halves(near, far)[1], near, far


def weight_copies(near_refs, far_ref, numbers, full_refs, sem):
    copies = []
    for index, (near_ref, number, full_ref) in enumerate(zip(near_refs, numbers, full_refs)):
        copies.append(pltpu.make_async_copy(near_ref, full_ref.at[pl.ds(0, HALF)], sem.at[2 * index]))
        copies.append(
            pltpu.make_async_copy(
                far_ref.at[pl.ds(number * HALF, HALF)], full_ref.at[pl.ds(HALF, HALF)], sem.at[2 * index + 1]
            )
        )
    for copy in copies:
        copy.start()
    return copies


def self_forward_kernel(
    core_ref, lens_ref, hidden_ref, vec_ref, near_ref, far_bias_ref, wq_near, wk_near, wv_near, wo_near, wc_near, far_ref,
    own_ref, n1_ref, q_ref, k_ref, v_ref, ctx_ref, r1_ref, n2_ref, qc_ref, lse_ref,
    w_ref, wo_ref, wc_ref, sem,
):
    core = core_ref[0]
    copies = weight_copies(
        (wq_near, wk_near, wv_near, wo_near, wc_near), far_ref, (0, 1, 2, 6, 3),
        (w_ref.at[pl.ds(0, D)], w_ref.at[pl.ds(D, D)], w_ref.at[pl.ds(2 * D, D)], wo_ref, wc_ref), sem,
    )
    first_bias, second_bias, _, _ = bias_rows(near_ref, far_bias_ref)
    q_bias, v_bias, c_bias = first_bias[0:1], second_bias[0:1], first_bias[1:2]

    def gather(block, carry):
        own_ref[rows_of(block, BLOCK), :] = hidden_ref[
            pl.ds(pl.multiple_of(own_row(block, core), BLOCK), BLOCK), :
        ]
        return carry

    lax.fori_loop(0, BLOCKS, gather, 0)
    for copy in copies:
        copy.wait()

    def project(chunk, carry):
        rows = rows_of(chunk, LINES)
        normed, _ = norm_parts(own_ref[rows, :].astype(f32))
        n1 = (normed * vec_ref[0:1, :] + vec_ref[1:2, :]).astype(bf16)
        n1_ref[rows, :] = n1
        all_three = dot_nt(n1, w_ref[...])
        q_ref[rows, :] = (all_three[:, :D] + q_bias).astype(bf16)
        k_ref[rows, :] = all_three[:, D : 2 * D].astype(bf16)
        v_ref[rows, :] = (all_three[:, 2 * D :] + v_bias).astype(bf16)
        return carry

    lax.fori_loop(0, ROWS // LINES, project, 0)
    low, high, is_low = head_masks()

    def attend(block):
        rows = pl.ds(block * BLOCK, BLOCK)
        first_key, key_count = key_span(block)
        keys = pl.ds(first_key, key_count)
        allowed = self_mask(block, core, lens_ref, key_count)
        cols = [slice(pair * 128, pair * 128 + 128) for pair in range(PAIRS)]
        scores = [dot_nt(stacked(q_ref[rows, c] * scale, low, high), k_ref[keys, c]) for c in cols]
        scores = [jnp.where(allowed, values, masked) for values in scores]
        tops = [jnp.max(values, -1, keepdims=True) for values in scores]
        expo = [jnp.exp(values - top) for values, top in zip(scores, tops)]
        totals = [jnp.sum(values, -1, keepdims=True) for values in expo]
        parts = [dot(values.astype(bf16), v_ref[keys, c]) for values, c in zip(expo, cols)]
        for pair in range(PAIRS):
            ctx_ref[rows, cols[pair]] = joined(parts[pair] * (1.0 / totals[pair]), is_low).astype(bf16)
            lse_ref[pl.ds(block * 2 * BLOCK, 2 * BLOCK), pair : pair + 1] = tops[pair] + jnp.log(totals[pair])

    for block in range(BLOCKS):
        attend(block)

    def finish(chunk, carry):
        rows = rows_of(chunk, LINES)
        r1 = own_ref[rows, :].astype(f32) + dot(ctx_ref[rows, :], wo_ref[...]) + vec_ref[2:3, :]
        r1_ref[rows, :] = r1
        normed, _ = norm_parts(r1)
        n2 = (normed * vec_ref[3:4, :] + vec_ref[4:5, :]).astype(bf16)
        n2_ref[rows, :] = n2
        qc_ref[rows, :] = (dot_nt(n2, wc_ref[...]) + c_bias).astype(bf16)
        return carry

    lax.fori_loop(0, ROWS // LINES, finish, 0)


def step_count(core):
    return jnp.where(core == 0, HEAD_SHORTS + 1, STEPS)


def step_seq(step, core):
    step = jnp.minimum(step, step_count(core) - 1)
    return jnp.where(core == 0, jnp.where(step < HEAD_SHORTS, step, SEQ_TOTAL - 1), HEAD_SHORTS + step)


def step_blocks(step, core):
    count = jnp.where(step < HEAD_SHORTS, 1, jnp.where(core == 0, REGION_BLOCKS, jnp.where(step < 5, 1, 2)))
    first = jnp.where(step < 6, step, 7)
    return first, count


def cross_forward_kernel(
    frame_total, core_ref, frames_ref, qc_ref, near_ref, far_bias_ref, wk_near, wv_near, far_ref,
    k_ref, v_ref, ctx_ref, lse_ref, w_ref, score_ref, sem,
):
    step = pl.program_id(0)
    core = core_ref[0]
    padded = k_ref.shape[1]
    tail = padded - 128
    low, high, is_low = head_masks()

    @pl.when(step == 0)
    def _():
        copies = weight_copies(
            (wk_near, wv_near), far_ref, (4, 5), (w_ref.at[pl.ds(0, D)], w_ref.at[pl.ds(D, D)]), sem
        )
        ctx_ref[ROWS - BLOCK :, :] = jnp.zeros((BLOCK, D), bf16)
        for copy in copies:
            copy.wait()

    @pl.when(step < step_count(core))
    def _():
        k_ref[0, padded - 64 :, :] = jnp.zeros((64, D), bf16)
        v_ref[0, padded - 64 :, :] = jnp.zeros((64, D), bf16)
        bias = bias_rows(near_ref, far_bias_ref)[1][1:2]
        for top in range(0, frame_total, 512):
            end = min(top + 512, frame_total)
            part = frames_ref[0, top:end, :]
            both = dot_nt(part, w_ref[...])
            k_ref[0, top:end, :] = both[:, :D].astype(bf16)
            v_ref[0, top:end, :] = (both[:, D:] + bias).astype(bf16)
        first, count = step_blocks(step, core)

        def attend(turn, carry):
            block = first + turn
            rows = rows_of(block, BLOCK)
            inside = lax.broadcasted_iota(jnp.int32, (2 * BLOCK, 128), 1) < frame_total - tail

            def score(pair):
                cols = slice(pair * 128, pair * 128 + 128)
                query = stacked(qc_ref[rows, cols] * scale, low, high)
                tops = jnp.full((2 * BLOCK, 128), masked, f32)
                for at in range(0, padded, CHUNK):
                    values = dot_nt(query, k_ref[0, at : at + CHUNK, cols])
                    if at + CHUNK == padded:
                        values = jnp.concatenate(
                            [values[:, : CHUNK - 128], jnp.where(inside, values[:, CHUNK - 128 :], masked)], 1
                        )
                    score_ref[pair % 2, :, at : at + CHUNK] = values
                    for lane in range(0, CHUNK, 128):
                        tops = jnp.maximum(tops, values[:, lane : lane + 128])
                return jnp.max(tops, -1, keepdims=True)

            def weigh(pair, top):
                cols = slice(pair * 128, pair * 128 + 128)
                totals = jnp.zeros((2 * BLOCK, 128), f32)
                product = jnp.zeros((2 * BLOCK, 128), f32)
                for at in range(0, padded, CHUNK):
                    expo = jnp.exp(score_ref[pair % 2, :, at : at + CHUNK] - top)
                    for lane in range(0, CHUNK, 128):
                        totals = totals + expo[:, lane : lane + 128]
                    product = product + dot(expo.astype(bf16), v_ref[0, at : at + CHUNK, cols])
                total = jnp.sum(totals, -1, keepdims=True)
                ctx_ref[rows, cols] = joined(product * (1.0 / total), is_low).astype(bf16)
                lse_ref[rows_of(block, 2 * BLOCK), pair : pair + 1] = top + jnp.log(total)

            top = score(0)
            for pair in range(PAIRS):
                following = score(pair + 1) if pair + 1 < PAIRS else None
                weigh(pair, top)
                top = following
            return carry

        lax.fori_loop(0, count, attend, 0)


def feed_kernel(
    core_ref, lens_ref, cot_ref, r1_ref, ctx_ref, vec_ref, near_ref, far_bias_ref,
    wo_near, far_ref, w1_near, w1_far, w2_near, w2_far,
    out_ref, g2_ref, dctx_ref, keep_ref, send_ref, small_ref,
    top_ref, n3_ref, act_ref, pre_ref, low_ref, wo_ref, w1_ref, w2_ref, sem,
):
    core = core_ref[0]
    half = w2_near.shape[0]
    copies = weight_copies((wo_near,), far_ref, (7,), (wo_ref,), sem)
    copies.append(pltpu.make_async_copy(w1_near, w1_ref.at[:, pl.ds(0, half)], sem.at[2]))
    copies.append(pltpu.make_async_copy(w1_far, w1_ref.at[:, pl.ds(half, half)], sem.at[3]))
    copies.append(pltpu.make_async_copy(w2_near, w2_ref.at[pl.ds(0, half)], sem.at[4]))
    copies.append(pltpu.make_async_copy(w2_far, w2_ref.at[pl.ds(half, half)], sem.at[5]))
    for copy in copies[2:]:
        copy.start()
    _, _, near, far = bias_rows(near_ref, far_bias_ref)
    b1 = jnp.concatenate([near[2:3], near[3:4], far[2:3], far[3:4]], 1)

    def block_rows(block, carry):
        rows = rows_of(block, BLOCK)
        start, length, padding = block_segment(block, core, lens_ref)
        place = jnp.where(block < HEAD_SHORTS, 0, (block - HEAD_SHORTS) * BLOCK) - start
        length = jnp.where(padding, 0, length)
        row = lax.broadcasted_iota(jnp.int32, (BLOCK, D), 0) + place
        cot = cot_ref[pl.ds(pl.multiple_of(own_row(block, core), BLOCK), BLOCK), :].astype(f32)
        top_ref[rows, :] = jnp.where(row < length, cot, 0.0).astype(bf16)
        return carry

    lax.fori_loop(0, BLOCKS, block_rows, 0)
    small_ref[...] = jnp.zeros(small_ref.shape, f32)
    for copy in copies:
        copy.wait()

    def chunk_rows(chunk, sums):
        rows = rows_of(chunk, LINES)
        r2 = r1_ref[rows, :] + dot(ctx_ref[rows, :], wo_ref[...]) + vec_ref[5:6, :]
        normed, inverse = norm_parts(r2)
        gain = vec_ref[6:7, :]
        n3 = (normed * gain + vec_ref[7:8, :]).astype(bf16)
        n3_ref[rows, :] = n3
        pre = dot(n3, w1_ref[...]) + b1
        phi = 0.5 * (1.0 + lax.erf(pre * (0.5**0.5)))
        act = (pre * phi).astype(bf16)
        act_ref[rows, :] = act
        out_ref[rows, :] = (r2 + dot(act, w2_ref[...]) + vec_ref[8:9, :]).astype(bf16)
        top = top_ref[rows, :]
        slope = phi + pre * (jnp.exp(-0.5 * pre * pre) * 0.3989422804014327)
        grad_pre = (dot_nt(top, w2_ref[...]) * slope).astype(bf16)
        pre_ref[rows, :] = grad_pre
        grad_n3 = dot_nt(grad_pre, w1_ref[...])
        top32 = top.astype(f32)
        g2 = top32 + norm_back(normed, inverse, gain, grad_n3)
        g2_ref[rows, :] = g2
        low = g2.astype(bf16)
        low_ref[rows, :] = low
        dctx_ref[rows, :] = dot_nt(low, wo_ref[...]).astype(bf16)
        small_ref[0:1, :] += column_sum(top32)
        small_ref[1:2, :] += column_sum(grad_n3 * normed)
        small_ref[2:3, :] += column_sum(grad_n3)
        small_ref[3:4, :] += column_sum(g2)
        bias = column_sum(grad_pre.astype(f32))
        for part in range(4):
            small_ref[4 + part : 5 + part, :] += bias[:, part * D : part * D + D]
        return sums

    lax.fori_loop(0, ROWS // LINES, chunk_rows, 0)

    def mask_rows(block, carry):
        rows = rows_of(block, BLOCK)
        start, length, _ = block_segment(block, core, lens_ref)
        place = jnp.where(block < HEAD_SHORTS, 0, (block - HEAD_SHORTS) * BLOCK) - start
        row = lax.broadcasted_iota(jnp.int32, (BLOCK, D), 0) + place
        out_ref[rows, :] = jnp.where(row < length, out_ref[rows, :].astype(f32), 0.0).astype(bf16)
        return carry

    lax.fori_loop(0, BLOCKS, mask_rows, 0)
    for part in range(4):
        cols = slice(part * D, part * D + D)
        target, at = (keep_ref, part) if part < 2 else (send_ref, part - 2)
        target[at * D : at * D + D, :] = dot_tn(n3_ref[...], pre_ref[:, cols]).astype(target.dtype)
        grad = dot_tn(act_ref[:, cols], top_ref[...])
        target[half + at * D : half + at * D + D, :] = grad.astype(target.dtype)
    grad = dot_tn(ctx_ref[...], low_ref[...])
    keep_ref[2 * half : 2 * half + HALF, :] = grad[:HALF]
    send_ref[2 * half : 2 * half + HALF, :] = grad[HALF:].astype(bf16)
    extra = keep_ref.shape[0] - (2 * half + HALF)
    if extra:
        keep_ref[2 * half + HALF :, :] = jnp.zeros((extra, D), f32)
        send_ref[2 * half + HALF :, :] = jnp.zeros((extra, D), bf16)


def cross_backward_kernel(
    frame_total, first_step, core_ref, frames_ref, k_ref, v_ref, qc_ref, ctx_ref, dctx_ref, lse_ref, *refs
):
    if first_step:
        dq_in_ref, grad_in_ref, bias_in_ref = refs[:3]
    dq_ref, grad_ref, bias_ref, dk_ref, dv_ref = refs[-5:]
    step = pl.program_id(0) + first_step
    core = core_ref[0]
    padded = k_ref.shape[1]
    low, high, is_low = head_masks()

    @pl.when(step == first_step)
    def _():
        if first_step:
            dq_ref[...] = dq_in_ref[...]
            dq_ref[ROWS - BLOCK :, :] = jnp.zeros((BLOCK, D), bf16)
            grad_ref[...] = grad_in_ref[...]
            bias_ref[...] = bias_in_ref[...]
        else:
            grad_ref[...] = jnp.zeros(grad_ref.shape, f32)
            bias_ref[...] = jnp.zeros(bias_ref.shape, f32)

    @pl.when(step < step_count(core))
    def _():
        first, count = step_blocks(step, core)

        def attend(turn, carry):
            block = first + turn
            rows = rows_of(block, BLOCK)
            carried = turn > 0
            setups = []
            for pair in range(PAIRS):
                cols = slice(pair * 128, pair * 128 + 128)
                query = stacked(qc_ref[rows, cols] * scale, low, high)
                grad_out = stacked(dctx_ref[rows, cols], low, high)
                ctx = ctx_ref[rows, cols].astype(f32)
                spread = jnp.sum(grad_out.astype(f32) * jnp.concatenate([ctx, ctx], 0), -1, keepdims=True)
                lse = lse_ref[rows_of(block, 2 * BLOCK), pair : pair + 1]
                setups.append((cols, query, grad_out, query.T, grad_out.T, spread, lse))

            def begin(pair, at):
                cols, query, grad_out = setups[pair][:3]
                keys = slice(at, at + CHUNK)
                return dot_nt(query, k_ref[0, keys, cols]), dot_nt(grad_out, v_ref[0, keys, cols])

            def end(pair, at, scores, grad_weights):
                cols, _, _, query_t, grad_out_t, spread, lse = setups[pair]
                keys = slice(at, at + CHUNK)
                weights = jnp.exp(scores - lse)
                grad_scores = (weights * (grad_weights - spread)).astype(bf16)
                old_key = jnp.where(carried, dk_ref[cols, keys], 0.0)
                old_value = jnp.where(carried, dv_ref[cols, keys], 0.0)
                dk_ref[cols, keys] = old_key + dot(query_t, grad_scores)
                dv_ref[cols, keys] = old_value + dot(grad_out_t, weights.astype(bf16))
                return dot(grad_scores, k_ref[0, keys, cols])

            order = [(pair, at) for pair in range(PAIRS) for at in range(0, padded, CHUNK)]
            ahead = begin(*order[0])
            grad_query = None
            for index, (pair, at) in enumerate(order):
                now = ahead
                if index + 1 < len(order):
                    ahead = begin(*order[index + 1])
                part = end(pair, at, *now)
                grad_query = part if at == 0 else grad_query + part
                if at + CHUNK == padded:
                    dq_ref[rows, setups[pair][0]] = (joined(grad_query, is_low) * scale).astype(bf16)
            return carry

        lax.fori_loop(0, count, attend, 0)
        frames = frames_ref[0]
        grad_ref[:D, :] += dot(dk_ref[:, :frame_total].astype(bf16), frames)
        grad_value = dv_ref[:, :frame_total].astype(bf16)
        grad_ref[D:, :] += dot(grad_value, frames)
        bias_ref[:, 0:1] += jnp.sum(grad_value.astype(f32), -1, keepdims=True)


def self_attention_back_kernel(
    core_ref, lens_ref, vec_ref, wo_near, wc_near, far_ref, q_ref, k_ref, v_ref, ctx_ref, r1_ref, lse_ref,
    dqc_ref, g2_ref, after_ref,
    g1_ref, low_ref, dq_ref, dk_ref, dv_ref, small_ref,
    dctx_ref, dk_acc, dv_acc, wo_ref, wc_ref, sem,
):
    core = core_ref[0]
    copies = weight_copies((wo_near, wc_near), far_ref, (6, 3), (wo_ref, wc_ref), sem)
    small_ref[...] = jnp.zeros(small_ref.shape, f32)
    dk_acc[...] = jnp.zeros(dk_acc.shape, f32)
    dv_acc[...] = jnp.zeros(dv_acc.shape, f32)
    for copy in copies:
        copy.wait()

    def enter(chunk, carry):
        rows = rows_of(chunk, LINES)
        dqc = dqc_ref[rows, :]
        grad_n2 = dot(dqc, wc_ref[...])
        normed, inverse = norm_parts(r1_ref[rows, :])
        g1 = g2_ref[rows, :] + norm_back(normed, inverse, vec_ref[3:4, :], grad_n2)
        g1_ref[rows, :] = g1
        low = g1.astype(bf16)
        low_ref[rows, :] = low
        dctx_ref[rows, :] = dot_nt(low, wo_ref[...]).astype(bf16)
        small_ref[0:1, :] += column_sum(dqc.astype(f32))
        small_ref[1:2, :] += column_sum(grad_n2 * normed)
        small_ref[2:3, :] += column_sum(grad_n2)
        small_ref[3:4, :] += column_sum(g1)
        return carry

    lax.fori_loop(0, ROWS // LINES, enter, 0)
    low, high, is_low = head_masks()

    def attend(block):
        rows = pl.ds(block * BLOCK, BLOCK)
        first_key, key_count = key_span(block)
        keys = pl.ds(first_key, key_count)
        allowed = self_mask(block, core, lens_ref, key_count)
        cols = [slice(pair * 128, pair * 128 + 128) for pair in range(PAIRS)]
        queries = [stacked(q_ref[rows, c] * scale, low, high) for c in cols]
        grad_outs = [stacked(dctx_ref[rows, c], low, high) for c in cols]
        ctxs = [ctx_ref[rows, c].astype(f32) for c in cols]
        spreads = [
            jnp.sum(grad_out.astype(f32) * jnp.concatenate([ctx, ctx], 0), -1, keepdims=True)
            for grad_out, ctx in zip(grad_outs, ctxs)
        ]
        scores = [dot_nt(query, k_ref[keys, c]) for query, c in zip(queries, cols)]
        grad_weights = [dot_nt(grad_out, v_ref[keys, c]) for grad_out, c in zip(grad_outs, cols)]
        for pair, c in enumerate(cols):
            lse = lse_ref[pl.ds(block * 2 * BLOCK, 2 * BLOCK), pair : pair + 1]
            weights = jnp.exp(jnp.where(allowed, scores[pair] - lse, masked))
            grad_scores = (weights * (grad_weights[pair] - spreads[pair])).astype(bf16)
            dq_ref[rows, c] = (joined(dot(grad_scores, k_ref[keys, c]), is_low) * scale).astype(bf16)
            if block < HEAD_SHORTS:
                dk_ref[rows, c] = dot_tn(grad_scores, queries[pair]).astype(bf16)
                dv_ref[rows, c] = dot_tn(weights.astype(bf16), grad_outs[pair]).astype(bf16)
            else:
                dk_acc[c, :key_count] += dot(queries[pair].T, grad_scores)
                dv_acc[c, :key_count] += dot(grad_outs[pair].T, weights.astype(bf16))

    for block in range(BLOCKS):
        attend(block)
    dk_ref[FIRST_ROWS:, :] = dk_acc[...].T.astype(bf16)
    dv_ref[FIRST_ROWS:, :] = dv_acc[...].T.astype(bf16)


def self_weights_kernel(
    n1_ref, n2_ref, ctx_ref, low_ref, dq_ref, dk_ref, dv_ref, dqc_ref, cross_ref, after_ref, keep_ref, send_ref
):
    def place(number, grad):
        rows = slice(number * HALF, number * HALF + HALF)
        keep_ref[rows, :] = grad[:HALF]
        send_ref[rows, :] = grad[HALF:].astype(bf16)

    place(0, cross_ref[:D, :])
    place(1, cross_ref[D:, :])
    place(2, dot_tn(dq_ref[...], n1_ref[...]))
    place(3, dot_tn(dk_ref[...], n1_ref[...]))
    place(4, dot_tn(dv_ref[...], n1_ref[...]))
    place(5, dot_tn(dqc_ref[...], n2_ref[...]))
    place(6, dot_tn(ctx_ref[...], low_ref[...]))
    base = 7 * HALF
    rest = keep_ref.shape[0] - base
    if rest:
        keep_ref[base:, :] = jnp.zeros((rest, D), f32)
        send_ref[base:, :] = jnp.zeros((rest, D), bf16)


def self_finish_kernel(
    own_ref, vec_ref, wq_near, wk_near, wv_near, far_ref,
    g1_ref, dq_ref, dk_ref, dv_ref, back_small_ref, feed_small_ref, cross_bias_ref, after_ref,
    dh_ref, out_small_ref,
    small_ref, wq_ref, wk_ref, wv_ref, sem,
):
    copies = weight_copies((wq_near, wk_near, wv_near), far_ref, (0, 1, 2), (wq_ref, wk_ref, wv_ref), sem)
    small_ref[...] = jnp.zeros(small_ref.shape, f32)
    for copy in copies:
        copy.wait()

    def leave(chunk, carry):
        rows = rows_of(chunk, LINES)
        dq, dk, dv = dq_ref[rows, :], dk_ref[rows, :], dv_ref[rows, :]
        grad_n1 = dot(dq, wq_ref[...]) + dot(dk, wk_ref[...]) + dot(dv, wv_ref[...])
        normed, inverse = norm_parts(own_ref[rows, :].astype(f32))
        g1 = g1_ref[rows, :] + norm_back(normed, inverse, vec_ref[0:1, :], grad_n1)
        dh_ref[rows, :] = g1.astype(bf16)
        small_ref[4:5, :] += column_sum(dq.astype(f32))
        small_ref[5:6, :] += column_sum(dv.astype(f32))
        small_ref[6:7, :] += column_sum(grad_n1 * normed)
        small_ref[7:8, :] += column_sum(grad_n1)
        return carry

    lax.fori_loop(0, ROWS // LINES, leave, 0)
    cross_bias = cross_bias_ref[...].T[0:8, :]
    left = jnp.concatenate([small_ref[4:5, :], back_small_ref[0:1, :], jnp.zeros((6, D), f32)], 0)
    right = jnp.concatenate([small_ref[5:6, :], cross_bias[0:1, :], jnp.zeros((6, D), f32)], 0)
    own, other = pack_halves(left, right)
    out_small_ref[...] = jnp.concatenate(
        [
            own[0:2], feed_small_ref[4:6, :],
            small_ref[6:7, :], small_ref[7:8, :], back_small_ref[3:4, :], back_small_ref[1:2, :], back_small_ref[2:3, :],
            feed_small_ref[3:4, :], feed_small_ref[1:2, :], feed_small_ref[2:3, :], feed_small_ref[0:1, :],
            jnp.zeros((3, D), f32),
            other[0:2], feed_small_ref[6:8, :],
            jnp.zeros((4, D), f32),
        ],
        0,
    )


vmem = pl.BlockSpec(memory_space=pltpu.VMEM)
smem = pl.BlockSpec(memory_space=pltpu.SMEM)
anywhere = pl.BlockSpec(memory_space=pl.ANY)


def shaped(shape, dtype):
    return jax.ShapeDtypeStruct(shape, dtype)


def constant(shape):
    return pl.BlockSpec(shape, lambda step, core: (0,) * len(shape))


def call(kernel, scalars, operands, outs, scratch=(), flops=0, nbytes=0, far=()):
    return pl.pallas_call(
        kernel,
        out_shape=outs,
        in_specs=[smem] * len(scalars) + [anywhere if place in far else vmem for place in range(len(operands))],
        out_specs=[vmem] * len(outs),
        scratch_shapes=list(scratch),
        cost_estimate=pl.CostEstimate(flops=flops, bytes_accessed=nbytes, transcendentals=0),
    )(*scalars, *operands)


def stage_list(count):
    stages = []
    stride = 1
    while stride < count:
        radix = 4 if count // stride % 4 == 0 else 2
        stages.append((stride, radix))
        stride = stride * radix
    return stages


def partner(count, stride, radix, turn):
    pairs = []
    for index in range(count):
        digit = index // stride % radix
        pairs.append((index, index + ((digit ^ turn) - digit) * stride))
    return pairs


def arrived_sum(total, arrived, rows):
    for ref in arrived:
        total = total + ref[rows, :].astype(f32)
    return total


def spread_kernel(received, unread, has_small, joined_small, digit_ref, keep_in_ref, *refs):
    if has_small:
        small_in_ref, refs = refs[0], refs[1:]
    arrived = refs[:received]
    outs = refs[received + unread :]
    if has_small:
        small_ref, outs = outs[0], outs[1:]
    digit = digit_ref[0]
    part = outs[0].shape[0]
    if has_small:
        small = small_in_ref[...]
        if joined_small:
            small = arrived_sum(small, arrived, pl.ds(keep_in_ref.shape[0], SMALL))
        small_ref[...] = small
    for turn, out_ref in enumerate(outs):
        rows = pl.ds(pl.multiple_of((digit ^ turn) * part, part), part)
        total = arrived_sum(keep_in_ref[rows, :], arrived, rows)
        out_ref[:part, :] = total.astype(out_ref.dtype)
        if has_small and turn:
            out_ref[part:, :] = small.astype(bf16)


def last_kernel(received, has_small, keep_in_ref, *refs):
    if has_small:
        small_in_ref, refs = refs[0], refs[1:]
    arrived, outs = refs[:received], refs[received:]
    outs[0][...] = arrived_sum(keep_in_ref[...], arrived, pl.ds(0, keep_in_ref.shape[0])).astype(bf16)
    if has_small:
        small = arrived_sum(small_in_ref[...], arrived, pl.ds(keep_in_ref.shape[0], SMALL))
        outs[1][...] = small
        outs[2][...] = small.astype(bf16)


def gather_kernel(digit_ref, *refs):
    out_ref = refs[-1]
    digit = digit_ref[0]
    part = refs[0].shape[0]
    for turn, ref in enumerate(refs[:-1]):
        out_ref[pl.ds(pl.multiple_of((digit ^ turn) * part, part), part), :] = ref[...]


class RowSum:
    def __init__(self, keep, send, swap):
        self.count = lax.axis_size("dp")
        self.index = lax.axis_index("dp")
        self.stages = stage_list(self.count)
        self.small = None
        self.after = None
        self.swap = swap
        self.current = keep
        self.arrived = [lax.ppermute(send, "tp", swap)]
        self.digits = [(self.index // stride % radix).reshape(1) for stride, radix in self.stages]

    def permute(self, value, number, turn):
        stride, radix = self.stages[number]
        return lax.ppermute(value, "dp", partner(self.count, stride, radix, turn))

    def spread(self, number):
        _, radix = self.stages[number]
        rows = self.current.shape[0] // radix
        small = [] if self.small is None else [self.small]
        extra = SMALL if small else 0
        after = [] if self.after is None or number else [self.after]
        operands = [self.current] + small + self.arrived
        pieces = call(
            partial(spread_kernel, len(self.arrived), len(after), bool(small), number > 0),
            [self.digits[number]], operands + after,
            [shaped(value.shape, f32) for value in small]
            + [shaped((rows, D), f32)] + [shaped((rows + extra, D), bf16)] * (radix - 1),
            nbytes=self.current.size * 8, far=range(len(operands), len(operands) + len(after)),
        )
        if small:
            self.small, pieces = pieces[0], pieces[1:]
        self.current = pieces[0]
        self.arrived = [self.permute(piece, number, turn + 1) for turn, piece in enumerate(pieces[1:])]
        return pieces[0]

    def last(self):
        small = [] if self.small is None else [self.small]
        total = call(
            partial(last_kernel, len(self.arrived), bool(small)), [],
            [self.current] + small + self.arrived,
            [shaped(self.current.shape, bf16)] + [shaped((SMALL, D), f32), shaped((SMALL, D), bf16)] * len(small),
            nbytes=self.current.size * 8,
        )
        if small:
            self.small = total[1]
            self.small_far = lax.ppermute(total[2], "tp", self.swap)
        return self.widen(total[0], len(self.stages) - 1)

    def widen(self, total, number):
        self.pieces = [total] + [self.permute(total, number, turn) for turn in range(1, self.stages[number][1])]
        return total

    def gather(self, number):
        total = self.pieces[0]
        total = call(
            gather_kernel, [self.digits[number]], self.pieces,
            [shaped((total.shape[0] * self.stages[number][1], D), bf16)], nbytes=total.size * 16,
        )[0]
        return self.widen(total, number - 1)

    def steps(self):
        numbers = range(len(self.stages))
        return (
            [partial(self.spread, number) for number in numbers]
            + [self.last]
            + [partial(self.gather, number) for number in reversed(numbers) if number]
        )


def assemble(digit, pieces, full_ref):
    part = pieces[0].shape[0]
    for turn, ref in enumerate(pieces):
        full_ref[pl.ds(pl.multiple_of((digit ^ turn) * part, part), part), :] = ref[...]


def feed_finish_kernel(count, digit_ref, *refs):
    w1_ref, w2_ref, wo_ref, full_ref = refs[count:]
    assemble(digit_ref[0], refs[:count], full_ref)
    half = w2_ref.shape[0]
    for part in range(half // D):
        w1_ref[:, part * D : part * D + D] = full_ref[part * D : part * D + D, :].astype(f32)
    w2_ref[...] = full_ref[half : 2 * half, :].astype(f32)
    wo_ref[...] = full_ref[2 * half : 2 * half + HALF, :].astype(f32)


def attention_finish_kernel(count, digit_ref, small_ref, far_ref, *refs):
    outs, full_ref = refs[count:-1], refs[-1]
    assemble(digit_ref[0], refs[:count], full_ref)
    for number, ref in enumerate(outs[:7]):
        ref[...] = full_ref[number * HALF : number * HALF + HALF, :].astype(f32)
    mine, far = small_ref[...], far_ref[...].astype(f32)
    half_rows = mine[0:4] + far[16:20]
    both = mine + far
    for number, ref in enumerate(outs[7:11]):
        at = number % 2 * HALF
        ref[...] = half_rows[number // 2 : number // 2 + 1, at : at + HALF].reshape(HALF)
    for part in range(2):
        outs[11][part * D : part * D + D] = half_rows[2 + part : 3 + part, :].reshape(D)
    for number, ref in enumerate(outs[12:]):
        ref[...] = both[4 + number : 5 + number, :].reshape(D)


def local(
    hidden, frames, lengths, cotangent,
    ln1_gain, ln1_bias, sq_weight, sq_bias, sk_weight, sv_weight, sv_bias, so_weight, so_bias,
    ln2_gain, ln2_bias, cq_weight, cq_bias, ck_weight, cv_weight, cv_bias, co_weight, co_bias,
    ln3_gain, ln3_bias, fc1_weight, fc1_bias, fc2_weight, fc2_bias,
):
    tp_index = lax.axis_index("tp")
    core = tp_index.astype(jnp.int32).reshape(1)
    swap = [(0, 1), (1, 0)]
    half = fc1_weight.shape[1]
    wide = 2 * half
    frame_total = frames.shape[1]
    padded = round_up(frame_total, CHUNK)

    near = [w.T for w in (sq_weight, sk_weight, sv_weight, cq_weight, ck_weight, cv_weight)] + [so_weight, co_weight]
    vectors = [ln1_gain, ln1_bias, so_bias, ln2_gain, ln2_bias, co_bias, ln3_gain, ln3_bias, fc2_bias]
    pack, vec, near_bias = call(
        pack_kernel, [], near + vectors + [sq_bias, sv_bias, cq_bias, cv_bias, fc1_bias],
        [shaped((WEIGHTS * HALF + 16, D), bf16), shaped((16, D), f32), shaped((16, D), f32)],
        nbytes=4 << 20,
    )
    far = lax.ppermute(pack, "tp", swap)
    fc1_far = lax.ppermute(fc1_weight, "tp", swap)
    fc2_far = lax.ppermute(fc2_weight, "tp", swap)
    far_bias = far[WEIGHTS * HALF :]

    row_low = shaped((ROWS, D), bf16)
    row_wide = shaped((ROWS, D), f32)
    lse_shape = shaped((2 * ROWS, 128), f32)
    square = pltpu.VMEM((D, D), bf16)
    own, n1, q, k, v, ctx, r1, n2, qc, lse = call(
        self_forward_kernel, [core, lengths],
        [hidden, vec, near_bias, far_bias, near[0], near[1], near[2], near[6], near[3], far],
        [row_low] * 6 + [row_wide, row_low, row_low, lse_shape],
        scratch=[pltpu.VMEM((3 * D, D), bf16), square, square, pltpu.SemaphoreType.DMA((10,))],
        flops=2 * ROWS * D * D * 5, nbytes=8 << 20, far=range(4, 10),
    )

    def cross_specs(first):
        frame_spec = pl.BlockSpec((1, frame_total, D), lambda step, core: (step_seq(step + first, core[0]), 0, 0))
        stored_spec = pl.BlockSpec(
            (1, padded, D), lambda step, core: (jnp.minimum(step + first, step_count(core[0]) - 1), 0, 0)
        )
        return frame_spec, stored_spec

    frame_spec, stored_spec = cross_specs(0)
    key_shape = shaped((STEPS, padded, D), bf16)
    ck, cv, ctx_cross, lse_cross = pl.pallas_call(
        partial(cross_forward_kernel, frame_total),
        out_shape=[key_shape, key_shape, row_low, lse_shape],
        grid_spec=pltpu.PrefetchScalarGridSpec(
            num_scalar_prefetch=1,
            grid=(STEPS,),
            in_specs=[frame_spec, constant((ROWS, D)), constant((16, D)), constant((16, D))] + [anywhere] * 3,
            out_specs=[stored_spec, stored_spec, constant((ROWS, D)), constant((2 * ROWS, 128))],
            scratch_shapes=[pltpu.VMEM((2 * D, D), bf16), pltpu.VMEM((2, 2 * BLOCK, padded), f32), pltpu.SemaphoreType.DMA((4,))],
        ),
        cost_estimate=pl.CostEstimate(flops=20 << 30, bytes_accessed=32 << 20, transcendentals=0),
        name="cross_forward",
    )(core, frames, qc, near_bias, far_bias, near[4], near[5], far)

    dp_count = lax.axis_size("dp")
    feed_rows = round_up(2 * half + HALF, 16 * dp_count)
    out_own, g2, dctx, feed_keep, feed_send, feed_small = call(
        feed_kernel, [core, lengths],
        [cotangent, r1, ctx_cross, vec, near_bias, far_bias, near[7], far, fc1_weight, fc1_far, fc2_weight, fc2_far],
        [row_low, row_wide, row_low, shaped((feed_rows, D), f32), shaped((feed_rows, D), bf16), shaped((8, D), f32)],
        scratch=[
            pltpu.VMEM((ROWS, D), bf16), pltpu.VMEM((ROWS, D), bf16), pltpu.VMEM((ROWS, wide), bf16),
            pltpu.VMEM((ROWS, wide), bf16), pltpu.VMEM((ROWS, D), bf16), square,
            pltpu.VMEM((D, wide), bf16), pltpu.VMEM((wide, D), bf16), pltpu.SemaphoreType.DMA((6,)),
        ],
        flops=2 * ROWS * D * wide * 6, nbytes=16 << 20, far=range(6, 12),
    )
    feed_sum = RowSum(feed_keep, feed_send, swap)
    pending = feed_sum.steps()

    def advance():
        return pending.pop(0)() if pending else feed_sum.current

    def cross_backward(first, count, chained):
        frame_spec, stored_spec = cross_specs(first)
        carried = [constant((ROWS, D)), constant((2 * D, D)), constant((D, 128))]
        return pl.pallas_call(
            partial(cross_backward_kernel, frame_total, first),
            out_shape=[row_low, shaped((2 * D, D), f32), shaped((D, 128), f32)],
            grid_spec=pltpu.PrefetchScalarGridSpec(
                num_scalar_prefetch=1,
                grid=(count,),
                in_specs=[frame_spec, stored_spec, stored_spec] + [constant((ROWS, D))] * 3
                + [constant((2 * ROWS, 128))] + (carried + [anywhere] if chained else []),
                out_specs=carried,
                scratch_shapes=[pltpu.VMEM((D, padded), f32), pltpu.VMEM((D, padded), f32)],
            ),
            cost_estimate=pl.CostEstimate(flops=20 << 30, bytes_accessed=16 << 20, transcendentals=0),
        )(core, frames, ck, cv, qc, ctx_cross, dctx, lse_cross, *chained)

    chained = cross_backward(0, 1, [])
    chained = cross_backward(1, HEAD_SHORTS - 1, [*chained, advance()])
    dqc, cross_grad, cross_bias = cross_backward(HEAD_SHORTS, STEPS - HEAD_SHORTS, [*chained, advance()])
    after = advance()
    half_acc = pltpu.VMEM((D, LONG_LEN), f32)
    g1, low, dq, dk, dv, back_small = call(
        self_attention_back_kernel, [core, lengths],
        [vec, near[6], near[3], far, q, k, v, ctx, r1, lse, dqc, g2, after],
        [row_wide, row_low, row_low, row_low, row_low, shaped((8, D), f32)],
        scratch=[pltpu.VMEM((ROWS, D), bf16), half_acc, half_acc, square, square, pltpu.SemaphoreType.DMA((4,))],
        flops=2 * ROWS * D * D * 10, nbytes=8 << 20, far=(1, 2, 3, 12),
    )
    after = advance()
    attention_rows = round_up(7 * HALF, 8 * dp_count)
    keep, send = call(
        self_weights_kernel, [],
        [n1, n2, ctx, low, dq, dk, dv, dqc, cross_grad, after],
        [shaped((attention_rows, D), f32), shaped((attention_rows, D), bf16)],
        flops=2 * ROWS * D * D * 5, nbytes=8 << 20, far=(9,),
    )
    attention_sum = RowSum(keep, send, swap)
    dh_own, attention_sum.small = call(
        self_finish_kernel, [],
        [own, vec, near[0], near[1], near[2], far, g1, dq, dk, dv, back_small, feed_small, cross_bias, send],
        [row_low, shaped((SMALL, D), f32)],
        scratch=[pltpu.VMEM((8, D), f32), square, square, square, pltpu.SemaphoreType.DMA((6,))],
        flops=2 * ROWS * D * D * 5, nbytes=4 << 20, far=(2, 3, 4, 5, 13),
    )
    while pending:
        advance()
    grad_fc1, grad_fc2, grad_co = call(
        partial(feed_finish_kernel, len(feed_sum.pieces)), [feed_sum.digits[0]], feed_sum.pieces,
        [shaped((D, half), f32), shaped((half, D), f32), shaped((HALF, D), f32)],
        scratch=[pltpu.VMEM((feed_rows, D), bf16)], nbytes=8 << 20,
    )
    attention_sum.after = grad_co
    out_far = lax.ppermute(out_own, "tp", swap)
    dh_far = lax.ppermute(dh_own, "tp", swap)
    for step in attention_sum.steps():
        step()
    pieces = attention_sum.pieces

    (
        grad_ck, grad_cv, grad_sq, grad_sk, grad_sv, grad_cq, grad_so,
        grad_sq_bias, grad_sv_bias, grad_cq_bias, grad_cv_bias, grad_fc1_bias,
        grad_ln1_gain, grad_ln1_bias, grad_so_bias, grad_ln2_gain, grad_ln2_bias,
        grad_co_bias, grad_ln3_gain, grad_ln3_bias, grad_fc2_bias,
    ) = call(
        partial(attention_finish_kernel, len(pieces)), [attention_sum.digits[0]],
        [attention_sum.small, attention_sum.small_far] + pieces,
        [shaped((HALF, D), f32)] * 7 + [shaped((HALF,), f32)] * 4 + [shaped((half,), f32)] + [shaped((D,), f32)] * 9,
        scratch=[pltpu.VMEM((attention_rows, D), bf16)], nbytes=8 << 20,
    )

    def group_rows(mine, far):
        first = jnp.where(tp_index == 0, mine, far)
        second = jnp.where(tp_index == 0, far, mine)
        return jnp.concatenate(
            [
                first[:FIRST_ROWS], second[:FIRST_ROWS],
                second[FIRST_ROWS : FIRST_ROWS + 2 * BLOCK + 2 * MID_LEN], first[FIRST_ROWS:],
            ],
            0,
        )

    return (
        group_rows(out_own, out_far),
        group_rows(dh_own, dh_far),
        grad_ln1_gain,
        grad_ln1_bias,
        grad_sq.T,
        grad_sq_bias,
        grad_sk.T,
        grad_sv.T,
        grad_sv_bias,
        grad_so,
        grad_so_bias,
        grad_ln2_gain,
        grad_ln2_bias,
        grad_cq.T,
        grad_cq_bias,
        grad_ck.T,
        grad_cv.T,
        grad_cv_bias,
        grad_co,
        grad_co_bias,
        grad_ln3_gain,
        grad_ln3_bias,
        grad_fc1,
        grad_fc1_bias,
        grad_fc2,
        grad_fc2_bias,
    )


def solution(mesh):
    return jax.shard_map(
        local,
        mesh=mesh,
        in_specs=(
            P("dp", None),
            P("dp", None, None),
            P("dp"),
            P("dp", None),
            P(),
            P(),
            P(None, "tp"),
            P("tp"),
            P(None, "tp"),
            P(None, "tp"),
            P("tp"),
            P("tp", None),
            P(),
            P(),
            P(),
            P(None, "tp"),
            P("tp"),
            P(None, "tp"),
            P(None, "tp"),
            P("tp"),
            P("tp", None),
            P(),
            P(),
            P(),
            P(None, "tp"),
            P("tp"),
            P("tp", None),
            P(),
        ),
        out_specs=(
            P("dp", None),
            P("dp", None),
            P(),
            P(),
            P(None, "tp"),
            P("tp"),
            P(None, "tp"),
            P(None, "tp"),
            P("tp"),
            P("tp", None),
            P(),
            P(),
            P(),
            P(None, "tp"),
            P("tp"),
            P(None, "tp"),
            P(None, "tp"),
            P("tp"),
            P("tp", None),
            P(),
            P(),
            P(),
            P(None, "tp"),
            P("tp"),
            P("tp", None),
            P(),
        ),
        check_vma=False,
    )
```

```python
from functools import partial

import jax
import jax.numpy as jnp
from jax import lax
from jax.experimental import pallas as pl
from jax.experimental.pallas import tpu as pltpu
from jax.sharding import PartitionSpec as P


D = 384
HEAD = 64
HALF = D // 2
SHORT_LEN = 64
MID_LEN = 128
LONG_LEN = 448
SHORT_N = 8
MID_N = 2
LONG_N = 1
SEQ_TOTAL = SHORT_N + MID_N + LONG_N

HEAD_SHORTS = 3
BLOCK = 64
FIRST_ROWS = HEAD_SHORTS * BLOCK
ROWS = FIRST_ROWS + LONG_LEN
BLOCKS = ROWS // BLOCK
REGION_BLOCKS = LONG_LEN // BLOCK
STEPS = 7
PAIRS = D // 128
CHUNK = 256
WEIGHTS = 8
LINES = 320
SMALL = 24


epsilon = 1e-05
masked = -1e30
scale = HEAD ** (-0.5)

f32 = jnp.float32
bf16 = jnp.bfloat16


def round_up(value, unit):
    return -(-value // unit) * unit


def dot(left, right):
    return lax.dot_general(left, right, (((1,), (0,)), ((), ())), preferred_element_type=f32)


def dot_nt(left, right):
    return lax.dot_general(left, right, (((1,), (1,)), ((), ())), preferred_element_type=f32)


def dot_tn(left, right):
    return lax.dot_general(left, right, (((0,), (0,)), ((), ())), preferred_element_type=f32)


def norm_parts(values):
    row_mean = jnp.mean(values, -1, keepdims=True)
    centered = values - row_mean
    variance = jnp.mean(centered * centered, -1, keepdims=True)
    inverse = lax.rsqrt(variance + epsilon)
    return centered * inverse, inverse


def norm_back(normed, inverse, gain, incoming):
    scaled = incoming * gain
    return inverse * (
        scaled
        - jnp.mean(scaled, -1, keepdims=True)
        - normed * jnp.mean(scaled * normed, -1, keepdims=True)
    )


def column_sum(values):
    return jnp.sum(values, 0, keepdims=True)


def own_row(block, core):
    first = (core * HEAD_SHORTS + block) * BLOCK
    region = jnp.where(core == 0, SHORT_N * SHORT_LEN + MID_N * MID_LEN, 2 * FIRST_ROWS)
    return jnp.where(block < HEAD_SHORTS, first, region + (block - HEAD_SHORTS) * BLOCK)


def block_segment(block, core, lens):
    place = block - HEAD_SHORTS
    start = jnp.where(
        place < 2, place * BLOCK, jnp.where(place < 4, 2 * BLOCK, jnp.where(place < 6, 4 * BLOCK, 6 * BLOCK))
    )
    start = jnp.where((block < HEAD_SHORTS) | (core == 0), 0, start)
    seq = jnp.where(place < 2, 2 * HEAD_SHORTS + place, jnp.where(place < 4, SHORT_N, SHORT_N + 1))
    seq = jnp.where(core == 0, SEQ_TOTAL - 1, seq)
    seq = jnp.where(block < HEAD_SHORTS, core * HEAD_SHORTS + block, seq)
    padding = (core == 1) & (block == BLOCKS - 1)
    length = jnp.where(padding, BLOCK, lens[seq])
    return start, length, padding


def rows_of(index, count):
    return pl.ds(pl.multiple_of(index * count, count), count)


def head_masks(count=BLOCK):
    lane = lax.broadcasted_iota(jnp.int32, (count, 128), 1)
    low = (lane < HEAD).astype(f32)
    return low.astype(bf16), (1.0 - low).astype(bf16), lane < HEAD


def stacked(values, low, high):
    return jnp.concatenate([values * low, values * high], 0)


def joined(product, is_low):
    count = is_low.shape[0]
    return jnp.where(is_low, product[:count], product[count:])


def key_span(block):
    if block < HEAD_SHORTS:
        return block * BLOCK, BLOCK
    return FIRST_ROWS, min(LONG_LEN, round_up((block - HEAD_SHORTS + 1) * BLOCK, 128))


def self_mask(block, core, lens, key_count):
    start, length, _ = block_segment(block, core, lens)
    place = jnp.where(block < HEAD_SHORTS, 0, (block - HEAD_SHORTS) * BLOCK)
    row = lax.broadcasted_iota(jnp.int32, (2 * BLOCK, key_count), 0) & (BLOCK - 1)
    column = lax.broadcasted_iota(jnp.int32, (2 * BLOCK, key_count), 1)
    return (column <= row + place) & (column >= start) & (column < start + length)


def pack_halves(left, right):
    lane = lax.broadcasted_iota(jnp.int32, left.shape, 1) < HALF
    own = jnp.where(lane, left, pltpu.roll(right, HALF, 1))
    other = jnp.where(lane, pltpu.roll(left, HALF, 1), right)
    return own, other


def pack_kernel(*refs):
    weights, vectors, biases = refs[:WEIGHTS], refs[WEIGHTS : WEIGHTS + 9], refs[WEIGHTS + 9 : WEIGHTS + 14]
    pack_ref, vec_ref, bias_ref = refs[WEIGHTS + 14 :]
    for number, ref in enumerate(weights):
        pack_ref[number * HALF : number * HALF + HALF, :] = ref[...]
    vec_ref[...] = jnp.zeros(vec_ref.shape, f32)
    bias_ref[...] = jnp.zeros(bias_ref.shape, f32)
    for number, ref in enumerate(vectors):
        vec_ref[number : number + 1, :] = ref[...].astype(f32).reshape(1, D)
    for number, ref in enumerate(biases[:4]):
        at = number % 2 * HALF
        bias_ref[number // 2 : number // 2 + 1, at : at + HALF] = ref[...].astype(f32).reshape(1, HALF)
    for part in range(2):
        bias_ref[2 + part : 3 + part, :] = biases[4][part * D : part * D + D].astype(f32).reshape(1, D)
    pack_ref[WEIGHTS * HALF :, :] = bias_ref[...].astype(bf16)


def bias_rows(near_ref, far_ref):
    near, far = near_ref[...].astype(f32)[:8], far_ref[...].astype(f32)[:8]
    return pack_halves(near, far)[0], pack_halves(near, far)[1], near, far


def weight_copies(near_refs, far_ref, numbers, full_refs, sem):
    copies = []
    for index, (near_ref, number, full_ref) in enumerate(zip(near_refs, numbers, full_refs)):
        copies.append(pltpu.make_async_copy(near_ref, full_ref.at[pl.ds(0, HALF)], sem.at[2 * index]))
        copies.append(
            pltpu.make_async_copy(
                far_ref.at[pl.ds(number * HALF, HALF)], full_ref.at[pl.ds(HALF, HALF)], sem.at[2 * index + 1]
            )
        )
    for copy in copies:
        copy.start()
    return copies


def self_forward_kernel(
    core_ref, lens_ref, hidden_ref, vec_ref, near_ref, far_bias_ref, wq_near, wk_near, wv_near, wo_near, wc_near, far_ref,
    own_ref, n1_ref, q_ref, k_ref, v_ref, ctx_ref, r1_ref, n2_ref, qc_ref, lse_ref,
    w_ref, wo_ref, wc_ref, sem,
):
    core = core_ref[0]
    copies = weight_copies(
        (wq_near, wk_near, wv_near, wo_near, wc_near), far_ref, (0, 1, 2, 6, 3),
        (w_ref.at[pl.ds(0, D)], w_ref.at[pl.ds(D, D)], w_ref.at[pl.ds(2 * D, D)], wo_ref, wc_ref), sem,
    )
    first_bias, second_bias, _, _ = bias_rows(near_ref, far_bias_ref)
    q_bias, v_bias, c_bias = first_bias[0:1], second_bias[0:1], first_bias[1:2]

    def gather(block, carry):
        own_ref[rows_of(block, BLOCK), :] = hidden_ref[
            pl.ds(pl.multiple_of(own_row(block, core), BLOCK), BLOCK), :
        ]
        return carry

    lax.fori_loop(0, BLOCKS, gather, 0)
    for copy in copies:
        copy.wait()

    def project(chunk, carry):
        rows = rows_of(chunk, LINES)
        normed, _ = norm_parts(own_ref[rows, :].astype(f32))
        n1 = (normed * vec_ref[0:1, :] + vec_ref[1:2, :]).astype(bf16)
        n1_ref[rows, :] = n1
        all_three = dot_nt(n1, w_ref[...])
        q_ref[rows, :] = (all_three[:, :D] + q_bias).astype(bf16)
        k_ref[rows, :] = all_three[:, D : 2 * D].astype(bf16)
        v_ref[rows, :] = (all_three[:, 2 * D :] + v_bias).astype(bf16)
        return carry

    lax.fori_loop(0, ROWS // LINES, project, 0)
    low, high, is_low = head_masks()

    def attend(block):
        rows = pl.ds(block * BLOCK, BLOCK)
        first_key, key_count = key_span(block)
        keys = pl.ds(first_key, key_count)
        allowed = self_mask(block, core, lens_ref, key_count)
        cols = [slice(pair * 128, pair * 128 + 128) for pair in range(PAIRS)]
        scores = [dot_nt(stacked(q_ref[rows, c] * scale, low, high), k_ref[keys, c]) for c in cols]
        scores = [jnp.where(allowed, values, masked) for values in scores]
        tops = [jnp.max(values, -1, keepdims=True) for values in scores]
        expo = [jnp.exp(values - top) for values, top in zip(scores, tops)]
        totals = [jnp.sum(values, -1, keepdims=True) for values in expo]
        parts = [dot(values.astype(bf16), v_ref[keys, c]) for values, c in zip(expo, cols)]
        for pair in range(PAIRS):
            ctx_ref[rows, cols[pair]] = joined(parts[pair] * (1.0 / totals[pair]), is_low).astype(bf16)
            lse_ref[pl.ds(block * 2 * BLOCK, 2 * BLOCK), pair : pair + 1] = tops[pair] + jnp.log(totals[pair])

    for block in range(BLOCKS):
        attend(block)

    def finish(chunk, carry):
        rows = rows_of(chunk, LINES)
        r1 = own_ref[rows, :].astype(f32) + dot(ctx_ref[rows, :], wo_ref[...]) + vec_ref[2:3, :]
        r1_ref[rows, :] = r1
        normed, _ = norm_parts(r1)
        n2 = (normed * vec_ref[3:4, :] + vec_ref[4:5, :]).astype(bf16)
        n2_ref[rows, :] = n2
        qc_ref[rows, :] = (dot_nt(n2, wc_ref[...]) + c_bias).astype(bf16)
        return carry

    lax.fori_loop(0, ROWS // LINES, finish, 0)


def step_count(core):
    return jnp.where(core == 0, HEAD_SHORTS + 1, STEPS)


def step_seq(step, core):
    step = jnp.minimum(step, step_count(core) - 1)
    return jnp.where(core == 0, jnp.where(step < HEAD_SHORTS, step, SEQ_TOTAL - 1), HEAD_SHORTS + step)


def step_blocks(step, core):
    count = jnp.where(step < HEAD_SHORTS, 1, jnp.where(core == 0, REGION_BLOCKS, jnp.where(step < 5, 1, 2)))
    first = jnp.where(step < 6, step, 7)
    return first, count


def each_block(first, count, attend):
    pairs = count // 2

    def two(turn, carry):
        attend(2 * BLOCK, first + 2 * turn)
        return carry

    lax.fori_loop(0, pairs, two, 0)

    @pl.when(count % 2 == 1)
    def _():
        attend(BLOCK, first + count - 1)


def cross_forward_kernel(
    frame_total, core_ref, frames_ref, qc_ref, near_ref, far_bias_ref, wk_near, wv_near, far_ref,
    k_ref, v_ref, ctx_ref, lse_ref, w_ref, score_ref, sem,
):
    step = pl.program_id(0)
    core = core_ref[0]
    padded = k_ref.shape[1]
    tail = padded - 128

    @pl.when(step == 0)
    def _():
        copies = weight_copies(
            (wk_near, wv_near), far_ref, (4, 5), (w_ref.at[pl.ds(0, D)], w_ref.at[pl.ds(D, D)]), sem
        )
        ctx_ref[ROWS - BLOCK :, :] = jnp.zeros((BLOCK, D), bf16)
        for copy in copies:
            copy.wait()

    @pl.when(step < step_count(core))
    def _():
        k_ref[0, padded - 64 :, :] = jnp.zeros((64, D), bf16)
        v_ref[0, padded - 64 :, :] = jnp.zeros((64, D), bf16)
        bias = bias_rows(near_ref, far_bias_ref)[1][1:2]
        for top in range(0, frame_total, 512):
            end = min(top + 512, frame_total)
            part = frames_ref[0, top:end, :]
            both = dot_nt(part, w_ref[...])
            k_ref[0, top:end, :] = both[:, :D].astype(bf16)
            v_ref[0, top:end, :] = (both[:, D:] + bias).astype(bf16)
        first, count = step_blocks(step, core)

        def attend(lines, block):
            rows = pl.ds(pl.multiple_of(block * BLOCK, BLOCK), lines)
            stack = 2 * lines
            low, high, is_low = head_masks(lines)
            inside = lax.broadcasted_iota(jnp.int32, (stack, 128), 1) < frame_total - tail

            def score(pair):
                cols = slice(pair * 128, pair * 128 + 128)
                query = stacked(qc_ref[rows, cols] * scale, low, high)
                tops = jnp.full((stack, 128), masked, f32)
                for at in range(0, padded, CHUNK):
                    values = dot_nt(query, k_ref[0, at : at + CHUNK, cols])
                    if at + CHUNK == padded:
                        values = jnp.concatenate(
                            [values[:, : CHUNK - 128], jnp.where(inside, values[:, CHUNK - 128 :], masked)], 1
                        )
                    score_ref[pair % 2, :stack, at : at + CHUNK] = values
                    for lane in range(0, CHUNK, 128):
                        tops = jnp.maximum(tops, values[:, lane : lane + 128])
                return jnp.max(tops, -1, keepdims=True)

            def weigh(pair, top):
                cols = slice(pair * 128, pair * 128 + 128)
                totals = jnp.zeros((stack, 128), f32)
                product = jnp.zeros((stack, 128), f32)
                for at in range(0, padded, CHUNK):
                    expo = jnp.exp(score_ref[pair % 2, :stack, at : at + CHUNK] - top)
                    for lane in range(0, CHUNK, 128):
                        totals = totals + expo[:, lane : lane + 128]
                    product = product + dot(expo.astype(bf16), v_ref[0, at : at + CHUNK, cols])
                total = jnp.sum(totals, -1, keepdims=True)
                ctx_ref[rows, cols] = joined(product * (1.0 / total), is_low).astype(bf16)
                lse_ref[pl.ds(pl.multiple_of(block * 2 * BLOCK, 128), stack), pair : pair + 1] = top + jnp.log(total)

            top = score(0)
            for pair in range(PAIRS):
                following = score(pair + 1) if pair + 1 < PAIRS else None
                weigh(pair, top)
                top = following

        each_block(first, count, attend)


def feed_kernel(
    core_ref, lens_ref, cot_ref, r1_ref, ctx_ref, vec_ref, near_ref, far_bias_ref,
    wo_near, far_ref, w1_near, w1_far, w2_near, w2_far,
    out_ref, g2_ref, dctx_ref, keep_ref, send_ref, small_ref,
    top_ref, n3_ref, act_ref, pre_ref, low_ref, wo_ref, w1_ref, w2_ref, sem,
):
    core = core_ref[0]
    half = w2_near.shape[0]
    copies = weight_copies((wo_near,), far_ref, (7,), (wo_ref,), sem)
    copies.append(pltpu.make_async_copy(w1_near, w1_ref.at[:, pl.ds(0, half)], sem.at[2]))
    copies.append(pltpu.make_async_copy(w1_far, w1_ref.at[:, pl.ds(half, half)], sem.at[3]))
    copies.append(pltpu.make_async_copy(w2_near, w2_ref.at[pl.ds(0, half)], sem.at[4]))
    copies.append(pltpu.make_async_copy(w2_far, w2_ref.at[pl.ds(half, half)], sem.at[5]))
    for copy in copies[2:]:
        copy.start()
    _, _, near, far = bias_rows(near_ref, far_bias_ref)
    b1 = jnp.concatenate([near[2:3], near[3:4], far[2:3], far[3:4]], 1)

    def block_rows(block, carry):
        rows = rows_of(block, BLOCK)
        start, length, padding = block_segment(block, core, lens_ref)
        place = jnp.where(block < HEAD_SHORTS, 0, (block - HEAD_SHORTS) * BLOCK) - start
        length = jnp.where(padding, 0, length)
        row = lax.broadcasted_iota(jnp.int32, (BLOCK, D), 0) + place
        cot = cot_ref[pl.ds(pl.multiple_of(own_row(block, core), BLOCK), BLOCK), :].astype(f32)
        top_ref[rows, :] = jnp.where(row < length, cot, 0.0).astype(bf16)
        return carry

    lax.fori_loop(0, BLOCKS, block_rows, 0)
    small_ref[...] = jnp.zeros(small_ref.shape, f32)
    for copy in copies:
        copy.wait()

    def chunk_rows(chunk, sums):
        rows = rows_of(chunk, LINES)
        r2 = r1_ref[rows, :] + dot(ctx_ref[rows, :], wo_ref[...]) + vec_ref[5:6, :]
        normed, inverse = norm_parts(r2)
        gain = vec_ref[6:7, :]
        n3 = (normed * gain + vec_ref[7:8, :]).astype(bf16)
        n3_ref[rows, :] = n3
        pre = dot(n3, w1_ref[...]) + b1
        phi = 0.5 * (1.0 + lax.erf(pre * (0.5**0.5)))
        act = (pre * phi).astype(bf16)
        act_ref[rows, :] = act
        out_ref[rows, :] = (r2 + dot(act, w2_ref[...]) + vec_ref[8:9, :]).astype(bf16)
        top = top_ref[rows, :]
        slope = phi + pre * (jnp.exp(-0.5 * pre * pre) * 0.3989422804014327)
        grad_pre = (dot_nt(top, w2_ref[...]) * slope).astype(bf16)
        pre_ref[rows, :] = grad_pre
        grad_n3 = dot_nt(grad_pre, w1_ref[...])
        top32 = top.astype(f32)
        g2 = top32 + norm_back(normed, inverse, gain, grad_n3)
        g2_ref[rows, :] = g2
        low = g2.astype(bf16)
        low_ref[rows, :] = low
        dctx_ref[rows, :] = dot_nt(low, wo_ref[...]).astype(bf16)
        small_ref[0:1, :] += column_sum(top32)
        small_ref[1:2, :] += column_sum(grad_n3 * normed)
        small_ref[2:3, :] += column_sum(grad_n3)
        small_ref[3:4, :] += column_sum(g2)
        bias = column_sum(grad_pre.astype(f32))
        for part in range(4):
            small_ref[4 + part : 5 + part, :] += bias[:, part * D : part * D + D]
        return sums

    lax.fori_loop(0, ROWS // LINES, chunk_rows, 0)

    def mask_rows(block, carry):
        rows = rows_of(block, BLOCK)
        start, length, _ = block_segment(block, core, lens_ref)
        place = jnp.where(block < HEAD_SHORTS, 0, (block - HEAD_SHORTS) * BLOCK) - start
        row = lax.broadcasted_iota(jnp.int32, (BLOCK, D), 0) + place
        out_ref[rows, :] = jnp.where(row < length, out_ref[rows, :].astype(f32), 0.0).astype(bf16)
        return carry

    lax.fori_loop(0, BLOCKS, mask_rows, 0)
    for part in range(4):
        cols = slice(part * D, part * D + D)
        target, at = (keep_ref, part) if part < 2 else (send_ref, part - 2)
        target[at * D : at * D + D, :] = dot_tn(n3_ref[...], pre_ref[:, cols]).astype(target.dtype)
        grad = dot_tn(act_ref[:, cols], top_ref[...])
        target[half + at * D : half + at * D + D, :] = grad.astype(target.dtype)
    grad = dot_tn(ctx_ref[...], low_ref[...])
    keep_ref[2 * half : 2 * half + HALF, :] = grad[:HALF]
    send_ref[2 * half : 2 * half + HALF, :] = grad[HALF:].astype(bf16)
    extra = keep_ref.shape[0] - (2 * half + HALF)
    if extra:
        keep_ref[2 * half + HALF :, :] = jnp.zeros((extra, D), f32)
        send_ref[2 * half + HALF :, :] = jnp.zeros((extra, D), bf16)


def cross_backward_kernel(
    frame_total, first_step, core_ref, frames_ref, k_ref, v_ref, qc_ref, ctx_ref, dctx_ref, lse_ref, *refs
):
    if first_step:
        dq_in_ref, grad_in_ref, bias_in_ref = refs[:3]
    dq_ref, grad_ref, bias_ref, both_ref = refs[-4:]
    step = pl.program_id(0) + first_step
    core = core_ref[0]
    padded = k_ref.shape[1]

    @pl.when(step == first_step)
    def _():
        if first_step:
            dq_ref[...] = dq_in_ref[...]
            dq_ref[ROWS - BLOCK :, :] = jnp.zeros((BLOCK, D), bf16)
            grad_ref[...] = grad_in_ref[...]
            bias_ref[...] = bias_in_ref[...]
        else:
            grad_ref[...] = jnp.zeros(grad_ref.shape, f32)
            bias_ref[...] = jnp.zeros(bias_ref.shape, f32)

    @pl.when(step < step_count(core))
    def _():
        first, count = step_blocks(step, core)

        def attend(lines, block):
            rows = pl.ds(pl.multiple_of(block * BLOCK, BLOCK), lines)
            low, high, is_low = head_masks(lines)
            carried = block > first
            setups = []
            for pair in range(PAIRS):
                cols = slice(pair * 128, pair * 128 + 128)
                query = stacked(qc_ref[rows, cols] * scale, low, high)
                grad_out = stacked(dctx_ref[rows, cols], low, high)
                ctx = ctx_ref[rows, cols].astype(f32)
                spread = jnp.sum(grad_out.astype(f32) * jnp.concatenate([ctx, ctx], 0), -1, keepdims=True)
                lse = lse_ref[pl.ds(pl.multiple_of(block * 2 * BLOCK, 128), 2 * lines), pair : pair + 1]
                setups.append((cols, query, grad_out, query.T, grad_out.T, spread, lse))

            def begin(pair, at):
                cols, query, grad_out = setups[pair][:3]
                keys = slice(at, at + CHUNK)
                return dot_nt(query, k_ref[0, keys, cols]), dot_nt(grad_out, v_ref[0, keys, cols])

            def end(pair, at, scores, grad_weights):
                cols, _, _, query_t, grad_out_t, spread, lse = setups[pair]
                keys = slice(at, at + CHUNK)
                weights = jnp.exp(scores - lse)
                grad_scores = (weights * (grad_weights - spread)).astype(bf16)
                values = slice(D + cols.start, D + cols.stop)
                old_key = jnp.where(carried, both_ref[cols, keys], 0.0)
                old_value = jnp.where(carried, both_ref[values, keys], 0.0)
                both_ref[cols, keys] = old_key + dot(query_t, grad_scores)
                both_ref[values, keys] = old_value + dot(grad_out_t, weights.astype(bf16))
                return dot(grad_scores, k_ref[0, keys, cols])

            order = [(pair, at) for pair in range(PAIRS) for at in range(0, padded, CHUNK)]
            ahead = begin(*order[0])
            grad_query = None
            for index, (pair, at) in enumerate(order):
                now = ahead
                if index + 1 < len(order):
                    ahead = begin(*order[index + 1])
                part = end(pair, at, *now)
                grad_query = part if at == 0 else grad_query + part
                if at + CHUNK == padded:
                    dq_ref[rows, setups[pair][0]] = (joined(grad_query, is_low) * scale).astype(bf16)

        if first_step < HEAD_SHORTS:
            attend(BLOCK, first)
        else:
            each_block(first, count, attend)
        both = both_ref[:, :frame_total].astype(bf16)
        grad_ref[...] += dot(both, frames_ref[0])
        bias_ref[:, 0:1] += jnp.sum(both[D:].astype(f32), -1, keepdims=True)


def self_attention_back_kernel(
    core_ref, lens_ref, vec_ref, wo_near, wc_near, far_ref, q_ref, k_ref, v_ref, ctx_ref, r1_ref, lse_ref,
    dqc_ref, g2_ref, after_ref,
    g1_ref, low_ref, dq_ref, dk_ref, dv_ref, small_ref,
    dctx_ref, dk_acc, dv_acc, wo_ref, wc_ref, sem,
):
    core = core_ref[0]
    copies = weight_copies((wo_near, wc_near), far_ref, (6, 3), (wo_ref, wc_ref), sem)
    small_ref[...] = jnp.zeros(small_ref.shape, f32)
    dk_acc[...] = jnp.zeros(dk_acc.shape, f32)
    dv_acc[...] = jnp.zeros(dv_acc.shape, f32)
    for copy in copies:
        copy.wait()

    def enter(chunk, carry):
        rows = rows_of(chunk, LINES)
        dqc = dqc_ref[rows, :]
        grad_n2 = dot(dqc, wc_ref[...])
        normed, inverse = norm_parts(r1_ref[rows, :])
        g1 = g2_ref[rows, :] + norm_back(normed, inverse, vec_ref[3:4, :], grad_n2)
        g1_ref[rows, :] = g1
        low = g1.astype(bf16)
        low_ref[rows, :] = low
        dctx_ref[rows, :] = dot_nt(low, wo_ref[...]).astype(bf16)
        small_ref[0:1, :] += column_sum(dqc.astype(f32))
        small_ref[1:2, :] += column_sum(grad_n2 * normed)
        small_ref[2:3, :] += column_sum(grad_n2)
        small_ref[3:4, :] += column_sum(g1)
        return carry

    lax.fori_loop(0, ROWS // LINES, enter, 0)
    low, high, is_low = head_masks()

    def attend(block):
        rows = pl.ds(block * BLOCK, BLOCK)
        first_key, key_count = key_span(block)
        keys = pl.ds(first_key, key_count)
        allowed = self_mask(block, core, lens_ref, key_count)
        cols = [slice(pair * 128, pair * 128 + 128) for pair in range(PAIRS)]
        queries = [stacked(q_ref[rows, c] * scale, low, high) for c in cols]
        grad_outs = [stacked(dctx_ref[rows, c], low, high) for c in cols]
        ctxs = [ctx_ref[rows, c].astype(f32) for c in cols]
        spreads = [
            jnp.sum(grad_out.astype(f32) * jnp.concatenate([ctx, ctx], 0), -1, keepdims=True)
            for grad_out, ctx in zip(grad_outs, ctxs)
        ]
        scores = [dot_nt(query, k_ref[keys, c]) for query, c in zip(queries, cols)]
        grad_weights = [dot_nt(grad_out, v_ref[keys, c]) for grad_out, c in zip(grad_outs, cols)]
        for pair, c in enumerate(cols):
            lse = lse_ref[pl.ds(block * 2 * BLOCK, 2 * BLOCK), pair : pair + 1]
            weights = jnp.exp(jnp.where(allowed, scores[pair] - lse, masked))
            grad_scores = (weights * (grad_weights[pair] - spreads[pair])).astype(bf16)
            dq_ref[rows, c] = (joined(dot(grad_scores, k_ref[keys, c]), is_low) * scale).astype(bf16)
            if block < HEAD_SHORTS:
                dk_ref[rows, c] = dot_tn(grad_scores, queries[pair]).astype(bf16)
                dv_ref[rows, c] = dot_tn(weights.astype(bf16), grad_outs[pair]).astype(bf16)
            else:
                dk_acc[c, :key_count] += dot(queries[pair].T, grad_scores)
                dv_acc[c, :key_count] += dot(grad_outs[pair].T, weights.astype(bf16))

    for block in range(BLOCKS):
        attend(block)
    dk_ref[FIRST_ROWS:, :] = dk_acc[...].T.astype(bf16)
    dv_ref[FIRST_ROWS:, :] = dv_acc[...].T.astype(bf16)


def self_weights_kernel(
    n1_ref, n2_ref, ctx_ref, low_ref, dq_ref, dk_ref, dv_ref, dqc_ref, cross_ref, after_ref, keep_ref, send_ref
):
    def place(number, grad):
        rows = slice(number * HALF, number * HALF + HALF)
        keep_ref[rows, :] = grad[:HALF]
        send_ref[rows, :] = grad[HALF:].astype(bf16)

    place(0, cross_ref[:D, :])
    place(1, cross_ref[D:, :])
    place(2, dot_tn(dq_ref[...], n1_ref[...]))
    place(3, dot_tn(dk_ref[...], n1_ref[...]))
    place(4, dot_tn(dv_ref[...], n1_ref[...]))
    place(5, dot_tn(dqc_ref[...], n2_ref[...]))
    place(6, dot_tn(ctx_ref[...], low_ref[...]))
    base = 7 * HALF
    rest = keep_ref.shape[0] - base
    if rest:
        keep_ref[base:, :] = jnp.zeros((rest, D), f32)
        send_ref[base:, :] = jnp.zeros((rest, D), bf16)


def self_finish_kernel(
    own_ref, vec_ref, wq_near, wk_near, wv_near, far_ref,
    g1_ref, dq_ref, dk_ref, dv_ref, back_small_ref, feed_small_ref, cross_bias_ref, after_ref,
    dh_ref, out_small_ref,
    small_ref, wq_ref, wk_ref, wv_ref, sem,
):
    copies = weight_copies((wq_near, wk_near, wv_near), far_ref, (0, 1, 2), (wq_ref, wk_ref, wv_ref), sem)
    small_ref[...] = jnp.zeros(small_ref.shape, f32)
    for copy in copies:
        copy.wait()

    def leave(chunk, carry):
        rows = rows_of(chunk, LINES)
        dq, dk, dv = dq_ref[rows, :], dk_ref[rows, :], dv_ref[rows, :]
        grad_n1 = dot(dq, wq_ref[...]) + dot(dk, wk_ref[...]) + dot(dv, wv_ref[...])
        normed, inverse = norm_parts(own_ref[rows, :].astype(f32))
        g1 = g1_ref[rows, :] + norm_back(normed, inverse, vec_ref[0:1, :], grad_n1)
        dh_ref[rows, :] = g1.astype(bf16)
        small_ref[4:5, :] += column_sum(dq.astype(f32))
        small_ref[5:6, :] += column_sum(dv.astype(f32))
        small_ref[6:7, :] += column_sum(grad_n1 * normed)
        small_ref[7:8, :] += column_sum(grad_n1)
        return carry

    lax.fori_loop(0, ROWS // LINES, leave, 0)
    cross_bias = cross_bias_ref[...].T[0:8, :]
    left = jnp.concatenate([small_ref[4:5, :], back_small_ref[0:1, :], jnp.zeros((6, D), f32)], 0)
    right = jnp.concatenate([small_ref[5:6, :], cross_bias[0:1, :], jnp.zeros((6, D), f32)], 0)
    own, other = pack_halves(left, right)
    out_small_ref[...] = jnp.concatenate(
        [
            own[0:2], feed_small_ref[4:6, :],
            small_ref[6:7, :], small_ref[7:8, :], back_small_ref[3:4, :], back_small_ref[1:2, :], back_small_ref[2:3, :],
            feed_small_ref[3:4, :], feed_small_ref[1:2, :], feed_small_ref[2:3, :], feed_small_ref[0:1, :],
            jnp.zeros((3, D), f32),
            other[0:2], feed_small_ref[6:8, :],
            jnp.zeros((4, D), f32),
        ],
        0,
    )


vmem = pl.BlockSpec(memory_space=pltpu.VMEM)
smem = pl.BlockSpec(memory_space=pltpu.SMEM)
anywhere = pl.BlockSpec(memory_space=pl.ANY)


def shaped(shape, dtype):
    return jax.ShapeDtypeStruct(shape, dtype)


def constant(shape):
    return pl.BlockSpec(shape, lambda step, core: (0,) * len(shape))


def call(kernel, scalars, operands, outs, scratch=(), flops=0, nbytes=0, far=()):
    return pl.pallas_call(
        kernel,
        out_shape=outs,
        in_specs=[smem] * len(scalars) + [anywhere if place in far else vmem for place in range(len(operands))],
        out_specs=[vmem] * len(outs),
        scratch_shapes=list(scratch),
        cost_estimate=pl.CostEstimate(flops=flops, bytes_accessed=nbytes, transcendentals=0),
    )(*scalars, *operands)


def stage_list(count):
    stages = []
    stride = 1
    while stride < count:
        radix = 4 if count // stride % 4 == 0 else 2
        stages.append((stride, radix))
        stride = stride * radix
    return stages


def partner(count, stride, radix, turn):
    pairs = []
    for index in range(count):
        digit = index // stride % radix
        pairs.append((index, index + ((digit ^ turn) - digit) * stride))
    return pairs


def arrived_sum(total, arrived, rows):
    for ref in arrived:
        total = total + ref[rows, :].astype(f32)
    return total


def spread_kernel(received, unread, has_small, joined_small, digit_ref, keep_in_ref, *refs):
    if has_small:
        small_in_ref, refs = refs[0], refs[1:]
    arrived = refs[:received]
    outs = refs[received + unread :]
    if has_small:
        small_ref, outs = outs[0], outs[1:]
    digit = digit_ref[0]
    part = outs[0].shape[0]
    if has_small:
        small = small_in_ref[...]
        if joined_small:
            small = arrived_sum(small, arrived, pl.ds(keep_in_ref.shape[0], SMALL))
        small_ref[...] = small
    for turn, out_ref in enumerate(outs):
        rows = pl.ds(pl.multiple_of((digit ^ turn) * part, part), part)
        total = arrived_sum(keep_in_ref[rows, :], arrived, rows)
        out_ref[:part, :] = total.astype(out_ref.dtype)
        if has_small and turn:
            out_ref[part:, :] = small.astype(bf16)


def last_kernel(received, has_small, keep_in_ref, *refs):
    if has_small:
        small_in_ref, refs = refs[0], refs[1:]
    arrived, outs = refs[:received], refs[received:]
    outs[0][...] = arrived_sum(keep_in_ref[...], arrived, pl.ds(0, keep_in_ref.shape[0])).astype(bf16)
    if has_small:
        small = arrived_sum(small_in_ref[...], arrived, pl.ds(keep_in_ref.shape[0], SMALL))
        outs[1][...] = small
        outs[2][...] = small.astype(bf16)


def gather_kernel(digit_ref, *refs):
    out_ref = refs[-1]
    digit = digit_ref[0]
    part = refs[0].shape[0]
    for turn, ref in enumerate(refs[:-1]):
        out_ref[pl.ds(pl.multiple_of((digit ^ turn) * part, part), part), :] = ref[...]


class RowSum:
    def __init__(self, keep, send, swap):
        self.count = lax.axis_size("dp")
        self.index = lax.axis_index("dp")
        self.stages = stage_list(self.count)
        self.small = None
        self.after = None
        self.swap = swap
        self.current = keep
        self.arrived = [lax.ppermute(send, "tp", swap)]
        self.digits = [(self.index // stride % radix).reshape(1) for stride, radix in self.stages]

    def permute(self, value, number, turn):
        stride, radix = self.stages[number]
        return lax.ppermute(value, "dp", partner(self.count, stride, radix, turn))

    def spread(self, number):
        _, radix = self.stages[number]
        rows = self.current.shape[0] // radix
        small = [] if self.small is None else [self.small]
        extra = SMALL if small else 0
        after = [] if self.after is None or number else [self.after]
        operands = [self.current] + small + self.arrived
        pieces = call(
            partial(spread_kernel, len(self.arrived), len(after), bool(small), number > 0),
            [self.digits[number]], operands + after,
            [shaped(value.shape, f32) for value in small]
            + [shaped((rows, D), f32)] + [shaped((rows + extra, D), bf16)] * (radix - 1),
            nbytes=self.current.size * 8, far=range(len(operands), len(operands) + len(after)),
        )
        if small:
            self.small, pieces = pieces[0], pieces[1:]
        self.current = pieces[0]
        self.arrived = [self.permute(piece, number, turn + 1) for turn, piece in enumerate(pieces[1:])]
        return pieces[0]

    def last(self):
        small = [] if self.small is None else [self.small]
        total = call(
            partial(last_kernel, len(self.arrived), bool(small)), [],
            [self.current] + small + self.arrived,
            [shaped(self.current.shape, bf16)] + [shaped((SMALL, D), f32), shaped((SMALL, D), bf16)] * len(small),
            nbytes=self.current.size * 8,
        )
        if small:
            self.small = total[1]
            self.small_far = lax.ppermute(total[2], "tp", self.swap)
        return self.widen(total[0], len(self.stages) - 1)

    def widen(self, total, number):
        self.pieces = [total] + [self.permute(total, number, turn) for turn in range(1, self.stages[number][1])]
        return total

    def gather(self, number):
        total = self.pieces[0]
        total = call(
            gather_kernel, [self.digits[number]], self.pieces,
            [shaped((total.shape[0] * self.stages[number][1], D), bf16)], nbytes=total.size * 16,
        )[0]
        return self.widen(total, number - 1)

    def steps(self):
        numbers = range(len(self.stages))
        return (
            [partial(self.spread, number) for number in numbers]
            + [self.last]
            + [partial(self.gather, number) for number in reversed(numbers) if number]
        )


def assemble(digit, pieces, full_ref):
    part = pieces[0].shape[0]
    for turn, ref in enumerate(pieces):
        full_ref[pl.ds(pl.multiple_of((digit ^ turn) * part, part), part), :] = ref[...]


def feed_finish_kernel(count, digit_ref, *refs):
    w1_ref, w2_ref, wo_ref, full_ref = refs[count:]
    assemble(digit_ref[0], refs[:count], full_ref)
    half = w2_ref.shape[0]
    for part in range(half // D):
        w1_ref[:, part * D : part * D + D] = full_ref[part * D : part * D + D, :].astype(f32)
    w2_ref[...] = full_ref[half : 2 * half, :].astype(f32)
    wo_ref[...] = full_ref[2 * half : 2 * half + HALF, :].astype(f32)


def attention_finish_kernel(count, digit_ref, small_ref, far_ref, *refs):
    outs, full_ref = refs[count:-1], refs[-1]
    assemble(digit_ref[0], refs[:count], full_ref)
    for number, ref in enumerate(outs[:7]):
        ref[...] = full_ref[number * HALF : number * HALF + HALF, :].astype(f32)
    mine, far = small_ref[...], far_ref[...].astype(f32)
    half_rows = mine[0:4] + far[16:20]
    both = mine + far
    for number, ref in enumerate(outs[7:11]):
        at = number % 2 * HALF
        ref[...] = half_rows[number // 2 : number // 2 + 1, at : at + HALF].reshape(HALF)
    for part in range(2):
        outs[11][part * D : part * D + D] = half_rows[2 + part : 3 + part, :].reshape(D)
    for number, ref in enumerate(outs[12:]):
        ref[...] = both[4 + number : 5 + number, :].reshape(D)


def local(
    hidden, frames, lengths, cotangent,
    ln1_gain, ln1_bias, sq_weight, sq_bias, sk_weight, sv_weight, sv_bias, so_weight, so_bias,
    ln2_gain, ln2_bias, cq_weight, cq_bias, ck_weight, cv_weight, cv_bias, co_weight, co_bias,
    ln3_gain, ln3_bias, fc1_weight, fc1_bias, fc2_weight, fc2_bias,
):
    tp_index = lax.axis_index("tp")
    core = tp_index.astype(jnp.int32).reshape(1)
    swap = [(0, 1), (1, 0)]
    half = fc1_weight.shape[1]
    wide = 2 * half
    frame_total = frames.shape[1]
    padded = round_up(frame_total, CHUNK)

    near = [w.T for w in (sq_weight, sk_weight, sv_weight, cq_weight, ck_weight, cv_weight)] + [so_weight, co_weight]
    vectors = [ln1_gain, ln1_bias, so_bias, ln2_gain, ln2_bias, co_bias, ln3_gain, ln3_bias, fc2_bias]
    pack, vec, near_bias = call(
        pack_kernel, [], near + vectors + [sq_bias, sv_bias, cq_bias, cv_bias, fc1_bias],
        [shaped((WEIGHTS * HALF + 16, D), bf16), shaped((16, D), f32), shaped((16, D), f32)],
        nbytes=4 << 20,
    )
    far = lax.ppermute(pack, "tp", swap)
    fc1_far = lax.ppermute(fc1_weight, "tp", swap)
    fc2_far = lax.ppermute(fc2_weight, "tp", swap)
    far_bias = far[WEIGHTS * HALF :]

    row_low = shaped((ROWS, D), bf16)
    row_wide = shaped((ROWS, D), f32)
    lse_shape = shaped((2 * ROWS, 128), f32)
    square = pltpu.VMEM((D, D), bf16)
    own, n1, q, k, v, ctx, r1, n2, qc, lse = call(
        self_forward_kernel, [core, lengths],
        [hidden, vec, near_bias, far_bias, near[0], near[1], near[2], near[6], near[3], far],
        [row_low] * 6 + [row_wide, row_low, row_low, lse_shape],
        scratch=[pltpu.VMEM((3 * D, D), bf16), square, square, pltpu.SemaphoreType.DMA((10,))],
        flops=2 * ROWS * D * D * 5, nbytes=8 << 20, far=range(4, 10),
    )

    def cross_specs(first):
        frame_spec = pl.BlockSpec((1, frame_total, D), lambda step, core: (step_seq(step + first, core[0]), 0, 0))
        stored_spec = pl.BlockSpec(
            (1, padded, D), lambda step, core: (jnp.minimum(step + first, step_count(core[0]) - 1), 0, 0)
        )
        return frame_spec, stored_spec

    frame_spec, stored_spec = cross_specs(0)
    key_shape = shaped((STEPS, padded, D), bf16)
    ck, cv, ctx_cross, lse_cross = pl.pallas_call(
        partial(cross_forward_kernel, frame_total),
        out_shape=[key_shape, key_shape, row_low, lse_shape],
        grid_spec=pltpu.PrefetchScalarGridSpec(
            num_scalar_prefetch=1,
            grid=(STEPS,),
            in_specs=[frame_spec, constant((ROWS, D)), constant((16, D)), constant((16, D))] + [anywhere] * 3,
            out_specs=[stored_spec, stored_spec, constant((ROWS, D)), constant((2 * ROWS, 128))],
            scratch_shapes=[pltpu.VMEM((2 * D, D), bf16), pltpu.VMEM((2, 4 * BLOCK, padded), f32), pltpu.SemaphoreType.DMA((4,))],
        ),
        cost_estimate=pl.CostEstimate(flops=20 << 30, bytes_accessed=32 << 20, transcendentals=0),
        name="cross_forward",
    )(core, frames, qc, near_bias, far_bias, near[4], near[5], far)

    dp_count = lax.axis_size("dp")
    feed_rows = round_up(2 * half + HALF, 16 * dp_count)
    out_own, g2, dctx, feed_keep, feed_send, feed_small = call(
        feed_kernel, [core, lengths],
        [cotangent, r1, ctx_cross, vec, near_bias, far_bias, near[7], far, fc1_weight, fc1_far, fc2_weight, fc2_far],
        [row_low, row_wide, row_low, shaped((feed_rows, D), f32), shaped((feed_rows, D), bf16), shaped((8, D), f32)],
        scratch=[
            pltpu.VMEM((ROWS, D), bf16), pltpu.VMEM((ROWS, D), bf16), pltpu.VMEM((ROWS, wide), bf16),
            pltpu.VMEM((ROWS, wide), bf16), pltpu.VMEM((ROWS, D), bf16), square,
            pltpu.VMEM((D, wide), bf16), pltpu.VMEM((wide, D), bf16), pltpu.SemaphoreType.DMA((6,)),
        ],
        flops=2 * ROWS * D * wide * 6, nbytes=16 << 20, far=range(6, 12),
    )
    feed_sum = RowSum(feed_keep, feed_send, swap)
    pending = feed_sum.steps()

    def advance():
        return pending.pop(0)() if pending else feed_sum.current

    def cross_backward(first, count, chained):
        frame_spec, stored_spec = cross_specs(first)
        carried = [constant((ROWS, D)), constant((2 * D, D)), constant((D, 128))]
        return pl.pallas_call(
            partial(cross_backward_kernel, frame_total, first),
            out_shape=[row_low, shaped((2 * D, D), f32), shaped((D, 128), f32)],
            grid_spec=pltpu.PrefetchScalarGridSpec(
                num_scalar_prefetch=1,
                grid=(count,),
                in_specs=[frame_spec, stored_spec, stored_spec] + [constant((ROWS, D))] * 3
                + [constant((2 * ROWS, 128))] + (carried + [anywhere] if chained else []),
                out_specs=carried,
                scratch_shapes=[pltpu.VMEM((2 * D, padded), f32)],
            ),
            cost_estimate=pl.CostEstimate(flops=20 << 30, bytes_accessed=16 << 20, transcendentals=0),
        )(core, frames, ck, cv, qc, ctx_cross, dctx, lse_cross, *chained)

    chained = cross_backward(0, 1, [])
    chained = cross_backward(1, HEAD_SHORTS - 1, [*chained, advance()])
    dqc, cross_grad, cross_bias = cross_backward(HEAD_SHORTS, STEPS - HEAD_SHORTS, [*chained, advance()])
    after = advance()
    half_acc = pltpu.VMEM((D, LONG_LEN), f32)
    g1, low, dq, dk, dv, back_small = call(
        self_attention_back_kernel, [core, lengths],
        [vec, near[6], near[3], far, q, k, v, ctx, r1, lse, dqc, g2, after],
        [row_wide, row_low, row_low, row_low, row_low, shaped((8, D), f32)],
        scratch=[pltpu.VMEM((ROWS, D), bf16), half_acc, half_acc, square, square, pltpu.SemaphoreType.DMA((4,))],
        flops=2 * ROWS * D * D * 10, nbytes=8 << 20, far=(1, 2, 3, 12),
    )
    after = advance()
    attention_rows = round_up(7 * HALF, 8 * dp_count)
    keep, send = call(
        self_weights_kernel, [],
        [n1, n2, ctx, low, dq, dk, dv, dqc, cross_grad, after],
        [shaped((attention_rows, D), f32), shaped((attention_rows, D), bf16)],
        flops=2 * ROWS * D * D * 5, nbytes=8 << 20, far=(9,),
    )
    attention_sum = RowSum(keep, send, swap)
    dh_own, attention_sum.small = call(
        self_finish_kernel, [],
        [own, vec, near[0], near[1], near[2], far, g1, dq, dk, dv, back_small, feed_small, cross_bias, send],
        [row_low, shaped((SMALL, D), f32)],
        scratch=[pltpu.VMEM((8, D), f32), square, square, square, pltpu.SemaphoreType.DMA((6,))],
        flops=2 * ROWS * D * D * 5, nbytes=4 << 20, far=(2, 3, 4, 5, 13),
    )
    while pending:
        advance()
    grad_fc1, grad_fc2, grad_co = call(
        partial(feed_finish_kernel, len(feed_sum.pieces)), [feed_sum.digits[0]], feed_sum.pieces,
        [shaped((D, half), f32), shaped((half, D), f32), shaped((HALF, D), f32)],
        scratch=[pltpu.VMEM((feed_rows, D), bf16)], nbytes=8 << 20,
    )
    attention_sum.after = feed_sum.pieces[-1]
    out_far = lax.ppermute(out_own, "tp", swap)
    dh_far = lax.ppermute(dh_own, "tp", swap)
    for step in attention_sum.steps():
        step()
    pieces = attention_sum.pieces

    (
        grad_ck, grad_cv, grad_sq, grad_sk, grad_sv, grad_cq, grad_so,
        grad_sq_bias, grad_sv_bias, grad_cq_bias, grad_cv_bias, grad_fc1_bias,
        grad_ln1_gain, grad_ln1_bias, grad_so_bias, grad_ln2_gain, grad_ln2_bias,
        grad_co_bias, grad_ln3_gain, grad_ln3_bias, grad_fc2_bias,
    ) = call(
        partial(attention_finish_kernel, len(pieces)), [attention_sum.digits[0]],
        [attention_sum.small, attention_sum.small_far] + pieces,
        [shaped((HALF, D), f32)] * 7 + [shaped((HALF,), f32)] * 4 + [shaped((half,), f32)] + [shaped((D,), f32)] * 9,
        scratch=[pltpu.VMEM((attention_rows, D), bf16)], nbytes=8 << 20,
    )

    def group_rows(mine, far):
        first = jnp.where(tp_index == 0, mine, far)
        second = jnp.where(tp_index == 0, far, mine)
        return jnp.concatenate(
            [
                first[:FIRST_ROWS], second[:FIRST_ROWS],
                second[FIRST_ROWS : FIRST_ROWS + 2 * BLOCK + 2 * MID_LEN], first[FIRST_ROWS:],
            ],
            0,
        )

    return (
        group_rows(out_own, out_far),
        group_rows(dh_own, dh_far),
        grad_ln1_gain,
        grad_ln1_bias,
        grad_sq.T,
        grad_sq_bias,
        grad_sk.T,
        grad_sv.T,
        grad_sv_bias,
        grad_so,
        grad_so_bias,
        grad_ln2_gain,
        grad_ln2_bias,
        grad_cq.T,
        grad_cq_bias,
        grad_ck.T,
        grad_cv.T,
        grad_cv_bias,
        grad_co,
        grad_co_bias,
        grad_ln3_gain,
        grad_ln3_bias,
        grad_fc1,
        grad_fc1_bias,
        grad_fc2,
        grad_fc2_bias,
    )


def solution(mesh):
    return jax.shard_map(
        local,
        mesh=mesh,
        in_specs=(
            P("dp", None),
            P("dp", None, None),
            P("dp"),
            P("dp", None),
            P(),
            P(),
            P(None, "tp"),
            P("tp"),
            P(None, "tp"),
            P(None, "tp"),
            P("tp"),
            P("tp", None),
            P(),
            P(),
            P(),
            P(None, "tp"),
            P("tp"),
            P(None, "tp"),
            P(None, "tp"),
            P("tp"),
            P("tp", None),
            P(),
            P(),
            P(),
            P(None, "tp"),
            P("tp"),
            P("tp", None),
            P(),
        ),
        out_specs=(
            P("dp", None),
            P("dp", None),
            P(),
            P(),
            P(None, "tp"),
            P("tp"),
            P(None, "tp"),
            P(None, "tp"),
            P("tp"),
            P("tp", None),
            P(),
            P(),
            P(),
            P(None, "tp"),
            P("tp"),
            P(None, "tp"),
            P(None, "tp"),
            P("tp"),
            P("tp", None),
            P(),
            P(),
            P(),
            P(None, "tp"),
            P("tp"),
            P("tp", None),
            P(),
        ),
        check_vma=False,
    )
```
